256 devices in a mesh: req: 4 (over x_hi, core), tp: 64 (over z, x_lo, y).
Axes of the slice: x: 4 (x_hi: 2, x_lo: 2; x = x_hi * 2 + x_lo), y: 4, z: 8, core: 2. Of those that a mesh axis runs over, the one named last changes fastest.
Arguments:
- hidden: bfloat16 [4096, 8192], P('req', 'tp'), may hold values from -6 to 6
- query_weight: bfloat16 [8192, 8192], P(None, 'tp'), may hold values from -0.0625 to 0.0625
- key_value_weight: bfloat16 [8192, 2048], P(None, 'tp'), may hold values from -0.0625 to 0.0625
- adapter_down_maps: bfloat16 [64, 8192, 32], P('req', 'tp'), may hold values from -0.0625 to 0.0625
- adapter_up_maps: bfloat16 [64, 32, 8192], P('req', None, 'tp'), may hold values from -1 to 1
- token_request_start: int32 [4096], P('req'), may hold values from 0 to 31, as said below
- adapter_per_block: int32 [32], P('req'), may hold values from 0 to 63
Outputs:
- context: bfloat16 [4096, 8192], P('req', 'tp')
The draws below stay inside these ranges and needn't reach their ends.
Inputs may be any that keep to these rules, and one draw needn't show every extreme that they name: `token_request_start`: each run of 1024 tokens along the req split holds whole requests; a request is a run of whole blocks of 128 tokens; the last block of each such run is a request of its own.
All inputs are finite; a program needn't handle non-finite values.
Results may differ from the reference program's by a relative error of at most 0.012.
Values may be sent and summed in bfloat16 or wider, within the bound.
No kernel may reach another device: no remote copies, remote signals or barrier semaphores. Data moves between devices by JAX's collectives and lax.ppermute only.
A program may use at most 64 MiB of HBM per device.

```python
import math
import jax
import jax.numpy as jnp
import numpy as np
from jax import lax

MODEL_WIDTH = 8192
HEAD_SIZE = 128
KVH = 8
ADAPTER_RANK = 32
BLOCK = 128
ADAPTER_COUNT = 64
GROUP_TOK = 1024
QUERY_HEADS = 64
TOKENS = 4096
N_REQ = 4


def draw_token_request_start(key, part):
    block_total = TOKENS // BLOCK
    per_group = GROUP_TOK // BLOCK
    places = jnp.arange(block_total, dtype=jnp.int32)
    coin_flips = jax.random.randint(key, (block_total,), 0, 4)
    begins = (coin_flips == 0) | (places % per_group == 0) | (places % per_group == per_group - 1)
    firsts = lax.cummax(jnp.where(begins, places, 0), axis=0)
    return jnp.repeat(firsts, BLOCK, total_repeat_length=TOKENS).astype(jnp.int32)


def touch_ends(array, own_key, least, largest):
    extent = array.shape
    index_at = [jax.random.randint(jax.random.fold_in(own_key, axis), (), 0, extent[axis]) for axis in range(len(extent))]
    array = array.at[tuple(index_at)].set(least)
    longest = extent.index(max(extent))
    index_at[longest] = (index_at[longest] + 1) % extent[longest]
    return array.at[tuple(index_at)].set(largest)


def shard_levels(rng, shape, cuts, least, top_value):
    def one(dim, shards_of):
        draws = jax.random.uniform(jax.random.fold_in(jax.random.fold_in(rng, 6), dim), (shards_of,), jnp.float32, least / len(cuts), top_value / len(cuts))
        return jnp.repeat(jnp.exp(draws), shape[dim] // shards_of).reshape((-1,) + (1,) * (len(shape) - dim - 1))

    level = one(*cuts[0])
    for cut in cuts[1:]:
        level = level * one(*cut)
    return level


def rank_bounds(number_of, lean):
    weights = [(1 << 20) // math.isqrt(grade ** lean) + 1 for grade in range(1, number_of + 1)]
    deviation = 1 + sum(weights) // (1 << 30)
    return np.cumsum(np.array([max(1, weight // deviation) for weight in weights]))


def ranked(key, dims, count, skew):
    grid = rank_bounds(count, skew)
    pick = jax.random.randint(jax.random.fold_in(key, 1), dims, 0, int(grid[count - 1]))
    rank = jnp.searchsorted(jnp.asarray(grid, jnp.int32), pick, side="right")
    return jax.random.permutation(jax.random.fold_in(key, 2), count)[rank].astype(jnp.int32)


def scatter_about(stream_key, dims, scale, reach, shards=(), held_as=jnp.bfloat16):
    entries = jax.random.normal(stream_key, dims, jnp.float32) * scale
    if len(shards) > 0:
        entries = shard_levels(stream_key, dims, shards, -0.22, 0.18) * entries
    return jnp.clip(entries, min=-reach, max=reach).astype(held_as)


def setup_inputs(seed: int = 0) -> dict:
    keys = jax.random.split(jax.random.key(seed), 8)
    hidden = scatter_about(keys[0], (TOKENS, MODEL_WIDTH), 1.0, 6.0, ((0, 4), (1, 64)))
    query_weight = scatter_about(keys[1], (MODEL_WIDTH, QUERY_HEADS * HEAD_SIZE), MODEL_WIDTH ** -0.5, 0.0625, ((1, 64),))
    key_value_weight = scatter_about(keys[2], (MODEL_WIDTH, KVH * 2 * HEAD_SIZE), MODEL_WIDTH ** -0.5, 0.0625, ((1, 64),))
    adapter_down_maps = scatter_about(keys[3], (ADAPTER_COUNT, MODEL_WIDTH, ADAPTER_RANK), MODEL_WIDTH ** -0.5, 0.0625, ((0, 4), (1, 64)))
    adapter_up_maps = scatter_about(keys[4], (ADAPTER_COUNT, ADAPTER_RANK, QUERY_HEADS * HEAD_SIZE), ADAPTER_RANK ** -0.5, 1.0, ((0, 4), (2, 64)))
    token_request_start = draw_token_request_start(jax.random.fold_in(keys[7], 71), 0)
    adapter_per_block = touch_ends(ranked(keys[6], (TOKENS // BLOCK,), ADAPTER_COUNT, 2), jax.random.fold_in(keys[6], 3), 0, ADAPTER_COUNT - 1).astype(jnp.int32)
    return {"hidden": hidden, "query_weight": query_weight, "key_value_weight": key_value_weight, "adapter_down_maps": adapter_down_maps, "adapter_up_maps": adapter_up_maps, "token_request_start": token_request_start, "adapter_per_block": adapter_per_block}


ROPE_BASE = 500000.0
ADAPTER_SCALE = 2.0

def rotate(vectors, positions):
    half_width = vectors.shape[-1] // 2
    steps_half = jnp.arange(half_width, dtype=jnp.float32)
    inverse = jnp.exp(-(2.0 * steps_half / vectors.shape[-1]) * math.log(ROPE_BASE))
    angles = positions.astype(jnp.float32)[:, None] * inverse[None, :]
    cosines = jnp.cos(angles)
    sines = jnp.sin(angles)
    front_half = vectors[:, :half_width]
    back_half = vectors[:, half_width:]
    return jnp.concatenate([front_half * cosines - back_half * sines, back_half * cosines + front_half * sines], axis=1)

def attend(queries, key_rows, value_rows, request):
    group_rows = queries.shape[0]
    block_rows = min(512, group_rows)
    block_total = group_rows // block_rows
    places = jnp.arange(group_rows, dtype=jnp.int32)
    score_scale = 1.0 / math.sqrt(queries.shape[1])

    def one_block(block_index):
        begin_row = block_index * block_rows
        q_blk = lax.dynamic_slice_in_dim(queries, begin_row, block_rows, 0)
        r_blk = lax.dynamic_slice_in_dim(request, begin_row, block_rows, 0)
        p_blk = lax.dynamic_slice_in_dim(places, begin_row, block_rows, 0)
        scores = lax.dot_general(q_blk, key_rows, (((1,), (1,)), ((), ())), preferred_element_type=jnp.float32) * score_scale
        allowed = (r_blk[:, None] == request[None, :]) & (places[None, :] <= p_blk[:, None])
        scores = jnp.where(allowed, scores, jnp.float32(-1e+30))
        row_max = lax.optimization_barrier(jnp.max(scores, axis=1, keepdims=True))
        weights = jnp.exp(scores - row_max)
        probs = (weights / lax.optimization_barrier(jnp.sum(weights, axis=1, keepdims=True))).astype(jnp.bfloat16)
        return jnp.dot(probs, value_rows, preferred_element_type=jnp.float32).astype(jnp.bfloat16)
    blocks = lax.map(one_block, jnp.arange(block_total, dtype=jnp.int32))
    return blocks.reshape(group_rows, value_rows.shape[1])

def reference(hidden, query_weight, key_value_weight, adapter_down_maps, adapter_up_maps, token_request_start, adapter_per_block):
    row_count_total = hidden.shape[0]
    block_total = row_count_total // BLOCK
    query_total = jnp.dot(hidden, query_weight, preferred_element_type=jnp.float32)
    kv_sum = jnp.dot(hidden, key_value_weight, preferred_element_type=jnp.float32)
    block_grouped = hidden.reshape(block_total, BLOCK, MODEL_WIDTH).astype(jnp.float32)
    chosen_down = adapter_down_maps[adapter_per_block].astype(jnp.float32)
    reduced_rank = jnp.einsum('uqo,uop->uqp', block_grouped, chosen_down).astype(jnp.bfloat16)
    chosen_up = adapter_up_maps[adapter_per_block].astype(jnp.float32)
    adapter_term = jnp.einsum('epl,elm->epm', reduced_rank.astype(jnp.float32), chosen_up).reshape(row_count_total, QUERY_HEADS * HEAD_SIZE)
    positions = jnp.arange(row_count_total, dtype=jnp.int32) - token_request_start * BLOCK
    complete_query = (query_total + ADAPTER_SCALE * adapter_term).reshape(row_count_total, QUERY_HEADS, HEAD_SIZE)
    queries = jax.vmap(rotate, in_axes=(1, None), out_axes=1)(complete_query, positions).astype(jnp.bfloat16)
    kv_round = lax.optimization_barrier(kv_sum.astype(jnp.bfloat16))
    kv_heads = kv_round.reshape(row_count_total, KVH, 2 * HEAD_SIZE)
    key_all = jax.vmap(rotate, in_axes=(1, None), out_axes=0)(kv_heads[:, :, :HEAD_SIZE].astype(jnp.float32), positions).astype(jnp.bfloat16)
    value_all = jnp.transpose(kv_heads[:, :, HEAD_SIZE:], (1, 0, 2))
    query_heads = jnp.transpose(queries, (1, 0, 2))
    per_kv = QUERY_HEADS // KVH

    def one_head(head_number):
        kv_number = head_number // per_kv
        head_query = lax.dynamic_index_in_dim(query_heads, head_number, 0, keepdims=False)
        head_keys = lax.dynamic_index_in_dim(key_all, kv_number, 0, keepdims=False)
        head_values = lax.dynamic_index_in_dim(value_all, kv_number, 0, keepdims=False)
        pieces = []
        for group_number in range(N_REQ):
            begin_row = group_number * GROUP_TOK
            pieces.append(attend(head_query[begin_row:begin_row + GROUP_TOK], head_keys[begin_row:begin_row + GROUP_TOK], head_values[begin_row:begin_row + GROUP_TOK], token_request_start[begin_row:begin_row + GROUP_TOK]))
        return jnp.concatenate(pieces, axis=0)
    heads_out = lax.map(one_head, jnp.arange(QUERY_HEADS, dtype=jnp.int32))
    return jnp.transpose(heads_out, (1, 0, 2)).reshape(row_count_total, QUERY_HEADS * HEAD_SIZE)
```

```python
import functools
import math

import jax
import jax.numpy as jnp
from jax import lax
from jax.experimental import pallas as pl
from jax.experimental.pallas import tpu as pltpu
from jax.sharding import Mesh, PartitionSpec as P

HEAD_SIZE = 128
BLOCK = 128
RANK = 32
ROPE_BASE = 500000.0
ADAPTER_SCALE = 2.0
NXH, NC, NZ, NX, NY = 2, 2, 8, 2, 4
REQ_AXES = ("xh", "c")
TP_AXES = ("z", "xl", "y")
NP = NX * NY
VMEM = pl.BlockSpec(memory_space=pltpu.VMEM)
SMEM = pl.BlockSpec(memory_space=pltpu.SMEM)


def z_shift(v, s):
    return lax.ppermute(v, "z", [(i, (i + s) % NZ) for i in range(NZ)])


def z_xor(v, s):
    return lax.ppermute(v, "z", [(i, i ^ s) for i in range(NZ)])


def y_xor(v, s):
    return lax.ppermute(v, "y", [(i, i ^ s) for i in range(NY)])


def x_swap(v):
    return lax.ppermute(v, "xl", [(0, 1), (1, 0)])


def core_swap(v):
    return lax.ppermute(v, "c", [(0, 1), (1, 0)])


def xh_swap(v):
    return lax.ppermute(v, "xh", [(0, 1), (1, 0)])


def plane_send(v, d):
    dx, dy = divmod(d, NY)
    route = [
        (a * NY + b, (a ^ dx) * NY + (b + dy) % NY) for a in range(NX) for b in range(NY)
    ]
    return lax.ppermute(v, ("xl", "y"), route)


def weight_send(v, d):
    dx, dy = divmod(d, NY)
    route = []
    for xh in range(NXH):
        for c in range(NC):
            for xl in range(NX):
                for y in range(NY):
                    at = xh * NX + xl
                    if dx:
                        to = at ^ 1 if c == 0 else (at + 1 if at % 2 else at - 1) % 4
                    else:
                        to = at
                    src = ((xh * NC + c) * NX + xl) * NY + y
                    dst = ((to // NX * NC + c) * NX + to % NX) * NY + (y + dy) % NY
                    route.append((src, dst))
    return lax.ppermute(v, ("xh", "c", "xl", "y"), route)


def pack_kernel(s_ref, wq_ref, kv_ref, *outs):
    z, xl, y, c = s_ref[0], s_ref[1], s_ref[2], s_ref[3]

    def fill(out, dx, dy, half):
        p = (xl ^ dx) * NY + ((y + dy) & (NY - 1))
        for j in range(NZ // 2):
            zz = (z + half * (NZ // 2) + j) & (NZ - 1)
            row = pl.multiple_of((zz * NP + p) * 128, 128)
            out[j * 128 : (j + 1) * 128, :] = wq_ref[pl.ds(row, 128), :]
            out[512 + j * 32 : 512 + (j + 1) * 32, :] = kv_ref[:, pl.ds(row, 128)]

    for d in range(NP):
        dx, dy = divmod(d, NY)
        fill(outs[d], dx, dy, c)
    fill(outs[NP], 0, 0, 1 - c)


def low_kernel(s_ref, ad_ref, h_ref, near_ref, far_ref, out_ref):
    c, xh = s_ref[3], s_ref[4]
    per = near_ref.shape[1]
    for b in range(h_ref.shape[0] // BLOCK):
        a = ad_ref[b]
        owner = a // per
        at = a - owner * per
        xr, cr = (owner // NC) ^ xh, (owner % NC) ^ c
        down = jnp.where(cr == 0, near_ref[xr, at, 0:RANK, :], far_ref[xr, at, 0:RANK, :])
        out_ref[:, b * BLOCK : (b + 1) * BLOCK] = lax.dot_general(
            down,
            h_ref[b * BLOCK : (b + 1) * BLOCK, :],
            (((1,), (1,)), ((), ())),
            preferred_element_type=jnp.float32,
        )


def matmul_kernel(s_ref, *refs):
    h_refs, wm = refs[0:8], refs[8:16]
    wo_own, wo_st = refs[16], refs[17]
    outs = refs[18:26]
    hbuf, wq_m, wq_o, kv_m, kv_o = refs[26:31]
    c = s_ref[3]
    for j in range(8):
        hbuf[:, j * 128 : (j + 1) * 128] = h_refs[j][...]
    for d in range(NP):
        own = wm[d]
        oth = wo_own if d == 0 else wo_st.at[d - 1]
        dx, dy = divmod(d, NY)
        wq_m[dy, :, dx * 128 : (dx + 1) * 128] = own[0:512, :]
        wq_o[dy, :, dx * 128 : (dx + 1) * 128] = oth[0:512, :]
        for j in range(4):
            kv_m[d * 32 : (d + 1) * 32, j * 128 : (j + 1) * 128] = own[512 + j * 32 : 544 + j * 32, :]
            kv_o[d * 32 : (d + 1) * 32, j * 128 : (j + 1) * 128] = oth[512 + j * 32 : 544 + j * 32, :]
    at_m = pl.multiple_of(c * 512, 512)
    at_o = pl.multiple_of((1 - c) * 512, 512)
    tile = 256
    nt = (((1,), (1,)), ((), ()))

    def step(i, carry):
        r = pl.multiple_of(i * tile, tile)
        hm = hbuf[pl.ds(r, tile), pl.ds(at_m, 512)]
        ho = hbuf[pl.ds(r, tile), pl.ds(at_o, 512)]
        kv = lax.dot_general(kv_m[...], hm, nt, preferred_element_type=jnp.float32)
        kv += lax.dot_general(kv_o[...], ho, nt, preferred_element_type=jnp.float32)
        kv = kv.astype(jnp.bfloat16)
        for d in range(NP):
            for t in range(tile // 128):
                at = pl.multiple_of(1024 + (i * (tile // 128) + t) * 32, 32)
                outs[d][pl.ds(at, 32), :] = kv[d * 32 : (d + 1) * 32, t * 128 : (t + 1) * 128]
        for dy in range(NY):
            q = jnp.dot(hm, wq_m[dy], preferred_element_type=jnp.float32)
            q += jnp.dot(ho, wq_o[dy], preferred_element_type=jnp.float32)
            q = q.astype(jnp.bfloat16)
            outs[dy][pl.ds(r, tile), :] = q[:, 0:128]
            outs[NY + dy][pl.ds(r, tile), :] = q[:, 128:256]
        return carry

    lax.fori_loop(0, 1024 // tile, step, 0)


def attention_kernel(s_ref, ad_ref, lo_ref, *refs):
    pieces = refs[0:8]
    kv_near, kv_far, low_ref, near_ref, far_ref, cos_ref, sin_ref = refs[8:15]
    out_ref = refs[15]
    kvt, k_buf, v_buf = refs[16:19]
    xl, y, c, xh = s_ref[1], s_ref[2], s_ref[3], s_ref[4]
    for half, ref in enumerate((kv_near, kv_far)):
        for i, m in enumerate((0, 2, 1, 3)):
            p = (xl ^ half) * NY + (y ^ m)
            at = pl.multiple_of(p * 32, 32)
            for t in range(8):
                kvt[pl.ds(at, 32), t * 128 : (t + 1) * 128] = ref[i * 256 + t * 32 : i * 256 + (t + 1) * 32, :]

    def rope(v, rows):
        return v * cos_ref[rows, :] + pltpu.roll(v, 64, 1) * sin_ref[rows, :]

    for t in range(8):
        rows = slice(t * 128, (t + 1) * 128)
        k = kvt[0:128, rows].astype(jnp.float32).T
        k_buf[rows, :] = rope(k, rows).astype(jnp.bfloat16)
        v_buf[rows, :] = kvt[128:256, rows].astype(jnp.float32).T.astype(jnp.bfloat16)
    per = near_ref.shape[1]
    factor = math.log2(math.e) / math.sqrt(HEAD_SIZE)
    for b in range(8):
        rows = slice(b * 128, (b + 1) * 128)
        a = ad_ref[b]
        owner = a // per
        at = a - owner * per
        xr, cr = (owner // NC) ^ xh, (owner % NC) ^ c
        up = jnp.where(cr == 0, near_ref[xr, at, RANK : 2 * RANK, :], far_ref[xr, at, RANK : 2 * RANK, :])
        low = low_ref[:, rows].T.astype(jnp.bfloat16)
        q = ADAPTER_SCALE * jnp.dot(low, up, preferred_element_type=jnp.float32)
        for piece in pieces:
            q += piece[rows, :].astype(jnp.float32)
        q = rope(q, rows).astype(jnp.bfloat16)
        n = (b + 1) * 128
        s = lax.dot_general(
            q, k_buf[0:n, :], (((1,), (1,)), ((), ())), preferred_element_type=jnp.float32
        )
        col = lax.broadcasted_iota(jnp.int32, (128, n), 1)
        row = lax.broadcasted_iota(jnp.int32, (128, n), 0) + b * 128
        allowed = (col >= lo_ref[b]) & (col <= row)
        s = jnp.where(allowed, s, -1e30)
        e = jnp.exp2((s - jnp.max(s, axis=1, keepdims=True)) * factor)
        probs = (e / jnp.sum(e, axis=1, keepdims=True)).astype(jnp.bfloat16)
        out_ref[rows, :] = jnp.dot(
            probs, v_buf[0:n, :], preferred_element_type=jnp.float32
        ).astype(jnp.bfloat16)


def rope_tables(positions):
    half = HEAD_SIZE // 2
    steps = jnp.arange(half, dtype=jnp.float32)
    inverse = jnp.exp(-(2.0 * steps / HEAD_SIZE) * math.log(ROPE_BASE))
    angles = positions.astype(jnp.float32)[:, None] * inverse[None, :]
    cosines, sines = jnp.cos(angles), jnp.sin(angles)
    return jnp.concatenate([cosines, cosines], 1), jnp.concatenate([-sines, sines], 1)


def after(value, *others):
    return lax.optimization_barrier((value, *others))[0]


def body(hidden, query_weight, key_value_weight, down_maps, up_maps, request_start, adapters):
    rows = hidden.shape[0]
    bf16, f32 = jnp.bfloat16, jnp.float32
    place = [lax.axis_index(a) for a in ("z", "xl", "y", "c", "xh")]
    scalars = jnp.stack(place).astype(jnp.int32)

    maps = jnp.concatenate([jnp.transpose(down_maps, (0, 2, 1)), up_maps], axis=1)
    near = jnp.stack([maps, xh_swap(maps)])
    far = core_swap(near)

    right, left = [hidden], [hidden]
    sends = pl.pallas_call(
        pack_kernel,
        out_shape=[jax.ShapeDtypeStruct((640, 128), bf16)] * (NP + 1),
        in_specs=[SMEM, VMEM, VMEM],
        out_specs=[VMEM] * (NP + 1),
        name="pack",
    )(scalars, query_weight, key_value_weight.T)
    got = {0: sends[0]}
    batches = ((6, 5), (7, 2), (1, 3), (4,))
    for step in range(4):
        right.append(z_shift(right[-1], 1))
        if step < 3:
            left.append(z_shift(left[-1], -1))
        for d in batches[step]:
            got[d] = weight_send(after(sends[d], right[step]) if step else sends[d], d)
    flip = [dx * NY + (-dy) % NY for dx in range(NX) for dy in range(NY)]
    mine = [got[flip[d]] for d in range(NP)]
    other = core_swap(jnp.stack(mine[1:]))

    low = pl.pallas_call(
        low_kernel,
        out_shape=jax.ShapeDtypeStruct((RANK, rows), f32),
        in_specs=[SMEM, SMEM, VMEM, VMEM, VMEM],
        out_specs=VMEM,
        name="low",
    )(scalars, adapters, hidden, near, far)
    low = low + x_swap(low)
    low = low + y_xor(low, 1)
    low = low + y_xor(low, 2)
    low = low + z_xor(low, 1)
    low = low + z_xor(low.astype(bf16), 2).astype(f32)
    low = low + z_xor(low.astype(bf16), 4).astype(f32)

    shards = [hidden, left[1], left[2], left[3], right[4], right[3], right[2], right[1]]
    parts = pl.pallas_call(
        matmul_kernel,
        out_shape=[jax.ShapeDtypeStruct((rows + 256, 128), bf16)] * NP,
        in_specs=[SMEM] + [VMEM] * 18,
        out_specs=[VMEM] * NP,
        scratch_shapes=[
            pltpu.VMEM((rows, 1024), bf16),
            pltpu.VMEM((NY, 512, 256), bf16),
            pltpu.VMEM((NY, 512, 256), bf16),
            pltpu.VMEM((256, 512), bf16),
            pltpu.VMEM((256, 512), bf16),
        ],
        name="product",
    )(scalars, *shards, *mine, sends[NP], other)
    pieces = [parts[0]] + [plane_send(parts[d], d) for d in (6, 5, 7, 2, 1, 3, 4)]
    kv = sum(p[rows:].astype(f32) for p in pieces).astype(bf16)
    kv = jnp.concatenate([kv, y_xor(kv, 2)])
    kv = jnp.concatenate([kv, y_xor(kv, 1)])
    kv_far = x_swap(kv)

    first = lax.axis_index("xh") * NC + lax.axis_index("c")
    places = first * rows + jnp.arange(rows, dtype=jnp.int32)
    cosines, sines = rope_tables(places - request_start * BLOCK)
    lowest = request_start[::BLOCK] * BLOCK - first * rows
    return pl.pallas_call(
        attention_kernel,
        out_shape=jax.ShapeDtypeStruct((rows, HEAD_SIZE), bf16),
        in_specs=[SMEM, SMEM, SMEM] + [VMEM] * 15,
        out_specs=VMEM,
        scratch_shapes=[
            pltpu.VMEM((256, rows), bf16),
            pltpu.VMEM((rows, HEAD_SIZE), bf16),
            pltpu.VMEM((rows, HEAD_SIZE), bf16),
        ],
        name="attention",
    )(scalars, adapters, lowest, *pieces, kv, kv_far, low, near, far, cosines, sines)


def solution(mesh):
    fine = Mesh(mesh.devices.reshape(NXH, NC, NZ, NX, NY), REQ_AXES + TP_AXES)
    in_specs = (
        P(REQ_AXES, TP_AXES),
        P(None, TP_AXES),
        P(None, TP_AXES),
        P(REQ_AXES, TP_AXES, None),
        P(REQ_AXES, None, TP_AXES),
        P(REQ_AXES),
        P(REQ_AXES),
    )
    return jax.shard_map(
        body, mesh=fine, in_specs=in_specs, out_specs=P(REQ_AXES, TP_AXES), check_vma=False
    )
```

```python
import functools
import math

import jax
import jax.numpy as jnp
from jax import lax
from jax.experimental import pallas as pl
from jax.experimental.pallas import tpu as pltpu
from jax.sharding import Mesh, PartitionSpec as P

HEAD_SIZE = 128
BLOCK = 128
RANK = 32
ROPE_BASE = 500000.0
ADAPTER_SCALE = 2.0
NXH, NC, NZ, NX, NY = 2, 2, 8, 2, 4
REQ_AXES = ("xh", "c")
TP_AXES = ("z", "xl", "y")
NP = NX * NY
VMEM = pl.BlockSpec(memory_space=pltpu.VMEM)
SMEM = pl.BlockSpec(memory_space=pltpu.SMEM)


def z_shift(v, s):
    return lax.ppermute(v, "z", [(i, (i + s) % NZ) for i in range(NZ)])


def z_xor(v, s):
    return lax.ppermute(v, "z", [(i, i ^ s) for i in range(NZ)])


def y_xor(v, s):
    return lax.ppermute(v, "y", [(i, i ^ s) for i in range(NY)])


def x_swap(v):
    return lax.ppermute(v, "xl", [(0, 1), (1, 0)])


def core_swap(v):
    return lax.ppermute(v, "c", [(0, 1), (1, 0)])


def xh_swap(v):
    return lax.ppermute(v, "xh", [(0, 1), (1, 0)])


def plane_send(v, d):
    dx, dy = divmod(d, NY)
    route = [
        (a * NY + b, (a ^ dx) * NY + (b + dy) % NY) for a in range(NX) for b in range(NY)
    ]
    return lax.ppermute(v, ("xl", "y"), route)


SERVED = ((4, 6, 1), (5, 7, 3, 2))
FLIP = [dx * NY + (-dy) % NY for dx in range(NX) for dy in range(NY)]


def weight_send(v, k):
    route = []
    for xh in range(NXH):
        for c in range(NC):
            if k >= len(SERVED[c]):
                continue
            dx, dy = divmod(SERVED[c][k], NY)
            for xl in range(NX):
                for y in range(NY):
                    at = xh * NX + xl
                    if dx:
                        to = at ^ 1 if c == 0 else (at + 1 if at % 2 else at - 1) % 4
                    else:
                        to = at
                    src = ((xh * NC + c) * NX + xl) * NY + y
                    dst = ((to // NX * NC + c) * NX + to % NX) * NY + (y + dy) % NY
                    route.append((src, dst))
    return lax.ppermute(v, ("xh", "c", "xl", "y"), route)


def weight_swap(v, k):
    return lax.ppermute(v, "c", [(c, 1 - c) for c in range(NC) if k < len(SERVED[c])])


def pack_kernel(s_ref, wq_ref, kv_ref, *outs):
    z, xl, y, c = s_ref[0], s_ref[1], s_ref[2], s_ref[3]
    for k in range(5):
        d = 0
        if k < 4:
            d = jnp.where(c == 0, (SERVED[0] + (0,))[k], SERVED[1][k])
        p = (xl ^ (d // NY)) * NY + ((y + d) & (NY - 1))
        for j in range(NZ):
            row = pl.multiple_of((((z + j) & (NZ - 1)) * NP + p) * 128, 128)
            outs[k][j * 128 : (j + 1) * 128, :] = wq_ref[pl.ds(row, 128), :]
            outs[k][1024 + j * 32 : 1024 + (j + 1) * 32, :] = kv_ref[:, pl.ds(row, 128)]


def low_kernel(s_ref, ad_ref, h_ref, near_ref, far_ref, out_ref):
    c, xh = s_ref[3], s_ref[4]
    per = near_ref.shape[1]
    for b in range(h_ref.shape[0] // BLOCK):
        a = ad_ref[b]
        owner = a // per
        at = a - owner * per
        xr, cr = (owner // NC) ^ xh, (owner % NC) ^ c
        down = jnp.where(cr == 0, near_ref[xr, at, 0:RANK, :], far_ref[xr, at, 0:RANK, :])
        out_ref[:, b * BLOCK : (b + 1) * BLOCK] = lax.dot_general(
            down,
            h_ref[b * BLOCK : (b + 1) * BLOCK, :],
            (((1,), (1,)), ((), ())),
            preferred_element_type=jnp.float32,
        )


def matmul_kernel(s_ref, *refs):
    h_refs, own, mine, other, low_ref = refs[0:8], refs[8], refs[9:13], refs[13:17], refs[17]
    outs = refs[18:26]
    hbuf, wq, kvw = refs[26:29]
    xl, y, c = s_ref[1], s_ref[2], s_ref[3]
    for j in range(8):
        hbuf[:, j * 128 : (j + 1) * 128] = h_refs[j][...]

    def place(ref, d):
        dx, dy = divmod(d, NY)
        wq[dy, :, dx * 128 : (dx + 1) * 128] = ref[0:1024, :]
        for j in range(NZ):
            kvw[d * 32 : (d + 1) * 32, j * 128 : (j + 1) * 128] = ref[1024 + j * 32 : 1056 + j * 32, :]

    place(own, 0)
    for core in range(NC):

        @pl.when(c == core)
        def _():
            for k, d in enumerate(SERVED[core]):
                place(mine[k], FLIP[d])
            for k, d in enumerate(SERVED[1 - core]):
                place(other[k], FLIP[d])

    for d in range(NP):
        dx, dy = divmod(d, NY)
        p = (xl ^ dx) * NY + ((y + dy) & (NY - 1))
        at = pl.multiple_of(p * 128, 128)
        outs[d][1280:1312, :] = low_ref[:, pl.ds(at, 128)].astype(jnp.bfloat16)
    tile = 512

    def step(i, carry):
        r = pl.multiple_of(i * tile, tile)
        h = hbuf[pl.ds(r, tile), :]
        kv = lax.dot_general(kvw[...], h, (((1,), (1,)), ((), ())), preferred_element_type=jnp.float32)
        kv = kv.astype(jnp.bfloat16)
        for d in range(NP):
            for t in range(tile // 128):
                at = pl.multiple_of(1024 + (i * (tile // 128) + t) * 32, 32)
                outs[d][pl.ds(at, 32), :] = kv[d * 32 : (d + 1) * 32, t * 128 : (t + 1) * 128]
        for dy in range(NY):
            q = jnp.dot(h, wq[dy], preferred_element_type=jnp.float32).astype(jnp.bfloat16)
            outs[dy][pl.ds(r, tile), :] = q[:, 0:128]
            outs[NY + dy][pl.ds(r, tile), :] = q[:, 128:256]
        return carry

    lax.fori_loop(0, 1024 // tile, step, 0)


def add_kernel(*refs):
    out_ref = refs[-1]

    def step(i, carry):
        rows = pl.ds(pl.multiple_of(i * 128, 128), 128)
        total = refs[0][rows, :].astype(jnp.float32)
        for piece in refs[1:-1]:
            total += piece[rows, :].astype(jnp.float32)
        out_ref[rows, :] = total
        return carry

    lax.fori_loop(0, out_ref.shape[0] // 128, step, 0)


def attention_kernel(s_ref, ad_ref, lo_ref, *refs):
    q_ref, kv_near, kv_far, near_ref, far_ref, cos_ref, sin_ref = refs[0:7]
    out_ref = refs[7]
    kvt, low_buf, k_buf, v_buf = refs[8:12]
    xl, y, c, xh = s_ref[1], s_ref[2], s_ref[3], s_ref[4]
    for half, ref in enumerate((kv_near, kv_far)):
        for i, m in enumerate((0, 2, 1, 3)):
            p = (xl ^ half) * NY + (y ^ m)
            at = pl.multiple_of(p * 32, 32)
            for t in range(8):
                kvt[pl.ds(at, 32), t * 128 : (t + 1) * 128] = ref[i * 288 + t * 32 : i * 288 + (t + 1) * 32, :]
            low_buf[p] = ref[i * 288 + 256 : (i + 1) * 288, :]

    def rope(v, rows):
        return v * cos_ref[rows, :] + pltpu.roll(v, 64, 1) * sin_ref[rows, :]

    for t in range(8):
        rows = slice(t * 128, (t + 1) * 128)
        k = kvt[0:128, rows].astype(jnp.float32).T
        k_buf[rows, :] = rope(k, rows).astype(jnp.bfloat16)
        v_buf[rows, :] = kvt[128:256, rows].T
    per = near_ref.shape[1]
    factor = math.log2(math.e) / math.sqrt(HEAD_SIZE)
    for b in range(8):
        rows = slice(b * 128, (b + 1) * 128)
        a = ad_ref[b]
        owner = a // per
        at = a - owner * per
        xr, cr = (owner // NC) ^ xh, (owner % NC) ^ c
        up = jnp.where(cr == 0, near_ref[xr, at, RANK : 2 * RANK, :], far_ref[xr, at, RANK : 2 * RANK, :])
        q = q_ref[rows, :] + ADAPTER_SCALE * lax.dot_general(
            low_buf[b], up, (((0,), (0,)), ((), ())), preferred_element_type=jnp.float32
        )
        q = rope(q, rows).astype(jnp.bfloat16)
        n = (b + 1) * 128
        s = lax.dot_general(
            q, k_buf[0:n, :], (((1,), (1,)), ((), ())), preferred_element_type=jnp.float32
        )
        col = lax.broadcasted_iota(jnp.int32, (128, n), 1)
        row = lax.broadcasted_iota(jnp.int32, (128, n), 0) + b * 128
        allowed = (col >= lo_ref[b]) & (col <= row)
        s = jnp.where(allowed, s, -1e30)
        e = jnp.exp2((s - jnp.max(s, axis=1, keepdims=True)) * factor)
        probs = (e * (1.0 / jnp.sum(e, axis=1, keepdims=True))).astype(jnp.bfloat16)
        out_ref[rows, :] = jnp.dot(
            probs, v_buf[0:n, :], preferred_element_type=jnp.float32
        ).astype(jnp.bfloat16)


def rope_tables(positions):
    half = HEAD_SIZE // 2
    steps = jnp.arange(half, dtype=jnp.float32)
    inverse = jnp.exp(-(2.0 * steps / HEAD_SIZE) * math.log(ROPE_BASE))
    angles = positions.astype(jnp.float32)[:, None] * inverse[None, :]
    cosines, sines = jnp.cos(angles), jnp.sin(angles)
    return jnp.concatenate([cosines, cosines], 1), jnp.concatenate([-sines, sines], 1)


def after(value, *others):
    return lax.optimization_barrier((value, *others))[0]


def body(hidden, query_weight, key_value_weight, down_maps, up_maps, request_start, adapters):
    rows = hidden.shape[0]
    bf16, f32 = jnp.bfloat16, jnp.float32
    place = [lax.axis_index(a) for a in ("z", "xl", "y", "c", "xh")]
    scalars = jnp.stack(place).astype(jnp.int32)

    maps = jnp.concatenate([jnp.transpose(down_maps, (0, 2, 1)), up_maps], axis=1)
    twin = xh_swap(maps)

    sends = pl.pallas_call(
        pack_kernel,
        out_shape=[jax.ShapeDtypeStruct((1280, 128), bf16)] * 5,
        in_specs=[SMEM, VMEM, VMEM],
        out_specs=[VMEM] * 5,
        name="pack",
    )(scalars, query_weight, key_value_weight.T)
    right, left = [hidden], [hidden]
    mine, other = [], []
    for step in range(4):
        gate = (right[-1], left[-1])
        right.append(z_shift(after(gate[0], gate[1]) if step else hidden, 1))
        if step < 3:
            left.append(z_shift(after(gate[1], gate[0]) if step else hidden, -1))
        if step < 2:
            for k in (2 * step, 2 * step + 1):
                mine.append(weight_send(after(sends[k], *gate) if step else sends[k], k))
    for k in range(4):
        other.append(weight_swap(mine[k], k))

    near = jnp.stack([maps, after(twin, right[1], left[1])])
    far = core_swap(near)
    low = pl.pallas_call(
        low_kernel,
        out_shape=jax.ShapeDtypeStruct((RANK, rows), f32),
        in_specs=[SMEM, SMEM, VMEM, VMEM, VMEM],
        out_specs=VMEM,
        name="low",
    )(scalars, adapters, hidden, near, far)
    low = low + z_xor(low, 1)
    low = low + z_xor(low, 2)
    low = low + z_xor(low.astype(bf16), 4).astype(f32)

    shards = [hidden, left[1], left[2], left[3], right[4], right[3], right[2], right[1]]
    parts = pl.pallas_call(
        matmul_kernel,
        out_shape=[jax.ShapeDtypeStruct((rows + 288, 128), bf16)] * NP,
        in_specs=[SMEM] + [VMEM] * 18,
        out_specs=[VMEM] * NP,
        scratch_shapes=[
            pltpu.VMEM((rows, 1024), bf16),
            pltpu.VMEM((NY, 1024, 256), bf16),
            pltpu.VMEM((256, 1024), bf16),
        ],
        name="product",
    )(scalars, *shards, sends[4], *mine, *other, low)
    pieces = [parts[0]] + [plane_send(parts[d], d) for d in (6, 5, 7, 2, 1, 3, 4)]
    kv = sum(p[rows:].astype(f32) for p in pieces).astype(bf16)
    kv = jnp.concatenate([kv, y_xor(kv, 2)])
    kv = jnp.concatenate([kv, y_xor(kv, 1)])
    kv_far = x_swap(kv)
    q = pl.pallas_call(
        add_kernel,
        out_shape=jax.ShapeDtypeStruct((rows, HEAD_SIZE), f32),
        in_specs=[VMEM] * NP,
        out_specs=VMEM,
        name="add",
    )(*pieces)

    first = lax.axis_index("xh") * NC + lax.axis_index("c")
    places = first * rows + jnp.arange(rows, dtype=jnp.int32)
    cosines, sines = rope_tables(places - request_start * BLOCK)
    lowest = request_start[::BLOCK] * BLOCK - first * rows
    return pl.pallas_call(
        attention_kernel,
        out_shape=jax.ShapeDtypeStruct((rows, HEAD_SIZE), bf16),
        in_specs=[SMEM, SMEM, SMEM] + [VMEM] * 7,
        out_specs=VMEM,
        scratch_shapes=[
            pltpu.VMEM((256, rows), bf16),
            pltpu.VMEM((NP, RANK, 128), bf16),
            pltpu.VMEM((rows, HEAD_SIZE), bf16),
            pltpu.VMEM((rows, HEAD_SIZE), bf16),
        ],
        name="attention",
    )(scalars, adapters, lowest, q, kv, kv_far, near, far, cosines, sines)


def solution(mesh):
    fine = Mesh(mesh.devices.reshape(NXH, NC, NZ, NX, NY), REQ_AXES + TP_AXES)
    in_specs = (
        P(REQ_AXES, TP_AXES),
        P(None, TP_AXES),
        P(None, TP_AXES),
        P(REQ_AXES, TP_AXES, None),
        P(REQ_AXES, None, TP_AXES),
        P(REQ_AXES),
        P(REQ_AXES),
    )
    return jax.shard_map(
        body, mesh=fine, in_specs=in_specs, out_specs=P(REQ_AXES, TP_AXES), check_vma=False
    )
```

```python
import functools
import math

import jax
import jax.numpy as jnp
from jax import lax
from jax.experimental import pallas as pl
from jax.experimental.pallas import tpu as pltpu
from jax.sharding import Mesh, PartitionSpec as P

HEAD_SIZE = 128
BLOCK = 128
RANK = 32
ROPE_BASE = 500000.0
ADAPTER_SCALE = 2.0
NXH, NC, NZ, NX, NY = 2, 2, 8, 2, 4
REQ_AXES = ("xh", "c")
TP_AXES = ("z", "xl", "y")
NP = NX * NY
TA, TB = 384, 640
VMEM = pl.BlockSpec(memory_space=pltpu.VMEM)
SMEM = pl.BlockSpec(memory_space=pltpu.SMEM)


def z_shift(v, s):
    return lax.ppermute(v, "z", [(i, (i + s) % NZ) for i in range(NZ)])


def z_xor(v, s):
    return lax.ppermute(v, "z", [(i, i ^ s) for i in range(NZ)])


def y_xor(v, s):
    return lax.ppermute(v, "y", [(i, i ^ s) for i in range(NY)])


def x_swap(v):
    return lax.ppermute(v, "xl", [(0, 1), (1, 0)])


def core_swap(v):
    return lax.ppermute(v, "c", [(0, 1), (1, 0)])


def xh_swap(v):
    return lax.ppermute(v, "xh", [(0, 1), (1, 0)])


def y_shift(v, s):
    return lax.ppermute(v, "y", [(i, (i + s) % NY) for i in range(NY)])


SERVED = ((4, 6, 1), (5, 7, 3, 2))
FLIP = [dx * NY + (-dy) % NY for dx in range(NX) for dy in range(NY)]


def weight_send(v, k):
    route = []
    for xh in range(NXH):
        for c in range(NC):
            if k >= len(SERVED[c]):
                continue
            dx, dy = divmod(SERVED[c][k], NY)
            for xl in range(NX):
                for y in range(NY):
                    at = xh * NX + xl
                    if dx:
                        to = at ^ 1 if c == 0 else (at + 1 if at % 2 else at - 1) % 4
                    else:
                        to = at
                    src = ((xh * NC + c) * NX + xl) * NY + y
                    dst = ((to // NX * NC + c) * NX + to % NX) * NY + (y + dy) % NY
                    route.append((src, dst))
    return lax.ppermute(v, ("xh", "c", "xl", "y"), route)


def weight_swap(v, k):
    return lax.ppermute(v, "c", [(c, 1 - c) for c in range(NC) if k < len(SERVED[c])])


def pack_kernel(s_ref, wq_ref, kv_ref, *outs):
    z, xl, y, c = s_ref[0], s_ref[1], s_ref[2], s_ref[3]
    for k in range(5):
        d = 0
        if k < 4:
            d = jnp.where(c == 0, (SERVED[0] + (0,))[k], SERVED[1][k])
        p = (xl ^ (d // NY)) * NY + ((y + d) & (NY - 1))
        for j in range(NZ):
            row = pl.multiple_of((((z + j) & (NZ - 1)) * NP + p) * 128, 128)
            outs[k][j * 128 : (j + 1) * 128, :] = wq_ref[pl.ds(row, 128), :]
            outs[k][1024 + j * 32 : 1024 + (j + 1) * 32, :] = kv_ref[:, pl.ds(row, 128)]


def low_kernel(s_ref, ad_ref, h_ref, near_ref, far_ref, out_ref):
    c, xh = s_ref[3], s_ref[4]
    per = near_ref.shape[1]
    for b in range(h_ref.shape[0] // BLOCK):
        a = ad_ref[b]
        owner = a // per
        at = a - owner * per
        xr, cr = (owner // NC) ^ xh, (owner % NC) ^ c
        down = jnp.where(cr == 0, near_ref[xr, at, 0:RANK, :], far_ref[xr, at, 0:RANK, :])
        out_ref[:, b * BLOCK : (b + 1) * BLOCK] = lax.dot_general(
            down,
            h_ref[b * BLOCK : (b + 1) * BLOCK, :],
            (((1,), (1,)), ((), ())),
            preferred_element_type=jnp.float32,
        )


def for_each_piece(c, own, mine, other, place):
    place(own, 0)
    for core in range(NC):

        @pl.when(c == core)
        def _():
            for k, d in enumerate(SERVED[core]):
                place(mine[k], FLIP[d])
            for k, d in enumerate(SERVED[1 - core]):
                place(other[k], FLIP[d])


def kv_product_kernel(s_ref, *refs):
    h_refs, own, mine, other = refs[0:8], refs[8], refs[9:13], refs[13:17]
    outs, hbuf, kvw = refs[17:21], refs[21], refs[22]
    for j in range(8):
        hbuf[:, j * 128 : (j + 1) * 128] = h_refs[j][...]

    def place(ref, d):
        for j in range(NZ):
            kvw[d * 32 : (d + 1) * 32, j * 128 : (j + 1) * 128] = ref[1024 + j * 32 : 1056 + j * 32, :]

    for_each_piece(s_ref[3], own, mine, other, place)
    kv = lax.dot_general(
        kvw[...], hbuf[...], (((1,), (1,)), ((), ())), preferred_element_type=jnp.float32
    ).astype(jnp.bfloat16)
    for d in range(NP):
        dx, dy = divmod(d, NY)
        for t in range(8):
            at = t * 64 + dx * 32
            outs[dy][at : at + 32, :] = kv[d * 32 : (d + 1) * 32, t * 128 : (t + 1) * 128]


def q_product_kernel(s_ref, *refs):
    h_refs, own, mine, other = refs[0:8], refs[8], refs[9:13], refs[13:17]
    near_ref, far_ref, outs, hbuf, wq = refs[17], refs[18], refs[19:23], refs[23], refs[24]
    for j in range(8):
        hbuf[:, j * 128 : (j + 1) * 128] = h_refs[j][...]

    def place(ref, d):
        dx, dy = divmod(d, NY)
        wq[dy, :, dx * 128 : (dx + 1) * 128] = ref[0:1024, :]

    for_each_piece(s_ref[3], own, mine, other, place)
    for dy in range(NY):
        q = jnp.dot(hbuf[0:TA, :], wq[dy], preferred_element_type=jnp.float32).astype(jnp.bfloat16)
        near_ref[dy * TA : (dy + 1) * TA, :] = q[:, 0:128]
        far_ref[dy * TA : (dy + 1) * TA, :] = q[:, 128:256]
    for dy in range(NY):
        q = jnp.dot(hbuf[TA:1024, :], wq[dy], preferred_element_type=jnp.float32).astype(jnp.bfloat16)
        outs[dy][0:TB, :] = q[:, 0:128]
        outs[dy][TB : 2 * TB, :] = q[:, 128:256]


def wide(ref, rows):
    return ref[rows, :].astype(jnp.float32)


def kv_join_kernel(k0, k1, k2, k3, far_ref, sum_ref, send_ref):
    total = wide(k0, ...) + wide(k1, ...) + wide(k2, ...) + wide(k3, ...)
    sum_ref[...] = total
    send_ref[0 : NY * TA, :] = far_ref[...]
    send_ref[NY * TA : NY * TA + 512, :] = total.astype(jnp.bfloat16)


def stage_a_kernel(near_ref, got_ref, kv_ref, own_ref, kv_out, *sends):
    for t in range(8):
        for dx in range(NX):
            a, b = t * 64 + dx * 32, NY * TA + t * 64 + (1 - dx) * 32
            kv_out[a : a + 32, :] = (kv_ref[a : a + 32, :] + wide(got_ref, slice(b, b + 32))).astype(jnp.bfloat16)
    for dy in range(NY):
        rows = slice(dy * TA, (dy + 1) * TA)
        total = wide(near_ref, rows) + wide(got_ref, rows)
        if dy == 0:
            own_ref[...] = total
        else:
            sends[dy - 1][0:TA, :] = total.astype(jnp.bfloat16)
            sends[dy - 1][TA : TA + 512, :] = kv_out[...]


def stage_b_kernel(b0, b1, b2, b3, own_ref, send_ref):
    for dx, out in enumerate((own_ref, send_ref)):
        rows = slice(dx * TB, (dx + 1) * TB)
        out[...] = (wide(b0, rows) + wide(b1, rows) + wide(b2, rows) + wide(b3, rows)).astype(out.dtype)


def attention_kernel(s_ref, ad_ref, lo_ref, *refs):
    a_own, a_got, b_own, b_got, kv_own = refs[0], refs[1:4], refs[4], refs[5], refs[6]
    low_ref, near_ref, far_ref, cos_ref, sin_ref = refs[7:12]
    out_ref = refs[12]
    kvt, k_buf, v_buf = refs[13:16]
    xl, y, c, xh = s_ref[1], s_ref[2], s_ref[3], s_ref[4]
    for i in range(NY):
        ref, base = (kv_own, 0) if i == 0 else (a_got[i - 1], TA)
        for dx in range(NX):
            p = (xl ^ dx) * NY + ((y - i) & (NY - 1))
            at = pl.multiple_of(p * 32, 32)
            for t in range(8):
                kvt[pl.ds(at, 32), t * 128 : (t + 1) * 128] = ref[base + t * 64 + dx * 32 : base + t * 64 + dx * 32 + 32, :]

    def rope(v, rows):
        return v * cos_ref[rows, :] + pltpu.roll(v, 64, 1) * sin_ref[rows, :]

    for t in range(8):
        rows = slice(t * 128, (t + 1) * 128)
        k = kvt[0:128, rows].astype(jnp.float32).T
        k_buf[rows, :] = rope(k, rows).astype(jnp.bfloat16)
        v_buf[rows, :] = kvt[128:256, rows].T
    per = near_ref.shape[1]
    factor = math.log2(math.e) / math.sqrt(HEAD_SIZE)
    for b in range(8):
        rows = slice(b * 128, (b + 1) * 128)
        a = ad_ref[b]
        owner = a // per
        at = a - owner * per
        xr, cr = (owner // NC) ^ xh, (owner % NC) ^ c
        up = jnp.where(cr == 0, near_ref[xr, at, RANK : 2 * RANK, :], far_ref[xr, at, RANK : 2 * RANK, :])
        q = ADAPTER_SCALE * lax.dot_general(
            low_ref[:, rows].astype(jnp.bfloat16), up, (((0,), (0,)), ((), ())), preferred_element_type=jnp.float32
        )
        if b * 128 < TA:
            q += a_own[rows, :]
            for ref in a_got:
                q += wide(ref, rows)
        else:
            part = slice(b * 128 - TA, (b + 1) * 128 - TA)
            q += b_own[part, :] + wide(b_got, part)
        q = rope(q, rows).astype(jnp.bfloat16)
        n = (b + 1) * 128
        s = lax.dot_general(
            q, k_buf[0:n, :], (((1,), (1,)), ((), ())), preferred_element_type=jnp.float32
        )
        col = lax.broadcasted_iota(jnp.int32, (128, n), 1)
        row = lax.broadcasted_iota(jnp.int32, (128, n), 0) + b * 128
        allowed = (col >= lo_ref[b]) & (col <= row)
        s = jnp.where(allowed, s, -1e30)
        e = jnp.exp2((s - jnp.max(s, axis=1, keepdims=True)) * factor)
        probs = (e * (1.0 / jnp.sum(e, axis=1, keepdims=True))).astype(jnp.bfloat16)
        out_ref[rows, :] = jnp.dot(
            probs, v_buf[0:n, :], preferred_element_type=jnp.float32
        ).astype(jnp.bfloat16)


def call(kernel, name, outs, *args, scalars=0, scratch=()):
    single = isinstance(outs, jax.ShapeDtypeStruct)
    return pl.pallas_call(
        kernel,
        out_shape=outs,
        in_specs=[SMEM] * scalars + [VMEM] * (len(args) - scalars),
        out_specs=VMEM if single else [VMEM] * len(outs),
        scratch_shapes=scratch,
        name=name,
    )(*args)


def rope_tables(positions):
    half = HEAD_SIZE // 2
    steps = jnp.arange(half, dtype=jnp.float32)
    inverse = jnp.exp(-(2.0 * steps / HEAD_SIZE) * math.log(ROPE_BASE))
    angles = positions.astype(jnp.float32)[:, None] * inverse[None, :]
    cosines, sines = jnp.cos(angles), jnp.sin(angles)
    return jnp.concatenate([cosines, cosines], 1), jnp.concatenate([-sines, sines], 1)


def after(value, *others):
    return lax.optimization_barrier((value, *others))[0]


def body(hidden, query_weight, key_value_weight, down_maps, up_maps, request_start, adapters):
    rows = hidden.shape[0]
    bf16, f32 = jnp.bfloat16, jnp.float32
    of = jax.ShapeDtypeStruct
    place = [lax.axis_index(a) for a in ("z", "xl", "y", "c", "xh")]
    scalars = jnp.stack(place).astype(jnp.int32)

    maps = jnp.concatenate([jnp.transpose(down_maps, (0, 2, 1)), up_maps], axis=1)
    twin = xh_swap(maps)

    sends = call(
        pack_kernel, "pack", [of((1280, 128), bf16)] * 5, scalars, query_weight, key_value_weight.T, scalars=1
    )
    right, left = [hidden], [hidden]
    mine = [weight_send(sends[k], k) for k in range(2)]
    gates = ((), (0,), (1, 2), (3,))
    for step in range(4):
        r, l = right[-1], left[-1]
        if step:
            waits = [mine[k] for k in gates[step]]
            r, l = after(right[-1], left[-1], *waits), after(left[-1], right[-1], *waits)
        right.append(z_shift(r, 1))
        if step < 3:
            left.append(z_shift(l, -1))
        if step == 1:
            mine += [weight_send(after(sends[k], right[1], left[1]), k) for k in (2, 3)]
    other = [weight_swap(mine[k], k) for k in range(4)]

    near = jnp.stack([maps, after(twin, right[1], left[1])])
    far = core_swap(near)
    low = call(
        low_kernel, "low", of((RANK, rows), f32), scalars, adapters, hidden, near, after(far, right[2], left[2]), scalars=2
    )
    low = low + x_swap(low)
    low = low + y_xor(low, 1)
    low = low + y_xor(low, 2)

    shards = [hidden, left[1], left[2], left[3], right[4], right[3], right[2], right[1]]
    weights = (sends[4], *mine, *other)
    kv_parts = call(
        kv_product_kernel,
        "kv_product",
        [of((512, 128), bf16)] * NY,
        scalars,
        *shards,
        *weights,
        scalars=1,
        scratch=[pltpu.VMEM((rows, 1024), bf16), pltpu.VMEM((256, 1024), bf16)],
    )
    kv_got = [y_shift(kv_parts[dy], dy) for dy in (2, 1, 3)]
    near_a, far_a, *b_parts = call(
        q_product_kernel,
        "q_product",
        [of((NY * TA, 128), bf16)] * 2 + [of((2 * TB, 128), bf16)] * NY,
        after(scalars, kv_parts[0]),
        *shards,
        *weights,
        scalars=1,
        scratch=[pltpu.VMEM((rows, 1024), bf16), pltpu.VMEM((NY, 1024, 256), bf16)],
    )
    b_got = [y_shift(b_parts[dy], dy) for dy in (2, 1, 3)]
    kv_sum, x_send = call(
        kv_join_kernel,
        "kv_join",
        [of((512, 128), f32), of((NY * TA + 512, 128), bf16)],
        kv_parts[0],
        *kv_got,
        far_a,
    )
    x_got = x_swap(x_send)
    low = low + z_xor(low, 1)
    low = low + z_xor(low, 2)
    low = low + z_xor(low.astype(bf16), 4).astype(f32)
    a_own, kv_own, *a_sends = call(
        stage_a_kernel,
        "stage_a",
        [of((TA, 128), f32), of((512, 128), bf16)] + [of((TA + 512, 128), bf16)] * (NY - 1),
        near_a,
        x_got,
        kv_sum,
    )
    a_got = {dy: y_shift(a_sends[dy - 1], dy) for dy in (2, 1, 3)}
    b_own, b_send = call(
        stage_b_kernel, "stage_b", [of((TB, 128), f32), of((TB, 128), bf16)], b_parts[0], *b_got
    )
    b_last = x_swap(b_send)

    first = lax.axis_index("xh") * NC + lax.axis_index("c")
    places = first * rows + jnp.arange(rows, dtype=jnp.int32)
    cosines, sines = rope_tables(places - request_start * BLOCK)
    lowest = request_start[::BLOCK] * BLOCK - first * rows
    return call(
        attention_kernel,
        "attention",
        of((rows, HEAD_SIZE), bf16),
        scalars,
        adapters,
        lowest,
        a_own,
        *[a_got[dy] for dy in (1, 2, 3)],
        b_own,
        b_last,
        kv_own,
        low,
        near,
        far,
        cosines,
        sines,
        scalars=3,
        scratch=[pltpu.VMEM((256, rows), bf16)] + [pltpu.VMEM((rows, HEAD_SIZE), bf16)] * 2,
    )


def solution(mesh):
    fine = Mesh(mesh.devices.reshape(NXH, NC, NZ, NX, NY), REQ_AXES + TP_AXES)
    in_specs = (
        P(REQ_AXES, TP_AXES),
        P(None, TP_AXES),
        P(None, TP_AXES),
        P(REQ_AXES, TP_AXES, None),
        P(REQ_AXES, None, TP_AXES),
        P(REQ_AXES),
        P(REQ_AXES),
    )
    return jax.shard_map(
        body, mesh=fine, in_specs=in_specs, out_specs=P(REQ_AXES, TP_AXES), check_vma=False
    )
```

```python
import functools
import math

import jax
import jax.numpy as jnp
from jax import lax
from jax.experimental import pallas as pl
from jax.experimental.pallas import tpu as pltpu
from jax.sharding import Mesh, PartitionSpec as P

HEAD_SIZE = 128
BLOCK = 128
RANK = 32
ROPE_BASE = 500000.0
ADAPTER_SCALE = 2.0
NXH, NC, NZ, NX, NY = 2, 2, 8, 2, 4
REQ_AXES = ("xh", "c")
TP_AXES = ("z", "xl", "y")
NP = NX * NY
TA, TB = 384, 640
VMEM = pl.BlockSpec(memory_space=pltpu.VMEM)
SMEM = pl.BlockSpec(memory_space=pltpu.SMEM)


def z_shift(v, s):
    return lax.ppermute(v, "z", [(i, (i + s) % NZ) for i in range(NZ)])


def z_xor(v, s):
    return lax.ppermute(v, "z", [(i, i ^ s) for i in range(NZ)])


def y_xor(v, s):
    return lax.ppermute(v, "y", [(i, i ^ s) for i in range(NY)])


def x_swap(v):
    return lax.ppermute(v, "xl", [(0, 1), (1, 0)])


def core_swap(v):
    return lax.ppermute(v, "c", [(0, 1), (1, 0)])


def xh_swap(v):
    return lax.ppermute(v, "xh", [(0, 1), (1, 0)])


def y_shift(v, s):
    return lax.ppermute(v, "y", [(i, (i + s) % NY) for i in range(NY)])


SERVED = ((4, 6, 1), (5, 7, 3, 2))
FLIP = [dx * NY + (-dy) % NY for dx in range(NX) for dy in range(NY)]


def weight_send(v, k):
    route = []
    for xh in range(NXH):
        for c in range(NC):
            if k >= len(SERVED[c]):
                continue
            dx, dy = divmod(SERVED[c][k], NY)
            for xl in range(NX):
                for y in range(NY):
                    at = xh * NX + xl
                    if dx:
                        to = at ^ 1 if c == 0 else (at + 1 if at % 2 else at - 1) % 4
                    else:
                        to = at
                    src = ((xh * NC + c) * NX + xl) * NY + y
                    dst = ((to // NX * NC + c) * NX + to % NX) * NY + (y + dy) % NY
                    route.append((src, dst))
    return lax.ppermute(v, ("xh", "c", "xl", "y"), route)


def weight_swap(v, k):
    return lax.ppermute(v, "c", [(c, 1 - c) for c in range(NC) if k < len(SERVED[c])])


def pack_kernel(wq_ref, kv_ref, *refs):
    outs, sem = refs[:5], refs[5]
    z, xl, y, c = (lax.axis_index(a) for a in ("z", "xl", "y", "c"))
    copies = []
    for k in range(5):
        d = 0
        if k < 4:
            d = jnp.where(c == 0, (SERVED[0] + (0,))[k], SERVED[1][k])
        p = (xl ^ (d // NY)) * NY + ((y + d) & (NY - 1))
        for j in range(NZ):
            row = pl.multiple_of((((z + j) & (NZ - 1)) * NP + p) * 128, 128)
            copies.append((wq_ref.at[pl.ds(row, 128), :], outs[k].at[j * 128 : (j + 1) * 128, :]))
            copies.append((kv_ref.at[:, pl.ds(row, 128)], outs[k].at[1024 + j * 32 : 1056 + j * 32, :]))
    copies = [pltpu.make_async_copy(src, dst, sem.at[i]) for i, (src, dst) in enumerate(copies)]
    for copy in copies:
        copy.start()
    for copy in copies:
        copy.wait()


def add_kernel(a_ref, b_ref, *outs):
    total = a_ref[...] + b_ref[...].astype(jnp.float32)
    outs[0][...] = total
    for out in outs[1:]:
        out[...] = total.astype(out.dtype)


def rope_kernel(start_ref, cos_ref, sin_ref):
    half = HEAD_SIZE // 2
    lane = lax.broadcasted_iota(jnp.int32, (BLOCK, HEAD_SIZE), 1)
    row = lax.broadcasted_iota(jnp.int32, (BLOCK, HEAD_SIZE), 0)
    steps = (lane & (half - 1)).astype(jnp.float32)
    inverse = jnp.exp(-(2.0 * steps / HEAD_SIZE) * math.log(ROPE_BASE))
    sign = jnp.where(lane < half, -1.0, 1.0).astype(jnp.float32)
    place = row.astype(jnp.float32) * inverse
    cos_in, sin_in = jnp.cos(place), jnp.sin(place)
    blocks = cos_ref.shape[0] // BLOCK
    ahead = lax.broadcasted_iota(jnp.int32, (8, HEAD_SIZE), 0).astype(jnp.float32) * BLOCK * inverse[0:8, :]
    cos_out, sin_out = jnp.cos(ahead), jnp.sin(ahead)
    first = (lax.axis_index("xh") * NC + lax.axis_index("c")) * blocks
    which = lax.broadcasted_iota(jnp.int32, (8, HEAD_SIZE), 0)
    for b in range(blocks):
        chosen = which == first + b - start_ref[b * BLOCK]
        co = jnp.sum(jnp.where(chosen, cos_out, 0.0), axis=0, keepdims=True)
        so = jnp.sum(jnp.where(chosen, sin_out, 0.0), axis=0, keepdims=True)
        rows = slice(b * BLOCK, (b + 1) * BLOCK)
        cos_ref[rows, :] = cos_in * co - sin_in * so
        sin_ref[rows, :] = (sin_in * co + cos_in * so) * sign


def low_kernel(ad_ref, h_ref, near_ref, far_ref, out_ref):
    c, xh = lax.axis_index("c"), lax.axis_index("xh")
    per = near_ref.shape[1]
    for b in range(h_ref.shape[0] // BLOCK):
        a = ad_ref[b]
        owner = a // per
        at = a - owner * per
        xr, cr = (owner // NC) ^ xh, (owner % NC) ^ c
        down = jnp.where(cr == 0, near_ref[xr, at, 0:RANK, :], far_ref[xr, at, 0:RANK, :])
        out_ref[:, b * BLOCK : (b + 1) * BLOCK] = lax.dot_general(
            down,
            h_ref[b * BLOCK : (b + 1) * BLOCK, :],
            (((1,), (1,)), ((), ())),
            preferred_element_type=jnp.float32,
        )


def for_each_piece(own, mine, other, place):
    place(own, 0)
    c = lax.axis_index("c")
    for core in range(NC):

        @pl.when(c == core)
        def _():
            for k, d in enumerate(SERVED[core]):
                place(mine[k], FLIP[d])
            for k, d in enumerate(SERVED[1 - core]):
                place(other[k], FLIP[d])


def kv_product_kernel(*refs):
    h_refs, own, mine, other = refs[0:8], refs[8], refs[9:13], refs[13:17]
    outs, hbuf, kvw = refs[17:21], refs[21], refs[22]
    for j in range(8):
        hbuf[:, j * 128 : (j + 1) * 128] = h_refs[j][...]

    def place(ref, d):
        for j in range(NZ):
            kvw[d * 32 : (d + 1) * 32, j * 128 : (j + 1) * 128] = ref[1024 + j * 32 : 1056 + j * 32, :]

    for_each_piece(own, mine, other, place)
    kv = lax.dot_general(
        kvw[...], hbuf[...], (((1,), (1,)), ((), ())), preferred_element_type=jnp.float32
    ).astype(jnp.bfloat16)
    for d in range(NP):
        dx, dy = divmod(d, NY)
        for t in range(8):
            at = t * 64 + dx * 32
            outs[dy][at : at + 32, :] = kv[d * 32 : (d + 1) * 32, t * 128 : (t + 1) * 128]


def q_product_kernel(hbuf, own, *refs):
    mine, other = refs[0:4], refs[4:8]
    near_ref, far_ref, outs, wq = refs[8], refs[9], refs[10:14], refs[14]

    def place(ref, d):
        dx, dy = divmod(d, NY)
        wq[dy, :, dx * 128 : (dx + 1) * 128] = ref[0:1024, :]

    for_each_piece(own, mine, other, place)
    for dy in range(NY):
        q = jnp.dot(hbuf[0:TA, :], wq[dy], preferred_element_type=jnp.float32).astype(jnp.bfloat16)
        near_ref[dy * TA : (dy + 1) * TA, :] = q[:, 0:128]
        far_ref[dy * TA : (dy + 1) * TA, :] = q[:, 128:256]
    for dy in range(NY):
        q = jnp.dot(hbuf[TA:1024, :], wq[dy], preferred_element_type=jnp.float32).astype(jnp.bfloat16)
        outs[dy][0:TB, :] = q[:, 0:128]
        outs[dy][TB : 2 * TB, :] = q[:, 128:256]


def wide(ref, rows):
    return ref[rows, :].astype(jnp.float32)


def kv_join_kernel(k0, k1, k2, k3, far_ref, sum_ref, send_ref):
    total = wide(k0, ...) + wide(k1, ...) + wide(k2, ...) + wide(k3, ...)
    sum_ref[...] = total
    send_ref[0 : NY * TA, :] = far_ref[...]
    send_ref[NY * TA : NY * TA + 512, :] = total.astype(jnp.bfloat16)


def stage_a_kernel(near_ref, got_ref, kv_ref, own_ref, kv_out, *sends):
    for t in range(8):
        for dx in range(NX):
            a, b = t * 64 + dx * 32, NY * TA + t * 64 + (1 - dx) * 32
            kv_out[a : a + 32, :] = (kv_ref[a : a + 32, :] + wide(got_ref, slice(b, b + 32))).astype(jnp.bfloat16)
    for dy in range(NY):
        rows = slice(dy * TA, (dy + 1) * TA)
        total = wide(near_ref, rows) + wide(got_ref, rows)
        if dy == 0:
            own_ref[...] = total
        else:
            sends[dy - 1][0:TA, :] = total.astype(jnp.bfloat16)
            sends[dy - 1][TA : TA + 512, :] = kv_out[...]


def stage_b_kernel(b0, b1, b2, b3, own_ref, send_ref):
    for dx, out in enumerate((own_ref, send_ref)):
        rows = slice(dx * TB, (dx + 1) * TB)
        out[...] = (wide(b0, rows) + wide(b1, rows) + wide(b2, rows) + wide(b3, rows)).astype(out.dtype)


def attention_kernel(ad_ref, start_ref, *refs):
    a_own, a_got, b_own, b_got, kv_own = refs[0], refs[1:4], refs[4], refs[5], refs[6]
    low_ref, near_ref, far_ref, cos_ref, sin_ref = refs[7:12]
    out_ref = refs[12]
    kvt, k_buf, v_buf = refs[13:16]
    xl, y, c, xh = (lax.axis_index(a) for a in ("xl", "y", "c", "xh"))
    first = (xh * NC + c) * 8
    for i in range(NY):
        ref, base = (kv_own, 0) if i == 0 else (a_got[i - 1], TA)
        for dx in range(NX):
            p = (xl ^ dx) * NY + ((y - i) & (NY - 1))
            at = pl.multiple_of(p * 32, 32)
            for t in range(8):
                kvt[pl.ds(at, 32), t * 128 : (t + 1) * 128] = ref[base + t * 64 + dx * 32 : base + t * 64 + dx * 32 + 32, :]

    def rope(v, rows):
        return v * cos_ref[rows, :] + pltpu.roll(v, 64, 1) * sin_ref[rows, :]

    for t in range(8):
        rows = slice(t * 128, (t + 1) * 128)
        k = kvt[0:128, rows].astype(jnp.float32).T
        k_buf[rows, :] = rope(k, rows).astype(jnp.bfloat16)
        v_buf[rows, :] = kvt[128:256, rows].T
    per = near_ref.shape[1]
    factor = math.log2(math.e) / math.sqrt(HEAD_SIZE)
    for b in range(8):
        rows = slice(b * 128, (b + 1) * 128)
        a = ad_ref[b]
        owner = a // per
        at = a - owner * per
        xr, cr = (owner // NC) ^ xh, (owner % NC) ^ c
        up = jnp.where(cr == 0, near_ref[xr, at, RANK : 2 * RANK, :], far_ref[xr, at, RANK : 2 * RANK, :])
        q = ADAPTER_SCALE * lax.dot_general(
            low_ref[:, rows], up, (((0,), (0,)), ((), ())), preferred_element_type=jnp.float32
        )
        if b * 128 < TA:
            q += a_own[rows, :]
            for ref in a_got:
                q += wide(ref, rows)
        else:
            part = slice(b * 128 - TA, (b + 1) * 128 - TA)
            q += b_own[part, :] + wide(b_got, part)
        q = rope(q, rows).astype(jnp.bfloat16)
        n = (b + 1) * 128
        s = lax.dot_general(
            q, k_buf[0:n, :], (((1,), (1,)), ((), ())), preferred_element_type=jnp.float32
        )
        col = lax.broadcasted_iota(jnp.int32, (128, n), 1)
        row = lax.broadcasted_iota(jnp.int32, (128, n), 0) + b * 128
        allowed = (col >= (start_ref[b * BLOCK] - first) * BLOCK) & (col <= row)
        s = jnp.where(allowed, s, -1e30)
        e = jnp.exp2((s - jnp.max(s, axis=1, keepdims=True)) * factor)
        probs = (e * (1.0 / jnp.sum(e, axis=1, keepdims=True))).astype(jnp.bfloat16)
        out_ref[rows, :] = jnp.dot(
            probs, v_buf[0:n, :], preferred_element_type=jnp.float32
        ).astype(jnp.bfloat16)


def call(kernel, name, outs, *args, scalars=0, scratch=(), mib=4, space=pltpu.VMEM):
    single = isinstance(outs, jax.ShapeDtypeStruct)
    return pl.pallas_call(
        kernel,
        out_shape=outs,
        in_specs=[SMEM] * scalars + [pl.BlockSpec(memory_space=space)] * (len(args) - scalars),
        out_specs=VMEM if single else [VMEM] * len(outs),
        scratch_shapes=scratch,
        compiler_params=pltpu.CompilerParams(vmem_limit_bytes=mib << 20),
        name=name,
    )(*args)


def after(value, *others):
    return lax.optimization_barrier((value, *others))[0]


def body(hidden, query_weight, key_value_weight, down_maps, up_maps, request_start, adapters):
    rows = hidden.shape[0]
    bf16, f32 = jnp.bfloat16, jnp.float32
    of = jax.ShapeDtypeStruct
    maps = jnp.concatenate([jnp.transpose(down_maps, (0, 2, 1)), up_maps], axis=1)
    twin = xh_swap(maps)

    sends = call(
        pack_kernel,
        "pack",
        [of((1280, 128), bf16)] * 5,
        query_weight,
        key_value_weight.T,
        scratch=[pltpu.SemaphoreType.DMA((10 * NZ,))],
        space=pltpu.HBM,
    )
    cosines, sines = call(rope_kernel, "rope", [of((rows, HEAD_SIZE), f32)] * 2, request_start, scalars=1)
    right, left = [hidden], [hidden]
    mine = [weight_send(sends[k], k) for k in range(2)]
    gates = ((), (0,), (1, 2), (3,))
    for step in range(4):
        r, l = right[-1], left[-1]
        if step:
            waits = [mine[k] for k in gates[step]] + [cosines] * (step == 2)
            r, l = after(right[-1], left[-1], *waits), after(left[-1], right[-1], *waits)
        right.append(z_shift(r, 1))
        if step < 3:
            left.append(z_shift(l, -1))
        if step == 1:
            mine += [weight_send(after(sends[k], right[1], left[1]), k) for k in (2, 3)]
    other = [weight_swap(mine[k], k) for k in range(4)]

    near = jnp.stack([maps, after(twin, right[1], left[1])])
    far = core_swap(near)
    low = call(
        low_kernel, "low", of((RANK, rows), f32), adapters, hidden, near, far, scalars=1
    )

    def added(low, sent, also=()):
        outs = [of((RANK, rows), f32)] + [of((RANK, rows), t) for t in also]
        return call(add_kernel, "low_add", outs, low, sent)

    (low,) = added(low, x_swap(low))
    (low,) = added(low, y_xor(low, 1))
    (low,) = added(low, y_xor(low, 2))

    shards = [after(hidden, low), left[1], left[2], left[3], right[4], right[3], right[2], right[1]]
    weights = (sends[4], *mine, *other)
    *kv_parts, gathered = call(
        kv_product_kernel,
        "kv_product",
        [of((512, 128), bf16)] * NY + [of((rows, 1024), bf16)],
        *shards,
        *weights,
        scratch=[pltpu.VMEM((256, 1024), bf16)],
        mib=8,
    )
    kv_got = [y_shift(kv_parts[dy], dy) for dy in (2, 1, 3)]
    near_a, far_a, *b_parts = call(
        q_product_kernel,
        "q_product",
        [of((NY * TA, 128), bf16)] * 2 + [of((2 * TB, 128), bf16)] * NY,
        gathered,
        *weights,
        scratch=[pltpu.VMEM((NY, 1024, 256), bf16)],
        mib=10,
    )
    b_got = [y_shift(b_parts[dy], dy) for dy in (2, 1, 3)]
    kv_sum, x_send = call(
        kv_join_kernel,
        "kv_join",
        [of((512, 128), f32), of((NY * TA + 512, 128), bf16)],
        kv_parts[0],
        *kv_got,
        far_a,
    )
    x_got = x_swap(x_send)
    low = after(low, kv_sum)
    (low,) = added(low, z_xor(low, 1))
    low = after(low, x_got)
    low, narrow = added(low, z_xor(low, 2), (bf16,))
    _, low = added(low, z_xor(narrow, 4), (bf16,))
    a_own, kv_own, *a_sends = call(
        stage_a_kernel,
        "stage_a",
        [of((TA, 128), f32), of((512, 128), bf16)] + [of((TA + 512, 128), bf16)] * (NY - 1),
        near_a,
        x_got,
        kv_sum,
    )
    a_got = {dy: y_shift(a_sends[dy - 1], dy) for dy in (2, 1, 3)}
    b_own, b_send = call(
        stage_b_kernel, "stage_b", [of((TB, 128), f32), of((TB, 128), bf16)], b_parts[0], *b_got
    )
    b_last = x_swap(b_send)

    return call(
        attention_kernel,
        "attention",
        of((rows, HEAD_SIZE), bf16),
        adapters,
        request_start,
        a_own,
        *[a_got[dy] for dy in (1, 2, 3)],
        b_own,
        b_last,
        kv_own,
        low,
        near,
        far,
        cosines,
        sines,
        scalars=2,
        scratch=[pltpu.VMEM((256, rows), bf16)] + [pltpu.VMEM((rows, HEAD_SIZE), bf16)] * 2,
        mib=8,
    )


def solution(mesh):
    fine = Mesh(mesh.devices.reshape(NXH, NC, NZ, NX, NY), REQ_AXES + TP_AXES)
    in_specs = (
        P(REQ_AXES, TP_AXES),
        P(None, TP_AXES),
        P(None, TP_AXES),
        P(REQ_AXES, TP_AXES, None),
        P(REQ_AXES, None, TP_AXES),
        P(REQ_AXES),
        P(REQ_AXES),
    )
    return jax.shard_map(
        body, mesh=fine, in_specs=in_specs, out_specs=P(REQ_AXES, TP_AXES), check_vma=False
    )
```

```python
import functools
import math

import jax
import jax.numpy as jnp
from jax import lax
from jax.experimental import pallas as pl
from jax.experimental.pallas import tpu as pltpu
from jax.sharding import Mesh, PartitionSpec as P

HEAD_SIZE = 128
BLOCK = 128
RANK = 32
ROPE_BASE = 500000.0
ADAPTER_SCALE = 2.0
NXH, NC, NZ, NX, NY = 2, 2, 8, 2, 4
REQ_AXES = ("xh", "c")
TP_AXES = ("z", "xl", "y")
NP = NX * NY
TA, TB = 384, 640
PACK_MIB = 4
VMEM = pl.BlockSpec(memory_space=pltpu.VMEM)
SMEM = pl.BlockSpec(memory_space=pltpu.SMEM)


def z_shift(v, s):
    return lax.ppermute(v, "z", [(i, (i + s) % NZ) for i in range(NZ)])


def z_xor(v, s):
    return lax.ppermute(v, "z", [(i, i ^ s) for i in range(NZ)])


def y_xor(v, s):
    return lax.ppermute(v, "y", [(i, i ^ s) for i in range(NY)])


def x_swap(v):
    return lax.ppermute(v, "xl", [(0, 1), (1, 0)])


def core_swap(v):
    return lax.ppermute(v, "c", [(0, 1), (1, 0)])


def xh_swap(v):
    return lax.ppermute(v, "xh", [(0, 1), (1, 0)])


def y_shift(v, s):
    return lax.ppermute(v, "y", [(i, (i + s) % NY) for i in range(NY)])


SERVED = ((4, 6, 1), (5, 7, 3, 2))
FLIP = [dx * NY + (-dy) % NY for dx in range(NX) for dy in range(NY)]


def weight_send(v, k):
    route = []
    for xh in range(NXH):
        for c in range(NC):
            if k >= len(SERVED[c]):
                continue
            dx, dy = divmod(SERVED[c][k], NY)
            for xl in range(NX):
                for y in range(NY):
                    at = xh * NX + xl
                    if dx:
                        to = at ^ 1 if c == 0 else (at + 1 if at % 2 else at - 1) % 4
                    else:
                        to = at
                    src = ((xh * NC + c) * NX + xl) * NY + y
                    dst = ((to // NX * NC + c) * NX + to % NX) * NY + (y + dy) % NY
                    route.append((src, dst))
    return lax.ppermute(v, ("xh", "c", "xl", "y"), route)


def run_copies(pairs, sem):
    copies = [pltpu.make_async_copy(src, dst, sem.at[i]) for i, (src, dst) in enumerate(pairs)]
    for copy in copies:
        copy.start()
    for copy in copies:
        copy.wait()


def pack_kernel(wq_ref, kv_ref, down_ref, up_ref, *refs):
    outs, maps, sem = refs[:5], refs[5], refs[6]
    z, xl, y, c = (lax.axis_index(a) for a in ("z", "xl", "y", "c"))
    pairs = [(down_ref, maps.at[:, 0:RANK, :]), (up_ref, maps.at[:, RANK : 2 * RANK, :])]
    for k in range(5):
        d = 0
        if k < 4:
            d = jnp.where(c == 0, (SERVED[0] + (0,))[k], SERVED[1][k])
        p = (xl ^ (d // NY)) * NY + ((y + d) & (NY - 1))
        for j in range(NZ):
            row = pl.multiple_of((((z + j) & (NZ - 1)) * NP + p) * 128, 128)
            pairs.append((wq_ref.at[pl.ds(row, 128), :], outs[k].at[j * 128 : (j + 1) * 128, :]))
            pairs.append((kv_ref.at[:, pl.ds(row, 128)], outs[k].at[1024 + j * 32 : 1056 + j * 32, :]))
    run_copies(pairs, sem)


def stack_kernel(*refs):
    for i, ref in enumerate(refs[:-1]):
        refs[-1][i] = ref[...]


def add_kernel(a_ref, b_ref, *outs):
    total = a_ref[...] + b_ref[...].astype(jnp.float32)
    outs[0][...] = total
    for out in outs[1:]:
        out[...] = total.astype(out.dtype)


def rope_kernel(start_ref, cos_ref, sin_ref):
    half = HEAD_SIZE // 2
    lane = lax.broadcasted_iota(jnp.int32, (BLOCK, HEAD_SIZE), 1)
    row = lax.broadcasted_iota(jnp.int32, (BLOCK, HEAD_SIZE), 0)
    steps = (lane & (half - 1)).astype(jnp.float32)
    inverse = jnp.exp(-(2.0 * steps / HEAD_SIZE) * math.log(ROPE_BASE))
    sign = jnp.where(lane < half, -1.0, 1.0).astype(jnp.float32)
    place = row.astype(jnp.float32) * inverse
    cos_in, sin_in = jnp.cos(place), jnp.sin(place)
    blocks = cos_ref.shape[0] // BLOCK
    ahead = lax.broadcasted_iota(jnp.int32, (8, HEAD_SIZE), 0).astype(jnp.float32) * BLOCK * inverse[0:8, :]
    cos_out, sin_out = jnp.cos(ahead), jnp.sin(ahead)
    first = (lax.axis_index("xh") * NC + lax.axis_index("c")) * blocks
    which = lax.broadcasted_iota(jnp.int32, (8, HEAD_SIZE), 0)
    for b in range(blocks):
        chosen = which == first + b - start_ref[b * BLOCK]
        co = jnp.sum(jnp.where(chosen, cos_out, 0.0), axis=0, keepdims=True)
        so = jnp.sum(jnp.where(chosen, sin_out, 0.0), axis=0, keepdims=True)
        rows = slice(b * BLOCK, (b + 1) * BLOCK)
        cos_ref[rows, :] = cos_in * co - sin_in * so
        sin_ref[rows, :] = (sin_in * co + cos_in * so) * sign


def low_kernel(ad_ref, h_ref, near_ref, far_ref, out_ref):
    c, xh = lax.axis_index("c"), lax.axis_index("xh")
    per = near_ref.shape[1]
    for b in range(h_ref.shape[0] // BLOCK):
        a = ad_ref[b]
        owner = a // per
        at = a - owner * per
        xr, cr = (owner // NC) ^ xh, (owner % NC) ^ c
        down = jnp.where(cr == 0, near_ref[xr, at, 0:RANK, :], far_ref[xr, at, 0:RANK, :])
        out_ref[:, b * BLOCK : (b + 1) * BLOCK] = lax.dot_general(
            down,
            h_ref[b * BLOCK : (b + 1) * BLOCK, :],
            (((1,), (1,)), ((), ())),
            preferred_element_type=jnp.float32,
        )


def for_each_piece(own, mine, other, place):
    place(own, 0)
    c = lax.axis_index("c")
    for core in range(NC):

        @pl.when(c == core)
        def _():
            for k, d in enumerate(SERVED[core]):
                place(mine[k], FLIP[d])
            for k, d in enumerate(SERVED[1 - core]):
                place(other[k], FLIP[d])


def kv_product_kernel(*refs):
    h_refs, own, mine, other, low_ref = refs[0:8], refs[8], refs[9:13], refs[13], refs[14]
    outs, hbuf, kvw = refs[15:19], refs[19], refs[20]
    other = [other.at[k] for k in range(4)]
    y = lax.axis_index("y")
    for j in range(8):
        hbuf[:, j * 128 : (j + 1) * 128] = h_refs[j][...]
    for dy in range(NY):
        for t in range(2):
            at = pl.multiple_of((((y + dy) & (NY - 1)) * 2 + t) * 128, 128)
            outs[dy][512 + t * 32 : 544 + t * 32, :] = low_ref[:, pl.ds(at, 128)].astype(jnp.bfloat16)

    def place(ref, d):
        for j in range(NZ):
            kvw[d * 32 : (d + 1) * 32, j * 128 : (j + 1) * 128] = ref[1024 + j * 32 : 1056 + j * 32, :]

    for_each_piece(own, mine, other, place)
    kv = lax.dot_general(
        kvw[...], hbuf[...], (((1,), (1,)), ((), ())), preferred_element_type=jnp.float32
    ).astype(jnp.bfloat16)
    for d in range(NP):
        dx, dy = divmod(d, NY)
        for t in range(8):
            at = t * 64 + dx * 32
            outs[dy][at : at + 32, :] = kv[d * 32 : (d + 1) * 32, t * 128 : (t + 1) * 128]


def q_product_kernel(hbuf, own, *refs):
    mine, other = refs[0:4], [refs[4].at[k] for k in range(4)]
    near_ref, far_ref, outs, wq = refs[5], refs[6], refs[7:11], refs[11]

    def place(ref, d):
        dx, dy = divmod(d, NY)
        wq[dy, :, dx * 128 : (dx + 1) * 128] = ref[0:1024, :]

    for_each_piece(own, mine, other, place)
    for dy in range(NY):
        q = jnp.dot(hbuf[0:TA, :], wq[dy], preferred_element_type=jnp.float32).astype(jnp.bfloat16)
        near_ref[dy * TA : (dy + 1) * TA, :] = q[:, 0:128]
        far_ref[dy * TA : (dy + 1) * TA, :] = q[:, 128:256]
    for dy in range(NY):
        q = jnp.dot(hbuf[TA:1024, :], wq[dy], preferred_element_type=jnp.float32).astype(jnp.bfloat16)
        outs[dy][0:TB, :] = q[:, 0:128]
        outs[dy][TB : 2 * TB, :] = q[:, 128:256]


def wide(ref, rows):
    return ref[rows, :].astype(jnp.float32)


def kv_join_kernel(k0, k1, k2, k3, far_ref, sum_ref, send_ref):
    total = wide(k0, ...) + wide(k1, ...) + wide(k2, ...) + wide(k3, ...)
    sum_ref[...] = total
    send_ref[0 : NY * TA, :] = far_ref[...]
    send_ref[NY * TA :, :] = total.astype(jnp.bfloat16)


def stage_a_kernel(near_ref, got_ref, kv_ref, own_ref, kv_out, *sends):
    for t in range(8):
        for dx in range(NX):
            a, b = t * 64 + dx * 32, NY * TA + t * 64 + (1 - dx) * 32
            kv_out[a : a + 32, :] = (kv_ref[a : a + 32, :] + wide(got_ref, slice(b, b + 32))).astype(jnp.bfloat16)
    kv_out[512:576, :] = (kv_ref[512:576, :] + wide(got_ref, slice(NY * TA + 512, NY * TA + 576))).astype(jnp.bfloat16)
    for dy in range(NY):
        rows = slice(dy * TA, (dy + 1) * TA)
        total = wide(near_ref, rows) + wide(got_ref, rows)
        if dy == 0:
            own_ref[...] = total
        else:
            sends[dy - 1][0:TA, :] = total.astype(jnp.bfloat16)
            sends[dy - 1][TA:, :] = kv_out[...]


def stage_b_kernel(b0, b1, b2, b3, own_ref, send_ref):
    for dx, out in enumerate((own_ref, send_ref)):
        rows = slice(dx * TB, (dx + 1) * TB)
        out[...] = (wide(b0, rows) + wide(b1, rows) + wide(b2, rows) + wide(b3, rows)).astype(out.dtype)


def attention_kernel(ad_ref, start_ref, *refs):
    a_own, a_got, b_own, b_got, kv_own = refs[0], refs[1:4], refs[4], refs[5], refs[6]
    near_ref, far_ref, cos_ref, sin_ref = refs[7:11]
    out_ref = refs[11]
    kvt, k_buf, v_buf, low_buf = refs[12:16]
    xl, y, c, xh = (lax.axis_index(a) for a in ("xl", "y", "c", "xh"))
    first = (xh * NC + c) * 8
    for i in range(NY):
        ref, base = (kv_own, 0) if i == 0 else (a_got[i - 1], TA)
        for t in range(2):
            low_buf[((y - i) & (NY - 1)) * 2 + t] = ref[base + 512 + t * 32 : base + 544 + t * 32, :]
        for dx in range(NX):
            p = (xl ^ dx) * NY + ((y - i) & (NY - 1))
            at = pl.multiple_of(p * 32, 32)
            for t in range(8):
                kvt[pl.ds(at, 32), t * 128 : (t + 1) * 128] = ref[base + t * 64 + dx * 32 : base + t * 64 + dx * 32 + 32, :]

    def rope(v, rows):
        return v * cos_ref[rows, :] + pltpu.roll(v, 64, 1) * sin_ref[rows, :]

    for t in range(8):
        rows = slice(t * 128, (t + 1) * 128)
        k = kvt[0:128, rows].astype(jnp.float32).T
        k_buf[rows, :] = rope(k, rows).astype(jnp.bfloat16)
        v_buf[rows, :] = kvt[128:256, rows].T
    per = near_ref.shape[1]
    factor = math.log2(math.e) / math.sqrt(HEAD_SIZE)
    for b in range(8):
        rows = slice(b * 128, (b + 1) * 128)
        a = ad_ref[b]
        owner = a // per
        at = a - owner * per
        xr, cr = (owner // NC) ^ xh, (owner % NC) ^ c
        up = jnp.where(cr == 0, near_ref[xr, at, RANK : 2 * RANK, :], far_ref[xr, at, RANK : 2 * RANK, :])
        q = ADAPTER_SCALE * lax.dot_general(
            low_buf[b], up, (((0,), (0,)), ((), ())), preferred_element_type=jnp.float32
        )
        if b * 128 < TA:
            q += a_own[rows, :]
            for ref in a_got:
                q += wide(ref, rows)
        else:
            part = slice(b * 128 - TA, (b + 1) * 128 - TA)
            q += b_own[part, :] + wide(b_got, part)
        q = rope(q, rows).astype(jnp.bfloat16)
        n = (b + 1) * 128
        s = lax.dot_general(
            q, k_buf[0:n, :], (((1,), (1,)), ((), ())), preferred_element_type=jnp.float32
        )
        col = lax.broadcasted_iota(jnp.int32, (128, n), 1)
        row = lax.broadcasted_iota(jnp.int32, (128, n), 0) + b * 128
        allowed = (col >= (start_ref[b * BLOCK] - first) * BLOCK) & (col <= row)
        s = jnp.where(allowed, s, -1e30)
        e = jnp.exp2((s - jnp.max(s, axis=1, keepdims=True)) * factor)
        mixed = jnp.dot(e.astype(jnp.bfloat16), v_buf[0:n, :], preferred_element_type=jnp.float32)
        out_ref[rows, :] = (mixed * (1.0 / jnp.sum(e, axis=1, keepdims=True))).astype(jnp.bfloat16)


def call(kernel, name, outs, *args, scalars=0, scratch=(), mib=4, space=pltpu.VMEM):
    single = isinstance(outs, jax.ShapeDtypeStruct)
    return pl.pallas_call(
        kernel,
        out_shape=outs,
        in_specs=[SMEM] * scalars + [pl.BlockSpec(memory_space=space)] * (len(args) - scalars),
        out_specs=VMEM if single else [VMEM] * len(outs),
        scratch_shapes=scratch,
        compiler_params=pltpu.CompilerParams(vmem_limit_bytes=mib << 20),
        name=name,
    )(*args)


def after(value, *others):
    return lax.optimization_barrier((value, *others))[0]


def body(hidden, query_weight, key_value_weight, down_maps, up_maps, request_start, adapters):
    rows = hidden.shape[0]
    bf16, f32 = jnp.bfloat16, jnp.float32
    of = jax.ShapeDtypeStruct
    *sends, maps = call(
        pack_kernel,
        "pack",
        [of((1280, 128), bf16)] * 5 + [of((down_maps.shape[0], 2 * RANK, 128), bf16)],
        query_weight,
        key_value_weight.T,
        jnp.transpose(down_maps, (0, 2, 1)),
        up_maps,
        scratch=[pltpu.SemaphoreType.DMA((10 * NZ + 2,))],
        space=pltpu.HBM,
        mib=PACK_MIB,
    )
    twin = xh_swap(maps)
    cosines, sines = call(rope_kernel, "rope", [of((rows, HEAD_SIZE), f32)] * 2, request_start, scalars=1)
    ring = [(hidden, hidden)]

    def ring_step(*others):
        r, l = ring[-1]
        if len(ring) > 1:
            r, l = after(r, l, *others), after(l, r, *others)
        ring.append((z_shift(r, 1), z_shift(l, -1) if len(ring) < 4 else None))

    def added(low, sent, also=()):
        outs = [of((RANK, rows), f32)] + [of((RANK, rows), t) for t in also]
        return call(add_kernel, "low_add", outs, low, sent)

    ring_step()
    mine = [weight_send(sends[0], 0), weight_send(after(sends[1], *ring[1]), 1)]
    ring_step(mine[0], twin)
    near = jnp.stack([maps, after(twin, *ring[1])])
    far = core_swap(near)
    mine += [weight_send(after(sends[k], *ring[2]), k) for k in (2, 3)]
    low = call(low_kernel, "low", of((RANK, rows), f32), adapters, hidden, near, far, scalars=1)
    ring_step(mine[1], low, cosines)
    (low,) = added(low, z_xor(low, 1))
    ring_step(mine[2], low)
    mine[3] = after(mine[3], *ring[3])
    other = core_swap(call(stack_kernel, "stack", of((4, 1280, 128), bf16), *mine))
    low = after(low, *ring[3])
    low, narrow = added(low, z_xor(low, 2), (bf16,))
    (low,) = added(low, z_xor(narrow, 4))
    right, left = zip(*ring)

    shards = [hidden, left[1], left[2], left[3], right[4], right[3], right[2], right[1]]
    weights = (sends[4], *mine, other)
    *kv_parts, gathered = call(
        kv_product_kernel,
        "kv_product",
        [of((576, 128), bf16)] * NY + [of((rows, 1024), bf16)],
        *shards,
        *weights,
        low,
        scratch=[pltpu.VMEM((256, 1024), bf16)],
        mib=8,
    )
    kv_got = [y_shift(kv_parts[dy], dy) for dy in (2, 1, 3)]
    near_a, far_a, *b_parts = call(
        q_product_kernel,
        "q_product",
        [of((NY * TA, 128), bf16)] * 2 + [of((2 * TB, 128), bf16)] * NY,
        gathered,
        *weights,
        scratch=[pltpu.VMEM((NY, 1024, 256), bf16)],
        mib=10,
    )
    b_got = [y_shift(b_parts[dy], dy) for dy in (2, 1, 3)]
    kv_sum, x_send = call(
        kv_join_kernel,
        "kv_join",
        [of((576, 128), f32), of((NY * TA + 576, 128), bf16)],
        kv_parts[0],
        *kv_got,
        far_a,
    )
    x_got = x_swap(x_send)
    a_own, kv_own, *a_sends = call(
        stage_a_kernel,
        "stage_a",
        [of((TA, 128), f32), of((576, 128), bf16)] + [of((TA + 576, 128), bf16)] * (NY - 1),
        near_a,
        x_got,
        kv_sum,
    )
    a_got = {dy: y_shift(a_sends[dy - 1], dy) for dy in (2, 1, 3)}
    b_own, b_send = call(
        stage_b_kernel, "stage_b", [of((TB, 128), f32), of((TB, 128), bf16)], b_parts[0], *b_got
    )
    b_last = x_swap(b_send)

    return call(
        attention_kernel,
        "attention",
        of((rows, HEAD_SIZE), bf16),
        adapters,
        request_start,
        a_own,
        *[a_got[dy] for dy in (1, 2, 3)],
        b_own,
        b_last,
        kv_own,
        near,
        far,
        cosines,
        sines,
        scalars=2,
        scratch=[pltpu.VMEM((256, rows), bf16)] + [pltpu.VMEM((rows, HEAD_SIZE), bf16)] * 2 + [pltpu.VMEM((8, RANK, 128), bf16)],
        mib=8,
    )


def solution(mesh):
    fine = Mesh(mesh.devices.reshape(NXH, NC, NZ, NX, NY), REQ_AXES + TP_AXES)
    in_specs = (
        P(REQ_AXES, TP_AXES),
        P(None, TP_AXES),
        P(None, TP_AXES),
        P(REQ_AXES, TP_AXES, None),
        P(REQ_AXES, None, TP_AXES),
        P(REQ_AXES),
        P(REQ_AXES),
    )
    return jax.shard_map(
        body, mesh=fine, in_specs=in_specs, out_specs=P(REQ_AXES, TP_AXES), check_vma=False
    )
```

```python
import functools
import math

import jax
import jax.numpy as jnp
from jax import lax
from jax.experimental import pallas as pl
from jax.experimental.pallas import tpu as pltpu
from jax.sharding import Mesh, PartitionSpec as P

HEAD_SIZE = 128
BLOCK = 128
RANK = 32
ROPE_BASE = 500000.0
ADAPTER_SCALE = 2.0
NXH, NC, NZ, NX, NY = 2, 2, 8, 2, 4
REQ_AXES = ("xh", "c")
TP_AXES = ("z", "xl", "y")
NP = NX * NY
TA, TB = 384, 640
PACK_MIB = 56
VMEM = pl.BlockSpec(memory_space=pltpu.VMEM)
SMEM = pl.BlockSpec(memory_space=pltpu.SMEM)


def z_shift(v, s):
    return lax.ppermute(v, "z", [(i, (i + s) % NZ) for i in range(NZ)])


def z_xor(v, s):
    return lax.ppermute(v, "z", [(i, i ^ s) for i in range(NZ)])


def y_xor(v, s):
    return lax.ppermute(v, "y", [(i, i ^ s) for i in range(NY)])


def x_swap(v):
    return lax.ppermute(v, "xl", [(0, 1), (1, 0)])


def core_swap(v):
    return lax.ppermute(v, "c", [(0, 1), (1, 0)])


def xh_swap(v):
    return lax.ppermute(v, "xh", [(0, 1), (1, 0)])


def y_shift(v, s):
    return lax.ppermute(v, "y", [(i, (i + s) % NY) for i in range(NY)])


SERVED = ((4, 6, 1), (5, 7, 3, 2))
FLIP = [dx * NY + (-dy) % NY for dx in range(NX) for dy in range(NY)]


def weight_send(v, k):
    route = []
    for xh in range(NXH):
        for c in range(NC):
            if k >= len(SERVED[c]):
                continue
            dx, dy = divmod(SERVED[c][k], NY)
            for xl in range(NX):
                for y in range(NY):
                    at = xh * NX + xl
                    if dx:
                        to = at ^ 1 if c == 0 else (at + 1 if at % 2 else at - 1) % 4
                    else:
                        to = at
                    src = ((xh * NC + c) * NX + xl) * NY + y
                    dst = ((to // NX * NC + c) * NX + to % NX) * NY + (y + dy) % NY
                    route.append((src, dst))
    return lax.ppermute(v, ("xh", "c", "xl", "y"), route)


def run_copies(pairs, sem):
    copies = [pltpu.make_async_copy(src, dst, sem.at[i]) for i, (src, dst) in enumerate(pairs)]
    for copy in copies:
        copy.start()
    for copy in copies:
        copy.wait()


def pack_kernel(wq_ref, kv_ref, down_ref, up_ref, *refs):
    outs, maps, sem = refs[:5], refs[5], refs[6]
    z, xl, y, c = (lax.axis_index(a) for a in ("z", "xl", "y", "c"))
    pairs = [(down_ref, maps.at[:, 0:RANK, :]), (up_ref, maps.at[:, RANK : 2 * RANK, :])]
    for k in range(5):
        d = 0
        if k < 4:
            d = jnp.where(c == 0, (SERVED[0] + (0,))[k], SERVED[1][k])
        p = (xl ^ (d // NY)) * NY + ((y + d) & (NY - 1))
        for j in range(NZ):
            row = pl.multiple_of((((z + j) & (NZ - 1)) * NP + p) * 128, 128)
            pairs.append((wq_ref.at[pl.ds(row, 128), :], outs[k].at[j * 128 : (j + 1) * 128, :]))
            pairs.append((kv_ref.at[:, pl.ds(row, 128)], outs[k].at[1024 + j * 32 : 1056 + j * 32, :]))
    run_copies(pairs, sem)


def stack_kernel(*refs):
    for i, ref in enumerate(refs[:-1]):
        refs[-1][i] = ref[...]


def add_kernel(a_ref, b_ref, *outs):
    total = a_ref[...] + b_ref[...].astype(jnp.float32)
    outs[0][...] = total
    for out in outs[1:]:
        out[...] = total.astype(out.dtype)


def rope_kernel(start_ref, cos_ref, sin_ref):
    half = HEAD_SIZE // 2
    lane = lax.broadcasted_iota(jnp.int32, (BLOCK, HEAD_SIZE), 1)
    row = lax.broadcasted_iota(jnp.int32, (BLOCK, HEAD_SIZE), 0)
    steps = (lane & (half - 1)).astype(jnp.float32)
    inverse = jnp.exp(-(2.0 * steps / HEAD_SIZE) * math.log(ROPE_BASE))
    sign = jnp.where(lane < half, -1.0, 1.0).astype(jnp.float32)
    place = row.astype(jnp.float32) * inverse
    cos_in, sin_in = jnp.cos(place), jnp.sin(place)
    blocks = cos_ref.shape[0] // BLOCK
    ahead = lax.broadcasted_iota(jnp.int32, (8, HEAD_SIZE), 0).astype(jnp.float32) * BLOCK * inverse[0:8, :]
    cos_out, sin_out = jnp.cos(ahead), jnp.sin(ahead)
    first = (lax.axis_index("xh") * NC + lax.axis_index("c")) * blocks
    which = lax.broadcasted_iota(jnp.int32, (8, HEAD_SIZE), 0)
    for b in range(blocks):
        chosen = which == first + b - start_ref[b * BLOCK]
        co = jnp.sum(jnp.where(chosen, cos_out, 0.0), axis=0, keepdims=True)
        so = jnp.sum(jnp.where(chosen, sin_out, 0.0), axis=0, keepdims=True)
        rows = slice(b * BLOCK, (b + 1) * BLOCK)
        cos_ref[rows, :] = cos_in * co - sin_in * so
        sin_ref[rows, :] = (sin_in * co + cos_in * so) * sign


def low_kernel(ad_ref, h_ref, near_ref, far_ref, out_ref):
    c, xh = lax.axis_index("c"), lax.axis_index("xh")
    per = near_ref.shape[1]
    for b in range(h_ref.shape[0] // BLOCK):
        a = ad_ref[b]
        owner = a // per
        at = a - owner * per
        xr, cr = (owner // NC) ^ xh, (owner % NC) ^ c
        down = jnp.where(cr == 0, near_ref[xr, at, 0:RANK, :], far_ref[xr, at, 0:RANK, :])
        out_ref[:, b * BLOCK : (b + 1) * BLOCK] = lax.dot_general(
            down,
            h_ref[b * BLOCK : (b + 1) * BLOCK, :],
            (((1,), (1,)), ((), ())),
            preferred_element_type=jnp.float32,
        )


def for_each_piece(own, mine, other, place):
    place(own, 0)
    c = lax.axis_index("c")
    for core in range(NC):

        @pl.when(c == core)
        def _():
            for k, d in enumerate(SERVED[core]):
                place(mine[k], FLIP[d])
            for k, d in enumerate(SERVED[1 - core]):
                place(other[k], FLIP[d])


def kv_product_kernel(*refs):
    h_refs, own, mine, other = refs[0:8], refs[8], refs[9:13], refs[13]
    outs, hbuf, kvw = refs[14:18], refs[18], refs[19]
    other = [other.at[k] for k in range(4)]
    for j in range(8):
        hbuf[:, j * 128 : (j + 1) * 128] = h_refs[j][...]

    def place(ref, d):
        for j in range(NZ):
            kvw[d * 32 : (d + 1) * 32, j * 128 : (j + 1) * 128] = ref[1024 + j * 32 : 1056 + j * 32, :]

    for_each_piece(own, mine, other, place)
    kv = lax.dot_general(
        kvw[...], hbuf[...], (((1,), (1,)), ((), ())), preferred_element_type=jnp.float32
    ).astype(jnp.bfloat16)
    for d in range(NP):
        dx, dy = divmod(d, NY)
        for t in range(8):
            at = t * 64 + dx * 32
            outs[dy][at : at + 32, :] = kv[d * 32 : (d + 1) * 32, t * 128 : (t + 1) * 128]


def q_product_kernel(hbuf, own, *refs):
    mine, other = refs[0:4], [refs[4].at[k] for k in range(4)]
    near_ref, far_ref, outs, wq = refs[5], refs[6], refs[7:11], refs[11]

    def place(ref, d):
        dx, dy = divmod(d, NY)
        wq[dy, :, dx * 128 : (dx + 1) * 128] = ref[0:1024, :]

    for_each_piece(own, mine, other, place)
    for dy in range(NY):
        q = jnp.dot(hbuf[0:TA, :], wq[dy], preferred_element_type=jnp.float32).astype(jnp.bfloat16)
        near_ref[dy * TA : (dy + 1) * TA, :] = q[:, 0:128]
        far_ref[dy * TA : (dy + 1) * TA, :] = q[:, 128:256]
    for dy in range(NY):
        q = jnp.dot(hbuf[TA:1024, :], wq[dy], preferred_element_type=jnp.float32).astype(jnp.bfloat16)
        outs[dy][0:TB, :] = q[:, 0:128]
        outs[dy][TB : 2 * TB, :] = q[:, 128:256]


def wide(ref, rows):
    return ref[rows, :].astype(jnp.float32)


def kv_join_kernel(k0, k1, k2, k3, far_ref, sum_ref, send_ref):
    total = wide(k0, ...) + wide(k1, ...) + wide(k2, ...) + wide(k3, ...)
    sum_ref[...] = total
    send_ref[0 : NY * TA, :] = far_ref[...]
    send_ref[NY * TA :, :] = total.astype(jnp.bfloat16)


def stage_a_kernel(near_ref, got_ref, kv_ref, own_ref, kv_out, *sends):
    for t in range(8):
        for dx in range(NX):
            a, b = t * 64 + dx * 32, NY * TA + t * 64 + (1 - dx) * 32
            kv_out[a : a + 32, :] = (kv_ref[a : a + 32, :] + wide(got_ref, slice(b, b + 32))).astype(jnp.bfloat16)
    for dy in range(NY):
        rows = slice(dy * TA, (dy + 1) * TA)
        total = wide(near_ref, rows) + wide(got_ref, rows)
        if dy == 0:
            own_ref[...] = total
        else:
            sends[dy - 1][0:TA, :] = total.astype(jnp.bfloat16)
            sends[dy - 1][TA:, :] = kv_out[...]


def stage_b_kernel(b0, b1, b2, b3, own_ref, send_ref):
    for dx, out in enumerate((own_ref, send_ref)):
        rows = slice(dx * TB, (dx + 1) * TB)
        out[...] = (wide(b0, rows) + wide(b1, rows) + wide(b2, rows) + wide(b3, rows)).astype(out.dtype)


def attention_kernel(ad_ref, start_ref, *refs):
    a_own, a_got, b_own, b_got, kv_own = refs[0], refs[1:4], refs[4], refs[5], refs[6]
    low_ref, near_ref, far_ref, cos_ref, sin_ref = refs[7:12]
    out_ref = refs[12]
    kvt, k_buf, v_buf = refs[13:16]
    xl, y, c, xh = (lax.axis_index(a) for a in ("xl", "y", "c", "xh"))
    first = (xh * NC + c) * 8
    for i in range(NY):
        ref, base = (kv_own, 0) if i == 0 else (a_got[i - 1], TA)
        for dx in range(NX):
            p = (xl ^ dx) * NY + ((y - i) & (NY - 1))
            at = pl.multiple_of(p * 32, 32)
            for t in range(8):
                kvt[pl.ds(at, 32), t * 128 : (t + 1) * 128] = ref[base + t * 64 + dx * 32 : base + t * 64 + dx * 32 + 32, :]

    def rope(v, rows):
        return v * cos_ref[rows, :] + pltpu.roll(v, 64, 1) * sin_ref[rows, :]

    for t in range(8):
        rows = slice(t * 128, (t + 1) * 128)
        k = kvt[0:128, rows].astype(jnp.float32).T
        k_buf[rows, :] = rope(k, rows).astype(jnp.bfloat16)
        v_buf[rows, :] = kvt[128:256, rows].T
    per = near_ref.shape[1]
    factor = math.log2(math.e) / math.sqrt(HEAD_SIZE)
    for b in range(8):
        rows = slice(b * 128, (b + 1) * 128)
        a = ad_ref[b]
        owner = a // per
        at = a - owner * per
        xr, cr = (owner // NC) ^ xh, (owner % NC) ^ c
        up = jnp.where(cr == 0, near_ref[xr, at, RANK : 2 * RANK, :], far_ref[xr, at, RANK : 2 * RANK, :])
        q = ADAPTER_SCALE * lax.dot_general(
            low_ref[:, rows], up, (((0,), (0,)), ((), ())), preferred_element_type=jnp.float32
        )
        if b * 128 < TA:
            q += a_own[rows, :]
            for ref in a_got:
                q += wide(ref, rows)
        else:
            part = slice(b * 128 - TA, (b + 1) * 128 - TA)
            q += b_own[part, :] + wide(b_got, part)
        q = rope(q, rows).astype(jnp.bfloat16)
        n = (b + 1) * 128
        s = lax.dot_general(
            q, k_buf[0:n, :], (((1,), (1,)), ((), ())), preferred_element_type=jnp.float32
        )
        col = lax.broadcasted_iota(jnp.int32, (128, n), 1)
        row = lax.broadcasted_iota(jnp.int32, (128, n), 0) + b * 128
        allowed = (col >= (start_ref[b * BLOCK] - first) * BLOCK) & (col <= row)
        s = jnp.where(allowed, s, -1e30)
        e = jnp.exp2((s - jnp.max(s, axis=1, keepdims=True)) * factor)
        mixed = jnp.dot(e.astype(jnp.bfloat16), v_buf[0:n, :], preferred_element_type=jnp.float32)
        out_ref[rows, :] = (mixed * (1.0 / jnp.sum(e, axis=1, keepdims=True))).astype(jnp.bfloat16)


def call(kernel, name, outs, *args, scalars=0, scratch=(), mib=4, space=pltpu.VMEM):
    single = isinstance(outs, jax.ShapeDtypeStruct)
    return pl.pallas_call(
        kernel,
        out_shape=outs,
        in_specs=[SMEM] * scalars + [pl.BlockSpec(memory_space=space)] * (len(args) - scalars),
        out_specs=VMEM if single else [VMEM] * len(outs),
        scratch_shapes=scratch,
        compiler_params=pltpu.CompilerParams(vmem_limit_bytes=mib << 20),
        name=name,
    )(*args)


def after(value, *others):
    return lax.optimization_barrier((value, *others))[0]


def body(hidden, query_weight, key_value_weight, down_maps, up_maps, request_start, adapters):
    rows = hidden.shape[0]
    bf16, f32 = jnp.bfloat16, jnp.float32
    of = jax.ShapeDtypeStruct
    *sends, maps = call(
        pack_kernel,
        "pack",
        [of((1280, 128), bf16)] * 5 + [of((down_maps.shape[0], 2 * RANK, 128), bf16)],
        query_weight,
        key_value_weight.T,
        jnp.transpose(down_maps, (0, 2, 1)),
        up_maps,
        scratch=[pltpu.SemaphoreType.DMA((10 * NZ + 2,))],
        space=pltpu.HBM,
        mib=PACK_MIB,
    )
    twin = xh_swap(maps)
    cosines, sines = call(rope_kernel, "rope", [of((rows, HEAD_SIZE), f32)] * 2, request_start, scalars=1)
    ring = [(hidden, hidden)]

    def ring_step(*others):
        r, l = ring[-1]
        if len(ring) > 1:
            r, l = after(r, l, *others), after(l, r, *others)
        ring.append((z_shift(r, 1), z_shift(l, -1) if len(ring) < 4 else None))

    def added(low, sent, also=()):
        outs = [of((RANK, rows), f32)] + [of((RANK, rows), t) for t in also]
        return call(add_kernel, "low_add", outs, low, sent)

    def added(low, sent, *first, also=()):
        outs = [of((RANK, rows), f32)] + [of((RANK, rows), t) for t in also]
        return call(add_kernel, "low_add", outs, low, after(sent, *first))

    ring_step()
    mine = [weight_send(sends[0], 0), weight_send(after(sends[1], *ring[1]), 1)]
    ring_step(sends[1])
    near = jnp.stack([maps, after(twin, *ring[1])])
    far = core_swap(near)
    mine += [weight_send(after(sends[k], *ring[2]), k) for k in (2, 3)]
    low = call(low_kernel, "low", of((RANK, rows), f32), adapters, hidden, near, far, scalars=1)
    ring_step(mine[0], low, cosines)
    (low,) = added(low, x_swap(low), *ring[3])
    ring_step(mine[1])
    mine[3] = after(mine[3], *ring[3])
    other = core_swap(call(stack_kernel, "stack", of((4, 1280, 128), bf16), *mine))
    hidden = after(hidden, low)
    (low,) = added(low, y_xor(low, 1), ring[4][0])
    right, left = zip(*ring)

    shards = [hidden, left[1], left[2], left[3], right[4], right[3], right[2], right[1]]
    weights = (sends[4], *mine, other)
    *kv_parts, gathered = call(
        kv_product_kernel,
        "kv_product",
        [of((512, 128), bf16)] * NY + [of((rows, 1024), bf16)],
        *shards,
        *weights,
        scratch=[pltpu.VMEM((256, 1024), bf16)],
        mib=8,
    )
    kv_got = [y_shift(kv_parts[dy], dy) for dy in (2, 1, 3)]
    near_a, far_a, *b_parts = call(
        q_product_kernel,
        "q_product",
        [of((NY * TA, 128), bf16)] * 2 + [of((2 * TB, 128), bf16)] * NY,
        after(gathered, low),
        *weights,
        scratch=[pltpu.VMEM((NY, 1024, 256), bf16)],
        mib=10,
    )
    (low,) = added(low, y_xor(low, 2))
    b_got = [y_shift(b_parts[dy], dy) for dy in (2, 1, 3)]
    kv_sum, x_send = call(
        kv_join_kernel,
        "kv_join",
        [of((512, 128), f32), of((NY * TA + 512, 128), bf16)],
        kv_parts[0],
        *kv_got,
        after(far_a, low),
    )
    x_got = x_swap(x_send)
    (low,) = added(low, z_xor(low, 1))
    a_own, kv_own, *a_sends = call(
        stage_a_kernel,
        "stage_a",
        [of((TA, 128), f32), of((512, 128), bf16)] + [of((TA + 512, 128), bf16)] * (NY - 1),
        after(near_a, low),
        x_got,
        kv_sum,
    )
    a_got = {dy: y_shift(a_sends[dy - 1], dy) for dy in (2, 1, 3)}
    low, narrow = added(low, z_xor(low, 2), x_got, also=(bf16,))
    b_own, b_send = call(
        stage_b_kernel,
        "stage_b",
        [of((TB, 128), f32), of((TB, 128), bf16)],
        after(b_parts[0], narrow),
        *b_got,
    )
    _, low = added(low, z_xor(narrow, 4), also=(bf16,))
    b_last = x_swap(b_send)

    return call(
        attention_kernel,
        "attention",
        of((rows, HEAD_SIZE), bf16),
        adapters,
        request_start,
        a_own,
        *[a_got[dy] for dy in (1, 2, 3)],
        b_own,
        b_last,
        kv_own,
        low,
        near,
        far,
        cosines,
        sines,
        scalars=2,
        scratch=[pltpu.VMEM((256, rows), bf16)] + [pltpu.VMEM((rows, HEAD_SIZE), bf16)] * 2,
        mib=8,
    )


def solution(mesh):
    fine = Mesh(mesh.devices.reshape(NXH, NC, NZ, NX, NY), REQ_AXES + TP_AXES)
    in_specs = (
        P(REQ_AXES, TP_AXES),
        P(None, TP_AXES),
        P(None, TP_AXES),
        P(REQ_AXES, TP_AXES, None),
        P(REQ_AXES, None, TP_AXES),
        P(REQ_AXES),
        P(REQ_AXES),
    )
    return jax.shard_map(
        body, mesh=fine, in_specs=in_specs, out_specs=P(REQ_AXES, TP_AXES), check_vma=False
    )
```

```python
import functools
import math

import jax
import jax.numpy as jnp
from jax import lax
from jax.experimental import pallas as pl
from jax.experimental.pallas import tpu as pltpu
from jax.sharding import Mesh, PartitionSpec as P

HEAD_SIZE = 128
BLOCK = 128
RANK = 32
ROPE_BASE = 500000.0
ADAPTER_SCALE = 2.0
NXH, NC, NZ, NX, NY = 2, 2, 8, 2, 4
REQ_AXES = ("xh", "c")
TP_AXES = ("z", "xl", "y")
NP = NX * NY
TA, TB = 384, 640
PACK_MIB = 56
VMEM = pl.BlockSpec(memory_space=pltpu.VMEM)
SMEM = pl.BlockSpec(memory_space=pltpu.SMEM)


def z_shift(v, s):
    return lax.ppermute(v, "z", [(i, (i + s) % NZ) for i in range(NZ)])


def z_xor(v, s):
    return lax.ppermute(v, "z", [(i, i ^ s) for i in range(NZ)])


def y_xor(v, s):
    return lax.ppermute(v, "y", [(i, i ^ s) for i in range(NY)])


def x_swap(v):
    return lax.ppermute(v, "xl", [(0, 1), (1, 0)])


def core_swap(v):
    return lax.ppermute(v, "c", [(0, 1), (1, 0)])


def xh_swap(v):
    return lax.ppermute(v, "xh", [(0, 1), (1, 0)])


def y_shift(v, s):
    return lax.ppermute(v, "y", [(i, (i + s) % NY) for i in range(NY)])


SERVED = ((4, 6, 1), (5, 7, 3, 2))
FLIP = [dx * NY + (-dy) % NY for dx in range(NX) for dy in range(NY)]


def weight_send(v, k):
    route = []
    for xh in range(NXH):
        for c in range(NC):
            if k >= len(SERVED[c]):
                continue
            dx, dy = divmod(SERVED[c][k], NY)
            for xl in range(NX):
                for y in range(NY):
                    at = xh * NX + xl
                    if dx:
                        to = at ^ 1 if c == 0 else (at + 1 if at % 2 else at - 1) % 4
                    else:
                        to = at
                    src = ((xh * NC + c) * NX + xl) * NY + y
                    dst = ((to // NX * NC + c) * NX + to % NX) * NY + (y + dy) % NY
                    route.append((src, dst))
    return lax.ppermute(v, ("xh", "c", "xl", "y"), route)


def run_copies(pairs, sem):
    copies = [pltpu.make_async_copy(src, dst, sem.at[i]) for i, (src, dst) in enumerate(pairs)]
    for copy in copies:
        copy.start()
    for copy in copies:
        copy.wait()


def pack_kernel(wq_ref, kv_ref, down_ref, up_ref, *refs):
    outs, maps, sem = refs[:5], refs[5], refs[6]
    z, xl, y, c = (lax.axis_index(a) for a in ("z", "xl", "y", "c"))
    pairs = [(down_ref, maps.at[:, 0:RANK, :]), (up_ref, maps.at[:, RANK : 2 * RANK, :])]
    for k in range(5):
        d = 0
        if k < 4:
            d = jnp.where(c == 0, (SERVED[0] + (0,))[k], SERVED[1][k])
        p = (xl ^ (d // NY)) * NY + ((y + d) & (NY - 1))
        for j in range(NZ):
            row = pl.multiple_of((((z + j) & (NZ - 1)) * NP + p) * 128, 128)
            pairs.append((wq_ref.at[pl.ds(row, 128), :], outs[k].at[j * 128 : (j + 1) * 128, :]))
            pairs.append((kv_ref.at[:, pl.ds(row, 128)], outs[k].at[1024 + j * 32 : 1056 + j * 32, :]))
    run_copies(pairs, sem)


def stack_kernel(*refs):
    for i, ref in enumerate(refs[:-1]):
        refs[-1][i] = ref[...]


def add_kernel(a_ref, b_ref, *outs):
    total = a_ref[...] + b_ref[...].astype(jnp.float32)
    outs[0][...] = total
    for out in outs[1:]:
        out[...] = total.astype(out.dtype)


def rope_kernel(start_ref, cos_ref, sin_ref):
    half = HEAD_SIZE // 2
    lane = lax.broadcasted_iota(jnp.int32, (BLOCK, HEAD_SIZE), 1)
    row = lax.broadcasted_iota(jnp.int32, (BLOCK, HEAD_SIZE), 0)
    steps = (lane & (half - 1)).astype(jnp.float32)
    inverse = jnp.exp(-(2.0 * steps / HEAD_SIZE) * math.log(ROPE_BASE))
    sign = jnp.where(lane < half, -1.0, 1.0).astype(jnp.float32)
    place = row.astype(jnp.float32) * inverse
    cos_in, sin_in = jnp.cos(place), jnp.sin(place)
    blocks = cos_ref.shape[0] // BLOCK
    ahead = lax.broadcasted_iota(jnp.int32, (8, HEAD_SIZE), 0).astype(jnp.float32) * BLOCK * inverse[0:8, :]
    cos_out, sin_out = jnp.cos(ahead), jnp.sin(ahead)
    first = (lax.axis_index("xh") * NC + lax.axis_index("c")) * blocks
    which = lax.broadcasted_iota(jnp.int32, (8, HEAD_SIZE), 0)
    for b in range(blocks):
        chosen = which == first + b - start_ref[b * BLOCK]
        co = jnp.sum(jnp.where(chosen, cos_out, 0.0), axis=0, keepdims=True)
        so = jnp.sum(jnp.where(chosen, sin_out, 0.0), axis=0, keepdims=True)
        rows = slice(b * BLOCK, (b + 1) * BLOCK)
        cos_ref[rows, :] = cos_in * co - sin_in * so
        sin_ref[rows, :] = (sin_in * co + cos_in * so) * sign


def low_kernel(ad_ref, h_ref, near_ref, far_ref, out_ref):
    c, xh = lax.axis_index("c"), lax.axis_index("xh")
    per = near_ref.shape[1]
    for b in range(h_ref.shape[0] // BLOCK):
        a = ad_ref[b]
        owner = a // per
        at = a - owner * per
        xr, cr = (owner // NC) ^ xh, (owner % NC) ^ c
        down = jnp.where(cr == 0, near_ref[xr, at, 0:RANK, :], far_ref[xr, at, 0:RANK, :])
        out_ref[:, b * BLOCK : (b + 1) * BLOCK] = lax.dot_general(
            down,
            h_ref[b * BLOCK : (b + 1) * BLOCK, :],
            (((1,), (1,)), ((), ())),
            preferred_element_type=jnp.float32,
        )


def for_each_piece(own, mine, other, place):
    place(own, 0)
    c = lax.axis_index("c")
    for core in range(NC):

        @pl.when(c == core)
        def _():
            for k, d in enumerate(SERVED[core]):
                place(mine[k], FLIP[d])
            for k, d in enumerate(SERVED[1 - core]):
                place(other[k], FLIP[d])


def kv_product_kernel(*refs):
    h_refs, own, mine, other = refs[0:8], refs[8], refs[9:13], refs[13]
    outs, hbuf, kvw = refs[14:18], refs[18], refs[19]
    other = [other.at[k] for k in range(4)]
    for j in range(8):
        hbuf[:, j * 128 : (j + 1) * 128] = h_refs[j][...]

    def place(ref, d):
        for j in range(NZ):
            kvw[d * 32 : (d + 1) * 32, j * 128 : (j + 1) * 128] = ref[1024 + j * 32 : 1056 + j * 32, :]

    for_each_piece(own, mine, other, place)
    kv = lax.dot_general(
        kvw[...], hbuf[...], (((1,), (1,)), ((), ())), preferred_element_type=jnp.float32
    ).astype(jnp.bfloat16)
    for d in range(NP):
        dx, dy = divmod(d, NY)
        for t in range(8):
            at = t * 64 + dx * 32
            outs[dy][at : at + 32, :] = kv[d * 32 : (d + 1) * 32, t * 128 : (t + 1) * 128]


def q_product_kernel(hbuf, own, *refs):
    mine, other = refs[0:4], [refs[4].at[k] for k in range(4)]
    near_ref, far_ref, outs, wq = refs[5], refs[6], refs[7:11], refs[11]

    def place(ref, d):
        dx, dy = divmod(d, NY)
        wq[dy, :, dx * 128 : (dx + 1) * 128] = ref[0:1024, :]

    for_each_piece(own, mine, other, place)
    for dy in range(NY):
        q = jnp.dot(hbuf[0:TA, :], wq[dy], preferred_element_type=jnp.float32).astype(jnp.bfloat16)
        near_ref[dy * TA : (dy + 1) * TA, :] = q[:, 0:128]
        far_ref[dy * TA : (dy + 1) * TA, :] = q[:, 128:256]
    for dy in range(NY):
        q = jnp.dot(hbuf[TA:1024, :], wq[dy], preferred_element_type=jnp.float32).astype(jnp.bfloat16)
        outs[dy][0:TB, :] = q[:, 0:128]
        outs[dy][TB : 2 * TB, :] = q[:, 128:256]


def wide(ref, rows):
    return ref[rows, :].astype(jnp.float32)


def kv_join_kernel(k0, k1, k2, k3, far_ref, sum_ref, send_ref):
    total = wide(k0, ...) + wide(k1, ...) + wide(k2, ...) + wide(k3, ...)
    sum_ref[...] = total
    send_ref[0 : NY * TA, :] = far_ref[...]
    send_ref[NY * TA :, :] = total.astype(jnp.bfloat16)


def stage_a_kernel(near_ref, got_ref, kv_ref, own_ref, kv_out, *sends):
    for t in range(8):
        for dx in range(NX):
            a, b = t * 64 + dx * 32, NY * TA + t * 64 + (1 - dx) * 32
            kv_out[a : a + 32, :] = (kv_ref[a : a + 32, :] + wide(got_ref, slice(b, b + 32))).astype(jnp.bfloat16)
    for dy in range(NY):
        rows = slice(dy * TA, (dy + 1) * TA)
        total = wide(near_ref, rows) + wide(got_ref, rows)
        if dy == 0:
            own_ref[...] = total
        else:
            sends[dy - 1][0:TA, :] = total.astype(jnp.bfloat16)
            sends[dy - 1][TA:, :] = kv_out[...]


def stage_b_kernel(b0, b1, b2, b3, own_ref, send_ref):
    for dx, out in enumerate((own_ref, send_ref)):
        rows = slice(dx * TB, (dx + 1) * TB)
        out[...] = (wide(b0, rows) + wide(b1, rows) + wide(b2, rows) + wide(b3, rows)).astype(out.dtype)


def attention_kernel(ad_ref, start_ref, *refs):
    a_own, a_got, b_own, b_got, kv_own = refs[0], refs[1:4], refs[4], refs[5], refs[6]
    low_ref, near_ref, far_ref, cos_ref, sin_ref = refs[7:12]
    out_ref = refs[12]
    kvt, k_buf, v_buf = refs[13:16]
    xl, y, c, xh = (lax.axis_index(a) for a in ("xl", "y", "c", "xh"))
    first = (xh * NC + c) * 8
    for i in range(NY):
        ref, base = (kv_own, 0) if i == 0 else (a_got[i - 1], TA)
        for dx in range(NX):
            p = (xl ^ dx) * NY + ((y - i) & (NY - 1))
            at = pl.multiple_of(p * 32, 32)
            for t in range(8):
                kvt[pl.ds(at, 32), t * 128 : (t + 1) * 128] = ref[base + t * 64 + dx * 32 : base + t * 64 + dx * 32 + 32, :]

    def rope(v, rows):
        return v * cos_ref[rows, :] + pltpu.roll(v, 64, 1) * sin_ref[rows, :]

    for t in range(8):
        rows = slice(t * 128, (t + 1) * 128)
        k = kvt[0:128, rows].astype(jnp.float32).T
        k_buf[rows, :] = rope(k, rows).astype(jnp.bfloat16)
        v_buf[rows, :] = kvt[128:256, rows].T
    per = near_ref.shape[1]
    factor = math.log2(math.e) / math.sqrt(HEAD_SIZE)
    for b in range(8):
        rows = slice(b * 128, (b + 1) * 128)
        a = ad_ref[b]
        owner = a // per
        at = a - owner * per
        xr, cr = (owner // NC) ^ xh, (owner % NC) ^ c
        up = jnp.where(cr == 0, near_ref[xr, at, RANK : 2 * RANK, :], far_ref[xr, at, RANK : 2 * RANK, :])
        q = ADAPTER_SCALE * lax.dot_general(
            low_ref[:, rows], up, (((0,), (0,)), ((), ())), preferred_element_type=jnp.float32
        )
        if b * 128 < TA:
            q += a_own[rows, :]
            for ref in a_got:
                q += wide(ref, rows)
        else:
            part = slice(b * 128 - TA, (b + 1) * 128 - TA)
            q += b_own[part, :] + wide(b_got, part)
        q = rope(q, rows).astype(jnp.bfloat16)
        n = (b + 1) * 128
        s = lax.dot_general(
            q, k_buf[0:n, :], (((1,), (1,)), ((), ())), preferred_element_type=jnp.float32
        )
        col = lax.broadcasted_iota(jnp.int32, (128, n), 1)
        row = lax.broadcasted_iota(jnp.int32, (128, n), 0) + b * 128
        allowed = (col >= (start_ref[b * BLOCK] - first) * BLOCK) & (col <= row)
        s = jnp.where(allowed, s, -1e30)
        e = jnp.exp2((s - jnp.max(s, axis=1, keepdims=True)) * factor)
        mixed = jnp.dot(e.astype(jnp.bfloat16), v_buf[0:n, :], preferred_element_type=jnp.float32)
        out_ref[rows, :] = (mixed * (1.0 / jnp.sum(e, axis=1, keepdims=True))).astype(jnp.bfloat16)


def call(kernel, name, outs, *args, scalars=0, scratch=(), mib=4, space=pltpu.VMEM):
    single = isinstance(outs, jax.ShapeDtypeStruct)
    return pl.pallas_call(
        kernel,
        out_shape=outs,
        in_specs=[SMEM] * scalars + [pl.BlockSpec(memory_space=space)] * (len(args) - scalars),
        out_specs=VMEM if single else [VMEM] * len(outs),
        scratch_shapes=scratch,
        compiler_params=pltpu.CompilerParams(vmem_limit_bytes=mib << 20),
        name=name,
    )(*args)


def after(value, *others):
    return lax.optimization_barrier((value, *others))[0]


def body(hidden, query_weight, key_value_weight, down_maps, up_maps, request_start, adapters):
    rows = hidden.shape[0]
    bf16, f32 = jnp.bfloat16, jnp.float32
    of = jax.ShapeDtypeStruct
    *sends, maps = call(
        pack_kernel,
        "pack",
        [of((1280, 128), bf16)] * 5 + [of((down_maps.shape[0], 2 * RANK, 128), bf16)],
        query_weight,
        key_value_weight.T,
        jnp.transpose(down_maps, (0, 2, 1)),
        up_maps,
        scratch=[pltpu.SemaphoreType.DMA((10 * NZ + 2,))],
        space=pltpu.HBM,
        mib=PACK_MIB,
    )
    twin = xh_swap(maps)
    cosines, sines = call(rope_kernel, "rope", [of((rows, HEAD_SIZE), f32)] * 2, request_start, scalars=1)
    hidden = after(hidden, sends[0])
    ring = [(hidden, hidden)]

    def ring_step(*others):
        r, l = ring[-1]
        if len(ring) > 1:
            r, l = after(r, l, *others), after(l, r, *others)
        ring.append((z_shift(r, 1), z_shift(l, -1) if len(ring) < 4 else None))

    def added(low, sent, also=()):
        outs = [of((RANK, rows), f32)] + [of((RANK, rows), t) for t in also]
        return call(add_kernel, "low_add", outs, low, sent)

    def added(low, sent, *first, also=()):
        outs = [of((RANK, rows), f32)] + [of((RANK, rows), t) for t in also]
        return call(add_kernel, "low_add", outs, low, after(sent, *first))

    ring_step()
    mine = [weight_send(sends[0], 0), weight_send(after(sends[1], *ring[1]), 1)]
    ring_step()
    near = jnp.stack([maps, after(twin, *ring[1])])
    far = core_swap(near)
    mine += [weight_send(after(sends[k], *ring[2], mine[k - 2]), k) for k in (2, 3)]
    ring_step(near)
    low = call(low_kernel, "low", of((RANK, rows), f32), adapters, hidden, near, after(far, *ring[2]), scalars=1)
    ring_step(low)
    (low,) = added(low, x_swap(low), *ring[3])
    mine[3] = after(mine[3], *ring[3], cosines)
    other = core_swap(call(stack_kernel, "stack", of((4, 1280, 128), bf16), *mine))
    hidden = after(hidden, low)
    (low,) = added(low, y_xor(low, 1), ring[4][0])
    right, left = zip(*ring)

    shards = [hidden, left[1], left[2], left[3], right[4], right[3], right[2], right[1]]
    weights = (sends[4], *mine, other)
    *kv_parts, gathered = call(
        kv_product_kernel,
        "kv_product",
        [of((512, 128), bf16)] * NY + [of((rows, 1024), bf16)],
        *shards,
        *weights,
        scratch=[pltpu.VMEM((256, 1024), bf16)],
        mib=8,
    )
    kv_got = [y_shift(kv_parts[dy], dy) for dy in (2, 1, 3)]
    near_a, far_a, *b_parts = call(
        q_product_kernel,
        "q_product",
        [of((NY * TA, 128), bf16)] * 2 + [of((2 * TB, 128), bf16)] * NY,
        after(gathered, low),
        *weights,
        scratch=[pltpu.VMEM((NY, 1024, 256), bf16)],
        mib=10,
    )
    (low,) = added(low, y_xor(low, 2))
    b_got = [y_shift(b_parts[dy], dy) for dy in (2, 1, 3)]
    kv_sum, x_send = call(
        kv_join_kernel,
        "kv_join",
        [of((512, 128), f32), of((NY * TA + 512, 128), bf16)],
        kv_parts[0],
        *kv_got,
        after(far_a, low),
    )
    x_got = x_swap(x_send)
    (low,) = added(low, z_xor(low, 1))
    a_own, kv_own, *a_sends = call(
        stage_a_kernel,
        "stage_a",
        [of((TA, 128), f32), of((512, 128), bf16)] + [of((TA + 512, 128), bf16)] * (NY - 1),
        after(near_a, low),
        x_got,
        kv_sum,
    )
    a_got = {dy: y_shift(a_sends[dy - 1], dy) for dy in (2, 1, 3)}
    low, narrow = added(low, z_xor(low, 2), x_got, also=(bf16,))
    _, low = added(low, z_xor(narrow, 4), also=(bf16,))
    b_own, b_send = call(
        stage_b_kernel,
        "stage_b",
        [of((TB, 128), f32), of((TB, 128), bf16)],
        after(b_parts[0], low),
        *b_got,
    )
    b_last = x_swap(b_send)

    return call(
        attention_kernel,
        "attention",
        of((rows, HEAD_SIZE), bf16),
        adapters,
        request_start,
        a_own,
        *[a_got[dy] for dy in (1, 2, 3)],
        b_own,
        b_last,
        kv_own,
        low,
        near,
        far,
        cosines,
        sines,
        scalars=2,
        scratch=[pltpu.VMEM((256, rows), bf16)] + [pltpu.VMEM((rows, HEAD_SIZE), bf16)] * 2,
        mib=8,
    )


def solution(mesh):
    fine = Mesh(mesh.devices.reshape(NXH, NC, NZ, NX, NY), REQ_AXES + TP_AXES)
    in_specs = (
        P(REQ_AXES, TP_AXES),
        P(None, TP_AXES),
        P(None, TP_AXES),
        P(REQ_AXES, TP_AXES, None),
        P(REQ_AXES, None, TP_AXES),
        P(REQ_AXES),
        P(REQ_AXES),
    )
    return jax.shard_map(
        body, mesh=fine, in_specs=in_specs, out_specs=P(REQ_AXES, TP_AXES), check_vma=False
    )
```

```python
import functools
import math

import jax
import jax.numpy as jnp
from jax import lax
from jax.experimental import pallas as pl
from jax.experimental.pallas import tpu as pltpu
from jax.sharding import Mesh, PartitionSpec as P

HEAD_SIZE = 128
BLOCK = 128
RANK = 32
ROPE_BASE = 500000.0
ADAPTER_SCALE = 2.0
NXH, NC, NZ, NX, NY = 2, 2, 8, 2, 4
REQ_AXES = ("xh", "c")
TP_AXES = ("z", "xl", "y")
NP = NX * NY
TA, TB = 384, 640
PACK_MIB = 56
VMEM = pl.BlockSpec(memory_space=pltpu.VMEM)
SMEM = pl.BlockSpec(memory_space=pltpu.SMEM)


def z_shift(v, s):
    return lax.ppermute(v, "z", [(i, (i + s) % NZ) for i in range(NZ)])


def z_xor(v, s):
    return lax.ppermute(v, "z", [(i, i ^ s) for i in range(NZ)])


def y_xor(v, s):
    return lax.ppermute(v, "y", [(i, i ^ s) for i in range(NY)])


def x_swap(v):
    return lax.ppermute(v, "xl", [(0, 1), (1, 0)])


def core_swap(v):
    return lax.ppermute(v, "c", [(0, 1), (1, 0)])


def xh_swap(v):
    return lax.ppermute(v, "xh", [(0, 1), (1, 0)])


def y_shift(v, s):
    return lax.ppermute(v, "y", [(i, (i + s) % NY) for i in range(NY)])


SERVED = ((4, 6, 1), (5, 7, 3, 2))
FLIP = [dx * NY + (-dy) % NY for dx in range(NX) for dy in range(NY)]


def weight_send(v, k):
    route = []
    for xh in range(NXH):
        for c in range(NC):
            if k >= len(SERVED[c]):
                continue
            dx, dy = divmod(SERVED[c][k], NY)
            for xl in range(NX):
                for y in range(NY):
                    at = xh * NX + xl
                    if dx:
                        to = at ^ 1 if c == 0 else (at + 1 if at % 2 else at - 1) % 4
                    else:
                        to = at
                    src = ((xh * NC + c) * NX + xl) * NY + y
                    dst = ((to // NX * NC + c) * NX + to % NX) * NY + (y + dy) % NY
                    route.append((src, dst))
    return lax.ppermute(v, ("xh", "c", "xl", "y"), route)


def run_copies(pairs, sem):
    copies = [pltpu.make_async_copy(src, dst, sem.at[i]) for i, (src, dst) in enumerate(pairs)]
    for copy in copies:
        copy.start()
    for copy in copies:
        copy.wait()


def weight_pairs(wq_ref, kv_ref, out, d):
    z, xl, y = (lax.axis_index(a) for a in ("z", "xl", "y"))
    p = (xl ^ (d // NY)) * NY + ((y + d) & (NY - 1))
    pairs = []
    for j in range(NZ):
        row = pl.multiple_of((((z + j) & (NZ - 1)) * NP + p) * 128, 128)
        pairs.append((wq_ref.at[pl.ds(row, 128), :], out.at[j * 128 : (j + 1) * 128, :]))
        pairs.append((kv_ref.at[:, pl.ds(row, 128)], out.at[1024 + j * 32 : 1056 + j * 32, :]))
    return pairs


def pack_first_kernel(wq_ref, kv_ref, down_ref, up_ref, out, maps, sem):
    d = jnp.where(lax.axis_index("c") == 0, SERVED[0][0], SERVED[1][0])
    pairs = [(down_ref, maps.at[:, 0:RANK, :]), (up_ref, maps.at[:, RANK : 2 * RANK, :])]
    run_copies(pairs + weight_pairs(wq_ref, kv_ref, out, d), sem)


def pack_kernel(wq_ref, kv_ref, *refs):
    outs, sem = refs[:4], refs[4]
    c = lax.axis_index("c")
    pairs = []
    for k, out in enumerate(outs, 1):
        d = jnp.where(c == 0, (SERVED[0] + (0,))[k], SERVED[1][k]) if k < 4 else 0
        pairs += weight_pairs(wq_ref, kv_ref, out, d)
    run_copies(pairs, sem)


def stack_kernel(*refs):
    for i, ref in enumerate(refs[:-1]):
        refs[-1][i] = ref[...]


def add_kernel(a_ref, b_ref, out_ref):
    out_ref[...] = a_ref[...] + b_ref[...]


def rope_kernel(start_ref, cos_ref, sin_ref):
    half = HEAD_SIZE // 2
    lane = lax.broadcasted_iota(jnp.int32, (BLOCK, HEAD_SIZE), 1)
    row = lax.broadcasted_iota(jnp.int32, (BLOCK, HEAD_SIZE), 0)
    steps = (lane & (half - 1)).astype(jnp.float32)
    inverse = jnp.exp(-(2.0 * steps / HEAD_SIZE) * math.log(ROPE_BASE))
    sign = jnp.where(lane < half, -1.0, 1.0).astype(jnp.float32)
    place = row.astype(jnp.float32) * inverse
    cos_in, sin_in = jnp.cos(place), jnp.sin(place)
    blocks = cos_ref.shape[0] // BLOCK
    ahead = lax.broadcasted_iota(jnp.int32, (8, HEAD_SIZE), 0).astype(jnp.float32) * BLOCK * inverse[0:8, :]
    cos_out, sin_out = jnp.cos(ahead), jnp.sin(ahead)
    first = (lax.axis_index("xh") * NC + lax.axis_index("c")) * blocks
    which = lax.broadcasted_iota(jnp.int32, (8, HEAD_SIZE), 0)
    for b in range(blocks):
        chosen = which == first + b - start_ref[b * BLOCK]
        co = jnp.sum(jnp.where(chosen, cos_out, 0.0), axis=0, keepdims=True)
        so = jnp.sum(jnp.where(chosen, sin_out, 0.0), axis=0, keepdims=True)
        rows = slice(b * BLOCK, (b + 1) * BLOCK)
        cos_ref[rows, :] = cos_in * co - sin_in * so
        sin_ref[rows, :] = (sin_in * co + cos_in * so) * sign


def low_kernel(ad_ref, h_ref, near_ref, far_ref, out_ref):
    c, xh = lax.axis_index("c"), lax.axis_index("xh")
    per = near_ref.shape[1]
    for b in range(h_ref.shape[0] // BLOCK):
        a = ad_ref[b]
        owner = a // per
        at = a - owner * per
        xr, cr = (owner // NC) ^ xh, (owner % NC) ^ c
        down = jnp.where(cr == 0, near_ref[xr, at, 0:RANK, :], far_ref[xr, at, 0:RANK, :])
        out_ref[:, b * BLOCK : (b + 1) * BLOCK] = lax.dot_general(
            down,
            h_ref[b * BLOCK : (b + 1) * BLOCK, :],
            (((1,), (1,)), ((), ())),
            preferred_element_type=jnp.float32,
        )


def for_each_piece(own, mine, other, place):
    place(own, 0)
    c = lax.axis_index("c")
    for core in range(NC):

        @pl.when(c == core)
        def _():
            for k, d in enumerate(SERVED[core]):
                place(mine[k], FLIP[d])
            for k, d in enumerate(SERVED[1 - core]):
                place(other[k], FLIP[d])


def kv_product_kernel(*refs):
    h_refs, own, mine, other, low_ref = refs[0:8], refs[8], refs[9:13], refs[13], refs[14]
    outs, hbuf, kvw = refs[15:19], refs[19], refs[20]
    other = [other.at[k] for k in range(4)]
    y = lax.axis_index("y")
    for j in range(8):
        hbuf[:, j * 128 : (j + 1) * 128] = h_refs[j][...]
    for dy in range(NY):
        for t in range(2):
            at = pl.multiple_of((((y + dy) & (NY - 1)) * 2 + t) * 128, 128)
            outs[dy][512 + t * 32 : 544 + t * 32, :] = low_ref[:, pl.ds(at, 128)].astype(jnp.bfloat16)

    def place(ref, d):
        for j in range(NZ):
            kvw[d * 32 : (d + 1) * 32, j * 128 : (j + 1) * 128] = ref[1024 + j * 32 : 1056 + j * 32, :]

    for_each_piece(own, mine, other, place)
    kv = lax.dot_general(
        kvw[...], hbuf[...], (((1,), (1,)), ((), ())), preferred_element_type=jnp.float32
    ).astype(jnp.bfloat16)
    for d in range(NP):
        dx, dy = divmod(d, NY)
        for t in range(8):
            at = t * 64 + dx * 32
            outs[dy][at : at + 32, :] = kv[d * 32 : (d + 1) * 32, t * 128 : (t + 1) * 128]


def q_product_kernel(hbuf, own, *refs):
    mine, other = refs[0:4], [refs[4].at[k] for k in range(4)]
    near_ref, far_ref, outs, wq = refs[5], refs[6], refs[7:11], refs[11]

    def place(ref, d):
        dx, dy = divmod(d, NY)
        wq[dy, :, dx * 128 : (dx + 1) * 128] = ref[0:1024, :]

    for_each_piece(own, mine, other, place)
    for dy in range(NY):
        q = jnp.dot(hbuf[0:TA, :], wq[dy], preferred_element_type=jnp.float32).astype(jnp.bfloat16)
        near_ref[dy * TA : (dy + 1) * TA, :] = q[:, 0:128]
        far_ref[dy * TA : (dy + 1) * TA, :] = q[:, 128:256]
    for dy in range(NY):
        q = jnp.dot(hbuf[TA:1024, :], wq[dy], preferred_element_type=jnp.float32).astype(jnp.bfloat16)
        outs[dy][0:TB, :] = q[:, 0:128]
        outs[dy][TB : 2 * TB, :] = q[:, 128:256]


def wide(ref, rows):
    return ref[rows, :].astype(jnp.float32)


def kv_join_kernel(k0, k1, k2, k3, far_ref, sum_ref, low_ref, send_ref):
    total = wide(k0, ...) + wide(k1, ...) + wide(k2, ...) + wide(k3, ...)
    sum_ref[...] = total[0:512, :]
    low_ref[...] = total[512:576, :]
    send_ref[0 : NY * TA, :] = far_ref[...]
    send_ref[NY * TA :, :] = total[0:512, :].astype(jnp.bfloat16)


def stage_a_kernel(near_ref, got_ref, kv_ref, low_ref, own_ref, kv_out, *sends):
    for t in range(8):
        for dx in range(NX):
            a, b = t * 64 + dx * 32, NY * TA + t * 64 + (1 - dx) * 32
            kv_out[a : a + 32, :] = (kv_ref[a : a + 32, :] + wide(got_ref, slice(b, b + 32))).astype(jnp.bfloat16)
    kv_out[512:576, :] = low_ref[...].astype(jnp.bfloat16)
    for dy in range(NY):
        rows = slice(dy * TA, (dy + 1) * TA)
        total = wide(near_ref, rows) + wide(got_ref, rows)
        if dy == 0:
            own_ref[...] = total
        else:
            sends[dy - 1][0:TA, :] = total.astype(jnp.bfloat16)
            sends[dy - 1][TA:, :] = kv_out[...]


def stage_b_kernel(b0, b1, b2, b3, own_ref, send_ref):
    for dx, out in enumerate((own_ref, send_ref)):
        rows = slice(dx * TB, (dx + 1) * TB)
        out[...] = (wide(b0, rows) + wide(b1, rows) + wide(b2, rows) + wide(b3, rows)).astype(out.dtype)


def attention_kernel(ad_ref, start_ref, *refs):
    a_own, a_got, b_own, b_got, kv_own = refs[0], refs[1:4], refs[4], refs[5], refs[6]
    near_ref, far_ref, cos_ref, sin_ref = refs[7:11]
    out_ref = refs[11]
    kvt, k_buf, v_buf, low_buf = refs[12:16]
    xl, y, c, xh = (lax.axis_index(a) for a in ("xl", "y", "c", "xh"))
    first = (xh * NC + c) * 8
    for i in range(NY):
        ref, base = (kv_own, 0) if i == 0 else (a_got[i - 1], TA)
        for t in range(2):
            low_buf[((y - i) & (NY - 1)) * 2 + t] = ref[base + 512 + t * 32 : base + 544 + t * 32, :]
        for dx in range(NX):
            p = (xl ^ dx) * NY + ((y - i) & (NY - 1))
            at = pl.multiple_of(p * 32, 32)
            for t in range(8):
                kvt[pl.ds(at, 32), t * 128 : (t + 1) * 128] = ref[base + t * 64 + dx * 32 : base + t * 64 + dx * 32 + 32, :]

    def rope(v, rows):
        return v * cos_ref[rows, :] + pltpu.roll(v, 64, 1) * sin_ref[rows, :]

    for t in range(8):
        rows = slice(t * 128, (t + 1) * 128)
        k = kvt[0:128, rows].astype(jnp.float32).T
        k_buf[rows, :] = rope(k, rows).astype(jnp.bfloat16)
        v_buf[rows, :] = kvt[128:256, rows].T
    per = near_ref.shape[1]
    factor = math.log2(math.e) / math.sqrt(HEAD_SIZE)
    for b in range(8):
        rows = slice(b * 128, (b + 1) * 128)
        a = ad_ref[b]
        owner = a // per
        at = a - owner * per
        xr, cr = (owner // NC) ^ xh, (owner % NC) ^ c
        up = jnp.where(cr == 0, near_ref[xr, at, RANK : 2 * RANK, :], far_ref[xr, at, RANK : 2 * RANK, :])
        q = ADAPTER_SCALE * lax.dot_general(
            low_buf[b], up, (((0,), (0,)), ((), ())), preferred_element_type=jnp.float32
        )
        if b * 128 < TA:
            q += a_own[rows, :]
            for ref in a_got:
                q += wide(ref, rows)
        else:
            part = slice(b * 128 - TA, (b + 1) * 128 - TA)
            q += b_own[part, :] + wide(b_got, part)
        q = rope(q, rows).astype(jnp.bfloat16)
        n = (b + 1) * 128
        s = lax.dot_general(
            q, k_buf[0:n, :], (((1,), (1,)), ((), ())), preferred_element_type=jnp.float32
        )
        col = lax.broadcasted_iota(jnp.int32, (128, n), 1)
        row = lax.broadcasted_iota(jnp.int32, (128, n), 0) + b * 128
        allowed = (col >= (start_ref[b * BLOCK] - first) * BLOCK) & (col <= row)
        s = jnp.where(allowed, s, -1e30)
        e = jnp.exp2((s - jnp.max(s, axis=1, keepdims=True)) * factor)
        mixed = jnp.dot(e.astype(jnp.bfloat16), v_buf[0:n, :], preferred_element_type=jnp.float32)
        out_ref[rows, :] = (mixed * (1.0 / jnp.sum(e, axis=1, keepdims=True))).astype(jnp.bfloat16)


def call(kernel, name, outs, *args, scalars=0, scratch=(), mib=4, space=pltpu.VMEM):
    single = isinstance(outs, jax.ShapeDtypeStruct)
    return pl.pallas_call(
        kernel,
        out_shape=outs,
        in_specs=[SMEM] * scalars + [pl.BlockSpec(memory_space=space)] * (len(args) - scalars),
        out_specs=VMEM if single else [VMEM] * len(outs),
        scratch_shapes=scratch,
        compiler_params=pltpu.CompilerParams(vmem_limit_bytes=mib << 20),
        name=name,
    )(*args)


def after(value, *others):
    return lax.optimization_barrier((value, *others))[0]


def body(hidden, query_weight, key_value_weight, down_maps, up_maps, request_start, adapters):
    rows = hidden.shape[0]
    bf16, f32 = jnp.bfloat16, jnp.float32
    of = jax.ShapeDtypeStruct
    kv_rows = key_value_weight.T
    first, maps = call(
        pack_first_kernel,
        "pack_first",
        [of((1280, 128), bf16), of((down_maps.shape[0], 2 * RANK, 128), bf16)],
        query_weight,
        kv_rows,
        jnp.transpose(down_maps, (0, 2, 1)),
        up_maps,
        scratch=[pltpu.SemaphoreType.DMA((2 * NZ + 2,))],
        space=pltpu.HBM,
        mib=PACK_MIB,
    )
    sends = call(
        pack_kernel,
        "pack",
        [of((1280, 128), bf16)] * 4,
        after(query_weight, first),
        kv_rows,
        scratch=[pltpu.SemaphoreType.DMA((8 * NZ,))],
        space=pltpu.HBM,
        mib=PACK_MIB,
    )
    sends = [first, *sends]
    twin = xh_swap(maps)
    cosines, sines = call(rope_kernel, "rope", [of((rows, HEAD_SIZE), f32)] * 2, request_start, scalars=1)
    ring = [(after(hidden, first),) * 2]

    def ring_step(*others):
        r, l = ring[-1]
        if len(ring) > 1:
            r, l = after(r, l, *others), after(l, r, *others)
        ring.append((z_shift(r, 1), z_shift(l, -1) if len(ring) < 4 else None))

    def added(low, sent):
        return call(add_kernel, "low_add", of(low.shape, f32), low, sent)

    ring_step()
    mine = [weight_send(sends[0], 0), weight_send(after(sends[1], *ring[1]), 1)]
    near = jnp.stack([maps, after(twin, *ring[1])])
    ring_step(mine[0], near, sends[1])
    far = core_swap(near)
    mine += [weight_send(after(sends[k], *ring[2]), k) for k in (2, 3)]
    low = call(low_kernel, "low", of((RANK, rows), f32), adapters, hidden, near, far, scalars=1)
    low = added(low, z_xor(low, 1))
    ring_step(mine[1], low)
    ring_step(*mine[2:], cosines)
    mine[3] = after(mine[3], *ring[3])
    other = core_swap(call(stack_kernel, "stack", of((4, 1280, 128), bf16), *mine))
    right, left = zip(*ring)

    shards = [hidden, left[1], left[2], left[3], right[4], right[3], right[2], right[1]]
    weights = (sends[4], *mine, other)
    *kv_parts, gathered = call(
        kv_product_kernel,
        "kv_product",
        [of((576, 128), bf16)] * NY + [of((rows, 1024), bf16)],
        *shards,
        *weights,
        low,
        scratch=[pltpu.VMEM((256, 1024), bf16)],
        mib=8,
    )
    kv_got = [y_shift(kv_parts[dy], dy) for dy in (2, 1, 3)]
    near_a, far_a, *b_parts = call(
        q_product_kernel,
        "q_product",
        [of((NY * TA, 128), bf16)] * 2 + [of((2 * TB, 128), bf16)] * NY,
        gathered,
        *weights,
        scratch=[pltpu.VMEM((NY, 1024, 256), bf16)],
        mib=10,
    )
    b_got = [y_shift(b_parts[dy], dy) for dy in (2, 1, 3)]
    kv_sum, low, x_send = call(
        kv_join_kernel,
        "kv_join",
        [of((512, 128), f32), of((64, 128), f32), of((NY * TA + 512, 128), bf16)],
        kv_parts[0],
        *kv_got,
        far_a,
    )
    x_got = x_swap(x_send)
    low = added(low, z_xor(low, 2))
    low = added(low, z_xor(low, 4))
    low = added(low, x_swap(low))
    a_own, kv_own, *a_sends = call(
        stage_a_kernel,
        "stage_a",
        [of((TA, 128), f32), of((576, 128), bf16)] + [of((TA + 576, 128), bf16)] * (NY - 1),
        near_a,
        x_got,
        kv_sum,
        low,
    )
    a_got = {dy: y_shift(a_sends[dy - 1], dy) for dy in (2, 1, 3)}
    b_own, b_send = call(
        stage_b_kernel, "stage_b", [of((TB, 128), f32), of((TB, 128), bf16)], b_parts[0], *b_got
    )
    b_last = x_swap(b_send)

    return call(
        attention_kernel,
        "attention",
        of((rows, HEAD_SIZE), bf16),
        adapters,
        request_start,
        a_own,
        *[a_got[dy] for dy in (1, 2, 3)],
        b_own,
        b_last,
        kv_own,
        near,
        far,
        cosines,
        sines,
        scalars=2,
        scratch=[pltpu.VMEM((256, rows), bf16)] + [pltpu.VMEM((rows, HEAD_SIZE), bf16)] * 2 + [pltpu.VMEM((8, RANK, 128), bf16)],
        mib=8,
    )


def solution(mesh):
    fine = Mesh(mesh.devices.reshape(NXH, NC, NZ, NX, NY), REQ_AXES + TP_AXES)
    in_specs = (
        P(REQ_AXES, TP_AXES),
        P(None, TP_AXES),
        P(None, TP_AXES),
        P(REQ_AXES, TP_AXES, None),
        P(REQ_AXES, None, TP_AXES),
        P(REQ_AXES),
        P(REQ_AXES),
    )
    return jax.shard_map(
        body, mesh=fine, in_specs=in_specs, out_specs=P(REQ_AXES, TP_AXES), check_vma=False
    )
```

```python
import functools
import math

import jax
import jax.numpy as jnp
from jax import lax
from jax.experimental import pallas as pl
from jax.experimental.pallas import tpu as pltpu
from jax.sharding import Mesh, PartitionSpec as P

HEAD_SIZE = 128
BLOCK = 128
RANK = 32
ROPE_BASE = 500000.0
ADAPTER_SCALE = 2.0
NXH, NC, NZ, NX, NY = 2, 2, 8, 2, 4
REQ_AXES = ("xh", "c")
TP_AXES = ("z", "xl", "y")
NP = NX * NY
TA, TB = 384, 640
PACK_MIB = 56
VMEM = pl.BlockSpec(memory_space=pltpu.VMEM)
SMEM = pl.BlockSpec(memory_space=pltpu.SMEM)


def z_shift(v, s):
    return lax.ppermute(v, "z", [(i, (i + s) % NZ) for i in range(NZ)])


def z_xor(v, s):
    return lax.ppermute(v, "z", [(i, i ^ s) for i in range(NZ)])


def y_xor(v, s):
    return lax.ppermute(v, "y", [(i, i ^ s) for i in range(NY)])


def x_swap(v):
    return lax.ppermute(v, "xl", [(0, 1), (1, 0)])


def core_swap(v):
    return lax.ppermute(v, "c", [(0, 1), (1, 0)])


def xh_swap(v):
    return lax.ppermute(v, "xh", [(0, 1), (1, 0)])


def y_shift(v, s):
    return lax.ppermute(v, "y", [(i, (i + s) % NY) for i in range(NY)])


SERVED = ((1, 4, 6), (3, 5, 7, 2))
FLIP = [dx * NY + (-dy) % NY for dx in range(NX) for dy in range(NY)]


def weight_send(v, k):
    route = []
    for xh in range(NXH):
        for c in range(NC):
            if k >= len(SERVED[c]):
                continue
            dx, dy = divmod(SERVED[c][k], NY)
            for xl in range(NX):
                for y in range(NY):
                    at = xh * NX + xl
                    if dx:
                        to = at ^ 1 if c == 0 else (at + 1 if at % 2 else at - 1) % 4
                    else:
                        to = at
                    src = ((xh * NC + c) * NX + xl) * NY + y
                    dst = ((to // NX * NC + c) * NX + to % NX) * NY + (y + dy) % NY
                    route.append((src, dst))
    return lax.ppermute(v, ("xh", "c", "xl", "y"), route)


def run_copies(pairs, sem):
    copies = [pltpu.make_async_copy(src, dst, sem.at[i]) for i, (src, dst) in enumerate(pairs)]
    for copy in copies:
        copy.start()
    for copy in copies:
        copy.wait()


def weight_pairs(wq_ref, kv_ref, out, d):
    z, xl, y = (lax.axis_index(a) for a in ("z", "xl", "y"))
    p = (xl ^ (d // NY)) * NY + ((y + d) & (NY - 1))
    pairs = []
    for j in range(NZ):
        row = pl.multiple_of((((z + j) & (NZ - 1)) * NP + p) * 128, 128)
        pairs.append((wq_ref.at[pl.ds(row, 128), :], out.at[j * 128 : (j + 1) * 128, :]))
        pairs.append((kv_ref.at[:, pl.ds(row, 128)], out.at[1024 + j * 32 : 1056 + j * 32, :]))
    return pairs


def pack_first_kernel(wq_ref, kv_ref, down_ref, up_ref, out, maps, sem):
    d = jnp.where(lax.axis_index("c") == 0, SERVED[0][0], SERVED[1][0])
    pairs = [(down_ref, maps.at[:, 0:RANK, :]), (up_ref, maps.at[:, RANK : 2 * RANK, :])]
    run_copies(pairs + weight_pairs(wq_ref, kv_ref, out, d), sem)


def pack_kernel(wq_ref, kv_ref, *refs):
    outs, sem = refs[:4], refs[4]
    c = lax.axis_index("c")
    pairs = []
    for k, out in enumerate(outs, 1):
        d = jnp.where(c == 0, (SERVED[0] + (0,))[k], SERVED[1][k]) if k < 4 else 0
        pairs += weight_pairs(wq_ref, kv_ref, out, d)
    run_copies(pairs, sem)


def stack_kernel(*refs):
    for i, ref in enumerate(refs[:-1]):
        refs[-1][i] = ref[...]


def add_kernel(a_ref, b_ref, out_ref):
    out_ref[...] = a_ref[...] + b_ref[...].astype(jnp.float32)


def rope_kernel(start_ref, cos_ref, sin_ref):
    half = HEAD_SIZE // 2
    lane = lax.broadcasted_iota(jnp.int32, (BLOCK, HEAD_SIZE), 1)
    row = lax.broadcasted_iota(jnp.int32, (BLOCK, HEAD_SIZE), 0)
    steps = (lane & (half - 1)).astype(jnp.float32)
    inverse = jnp.exp(-(2.0 * steps / HEAD_SIZE) * math.log(ROPE_BASE))
    sign = jnp.where(lane < half, -1.0, 1.0).astype(jnp.float32)
    place = row.astype(jnp.float32) * inverse
    cos_in, sin_in = jnp.cos(place), jnp.sin(place)
    blocks = cos_ref.shape[0] // BLOCK
    ahead = lax.broadcasted_iota(jnp.int32, (8, HEAD_SIZE), 0).astype(jnp.float32) * BLOCK * inverse[0:8, :]
    cos_out, sin_out = jnp.cos(ahead), jnp.sin(ahead)
    first = (lax.axis_index("xh") * NC + lax.axis_index("c")) * blocks
    which = lax.broadcasted_iota(jnp.int32, (8, HEAD_SIZE), 0)
    for b in range(blocks):
        chosen = which == first + b - start_ref[b * BLOCK]
        co = jnp.sum(jnp.where(chosen, cos_out, 0.0), axis=0, keepdims=True)
        so = jnp.sum(jnp.where(chosen, sin_out, 0.0), axis=0, keepdims=True)
        rows = slice(b * BLOCK, (b + 1) * BLOCK)
        cos_ref[rows, :] = cos_in * co - sin_in * so
        sin_ref[rows, :] = (sin_in * co + cos_in * so) * sign


def low_kernel(ad_ref, h_ref, near_ref, far_ref, out_ref, narrow_ref):
    c, xh = lax.axis_index("c"), lax.axis_index("xh")
    per = near_ref.shape[1]
    for b in range(h_ref.shape[0] // BLOCK):
        a = ad_ref[b]
        owner = a // per
        at = a - owner * per
        xr, cr = (owner // NC) ^ xh, (owner % NC) ^ c
        down = jnp.where(cr == 0, near_ref[xr, at, 0:RANK, :], far_ref[xr, at, 0:RANK, :])
        out_ref[:, b * BLOCK : (b + 1) * BLOCK] = lax.dot_general(
            down,
            h_ref[b * BLOCK : (b + 1) * BLOCK, :],
            (((1,), (1,)), ((), ())),
            preferred_element_type=jnp.float32,
        )
    narrow_ref[...] = out_ref[...].astype(jnp.bfloat16)


def for_each_piece(own, mine, other, place):
    place(own, 0)
    c = lax.axis_index("c")
    for core in range(NC):

        @pl.when(c == core)
        def _():
            for k, d in enumerate(SERVED[core]):
                place(mine[k], FLIP[d])
            for k, d in enumerate(SERVED[1 - core]):
                place(other[k], FLIP[d])


def kv_product_kernel(*refs):
    h_refs, own, mine, other, low_ref = refs[0:8], refs[8], refs[9:13], refs[13], refs[14]
    outs, hbuf, kvw = refs[15:19], refs[19], refs[20]
    other = [other.at[k] for k in range(4)]
    y = lax.axis_index("y")
    for j in range(8):
        hbuf[:, j * 128 : (j + 1) * 128] = h_refs[j][...]
    for dy in range(NY):
        for t in range(2):
            at = pl.multiple_of((((y + dy) & (NY - 1)) * 2 + t) * 128, 128)
            outs[dy][512 + t * 32 : 544 + t * 32, :] = low_ref[:, pl.ds(at, 128)].astype(jnp.bfloat16)

    def place(ref, d):
        for j in range(NZ):
            kvw[d * 32 : (d + 1) * 32, j * 128 : (j + 1) * 128] = ref[1024 + j * 32 : 1056 + j * 32, :]

    for_each_piece(own, mine, other, place)
    kv = lax.dot_general(
        kvw[...], hbuf[...], (((1,), (1,)), ((), ())), preferred_element_type=jnp.float32
    ).astype(jnp.bfloat16)
    for d in range(NP):
        dx, dy = divmod(d, NY)
        for t in range(8):
            at = t * 64 + dx * 32
            outs[dy][at : at + 32, :] = kv[d * 32 : (d + 1) * 32, t * 128 : (t + 1) * 128]


def q_product_kernel(hbuf, own, *refs):
    mine, other = refs[0:4], [refs[4].at[k] for k in range(4)]
    near_ref, far_ref, outs, wq = refs[5], refs[6], refs[7:11], refs[11]

    def place(ref, d):
        dx, dy = divmod(d, NY)
        wq[dy, :, dx * 128 : (dx + 1) * 128] = ref[0:1024, :]

    for_each_piece(own, mine, other, place)
    for dy in range(NY):
        q = jnp.dot(hbuf[0:TA, :], wq[dy], preferred_element_type=jnp.float32).astype(jnp.bfloat16)
        near_ref[dy * TA : (dy + 1) * TA, :] = q[:, 0:128]
        far_ref[dy * TA : (dy + 1) * TA, :] = q[:, 128:256]
    for dy in range(NY):
        q = jnp.dot(hbuf[TA:1024, :], wq[dy], preferred_element_type=jnp.float32).astype(jnp.bfloat16)
        outs[dy][0:TB, :] = q[:, 0:128]
        outs[dy][TB : 2 * TB, :] = q[:, 128:256]


def wide(ref, rows):
    return ref[rows, :].astype(jnp.float32)


def kv_join_kernel(k0, k1, k2, k3, far_ref, sum_ref, low_ref, send_ref):
    total = wide(k0, ...) + wide(k1, ...) + wide(k2, ...) + wide(k3, ...)
    sum_ref[...] = total[0:512, :]
    low_ref[...] = total[512:576, :]
    send_ref[0 : NY * TA, :] = far_ref[...]
    send_ref[NY * TA :, :] = total[0:512, :].astype(jnp.bfloat16)


def stage_a_kernel(near_ref, got_ref, kv_ref, low_ref, own_ref, kv_out, *sends):
    for t in range(8):
        for dx in range(NX):
            a, b = t * 64 + dx * 32, NY * TA + t * 64 + (1 - dx) * 32
            kv_out[a : a + 32, :] = (kv_ref[a : a + 32, :] + wide(got_ref, slice(b, b + 32))).astype(jnp.bfloat16)
    kv_out[512:576, :] = low_ref[...].astype(jnp.bfloat16)
    for dy in range(NY):
        rows = slice(dy * TA, (dy + 1) * TA)
        total = wide(near_ref, rows) + wide(got_ref, rows)
        if dy == 0:
            own_ref[...] = total
        else:
            sends[dy - 1][0:TA, :] = total.astype(jnp.bfloat16)
            sends[dy - 1][TA:, :] = kv_out[...]


def stage_b_kernel(b0, b1, b2, b3, own_ref, send_ref):
    for dx, out in enumerate((own_ref, send_ref)):
        rows = slice(dx * TB, (dx + 1) * TB)
        out[...] = (wide(b0, rows) + wide(b1, rows) + wide(b2, rows) + wide(b3, rows)).astype(out.dtype)


def attention_kernel(ad_ref, start_ref, *refs):
    a_own, a_got, b_own, b_got, kv_own = refs[0], refs[1:4], refs[4], refs[5], refs[6]
    near_ref, far_ref, cos_ref, sin_ref = refs[7:11]
    out_ref = refs[11]
    kvt, k_buf, v_buf, low_buf = refs[12:16]
    xl, y, c, xh = (lax.axis_index(a) for a in ("xl", "y", "c", "xh"))
    first = (xh * NC + c) * 8
    for i in range(NY):
        ref, base = (kv_own, 0) if i == 0 else (a_got[i - 1], TA)
        for t in range(2):
            low_buf[((y - i) & (NY - 1)) * 2 + t] = ref[base + 512 + t * 32 : base + 544 + t * 32, :]
        for dx in range(NX):
            p = (xl ^ dx) * NY + ((y - i) & (NY - 1))
            at = pl.multiple_of(p * 32, 32)
            for t in range(8):
                kvt[pl.ds(at, 32), t * 128 : (t + 1) * 128] = ref[base + t * 64 + dx * 32 : base + t * 64 + dx * 32 + 32, :]

    def rope(v, rows):
        return v * cos_ref[rows, :] + pltpu.roll(v, 64, 1) * sin_ref[rows, :]

    for t in range(8):
        rows = slice(t * 128, (t + 1) * 128)
        k = kvt[0:128, rows].astype(jnp.float32).T
        k_buf[rows, :] = rope(k, rows).astype(jnp.bfloat16)
        v_buf[rows, :] = kvt[128:256, rows].T
    per = near_ref.shape[1]
    factor = math.log2(math.e) / math.sqrt(HEAD_SIZE)
    for b in range(8):
        rows = slice(b * 128, (b + 1) * 128)
        a = ad_ref[b]
        owner = a // per
        at = a - owner * per
        xr, cr = (owner // NC) ^ xh, (owner % NC) ^ c
        up = jnp.where(cr == 0, near_ref[xr, at, RANK : 2 * RANK, :], far_ref[xr, at, RANK : 2 * RANK, :])
        q = ADAPTER_SCALE * lax.dot_general(
            low_buf[b], up, (((0,), (0,)), ((), ())), preferred_element_type=jnp.float32
        )
        if b * 128 < TA:
            q += a_own[rows, :]
            for ref in a_got:
                q += wide(ref, rows)
        else:
            part = slice(b * 128 - TA, (b + 1) * 128 - TA)
            q += b_own[part, :] + wide(b_got, part)
        q = rope(q, rows).astype(jnp.bfloat16)
        n = (b + 1) * 128
        s = lax.dot_general(
            q, k_buf[0:n, :], (((1,), (1,)), ((), ())), preferred_element_type=jnp.float32
        )
        col = lax.broadcasted_iota(jnp.int32, (128, n), 1)
        row = lax.broadcasted_iota(jnp.int32, (128, n), 0) + b * 128
        allowed = (col >= (start_ref[b * BLOCK] - first) * BLOCK) & (col <= row)
        s = jnp.where(allowed, s, -1e30)
        e = jnp.exp2((s - jnp.max(s, axis=1, keepdims=True)) * factor)
        mixed = jnp.dot(e.astype(jnp.bfloat16), v_buf[0:n, :], preferred_element_type=jnp.float32)
        out_ref[rows, :] = (mixed * (1.0 / jnp.sum(e, axis=1, keepdims=True))).astype(jnp.bfloat16)


def call(kernel, name, outs, *args, scalars=0, scratch=(), mib=4, space=pltpu.VMEM):
    single = isinstance(outs, jax.ShapeDtypeStruct)
    return pl.pallas_call(
        kernel,
        out_shape=outs,
        in_specs=[SMEM] * scalars + [pl.BlockSpec(memory_space=space)] * (len(args) - scalars),
        out_specs=VMEM if single else [VMEM] * len(outs),
        scratch_shapes=scratch,
        compiler_params=pltpu.CompilerParams(vmem_limit_bytes=mib << 20),
        name=name,
    )(*args)


def after(value, *others):
    return lax.optimization_barrier((value, *others))[0]


def body(hidden, query_weight, key_value_weight, down_maps, up_maps, request_start, adapters):
    rows = hidden.shape[0]
    bf16, f32 = jnp.bfloat16, jnp.float32
    of = jax.ShapeDtypeStruct
    kv_rows = key_value_weight.T
    first, maps = call(
        pack_first_kernel,
        "pack_first",
        [of((1280, 128), bf16), of((down_maps.shape[0], 2 * RANK, 128), bf16)],
        query_weight,
        kv_rows,
        jnp.transpose(down_maps, (0, 2, 1)),
        up_maps,
        scratch=[pltpu.SemaphoreType.DMA((2 * NZ + 2,))],
        space=pltpu.HBM,
        mib=PACK_MIB,
    )
    cosines, sines = call(rope_kernel, "rope", [of((rows, HEAD_SIZE), f32)] * 2, request_start, scalars=1)
    sends = call(
        pack_kernel,
        "pack",
        [of((1280, 128), bf16)] * 4,
        after(query_weight, first, cosines),
        kv_rows,
        scratch=[pltpu.SemaphoreType.DMA((8 * NZ,))],
        space=pltpu.HBM,
        mib=PACK_MIB,
    )
    sends = [first, *sends]
    twin = xh_swap(maps)
    ring = [(hidden, hidden)]

    def ring_step(*others):
        r, l = ring[-1]
        if len(ring) > 1:
            r, l = after(r, l, *others), after(l, r, *others)
        ring.append((z_shift(r, 1), z_shift(l, -1) if len(ring) < 4 else None))

    def added(low, sent):
        return call(add_kernel, "low_add", of(low.shape, f32), low, sent)

    ring_step()
    mine = [weight_send(sends[0], 0), weight_send(after(sends[1], *ring[1]), 1), None, weight_send(sends[3], 3)]
    near = jnp.stack([maps, after(twin, *ring[1])])
    ring_step(mine[0], mine[3], near)
    far = core_swap(near)
    mine[2] = weight_send(after(sends[2], *ring[2]), 2)
    low, narrow = call(
        low_kernel, "low", [of((RANK, rows), f32), of((RANK, rows), bf16)], adapters, hidden, near, far, scalars=1
    )
    low = added(low, z_xor(narrow, 4))
    ring_step(mine[1], low)
    ring_step(mine[2])
    mine[3] = after(mine[3], *ring[3])
    other = core_swap(call(stack_kernel, "stack", of((4, 1280, 128), bf16), *mine))
    right, left = zip(*ring)

    shards = [hidden, left[1], left[2], left[3], right[4], right[3], right[2], right[1]]
    weights = (sends[4], *mine, other)
    *kv_parts, gathered = call(
        kv_product_kernel,
        "kv_product",
        [of((576, 128), bf16)] * NY + [of((rows, 1024), bf16)],
        *shards,
        *weights,
        low,
        scratch=[pltpu.VMEM((256, 1024), bf16)],
        mib=8,
    )
    kv_got = [y_shift(kv_parts[dy], dy) for dy in (2, 1, 3)]
    near_a, far_a, *b_parts = call(
        q_product_kernel,
        "q_product",
        [of((NY * TA, 128), bf16)] * 2 + [of((2 * TB, 128), bf16)] * NY,
        gathered,
        *weights,
        scratch=[pltpu.VMEM((NY, 1024, 256), bf16)],
        mib=10,
    )
    b_got = [y_shift(b_parts[dy], dy) for dy in (2, 1, 3)]
    kv_sum, low, x_send = call(
        kv_join_kernel,
        "kv_join",
        [of((512, 128), f32), of((64, 128), f32), of((NY * TA + 512, 128), bf16)],
        kv_parts[0],
        *kv_got,
        far_a,
    )
    x_got = x_swap(x_send)
    low = added(low, z_xor(low, 1))
    low = added(low, z_xor(low, 2))
    low = added(low, x_swap(low))
    a_own, kv_own, *a_sends = call(
        stage_a_kernel,
        "stage_a",
        [of((TA, 128), f32), of((576, 128), bf16)] + [of((TA + 576, 128), bf16)] * (NY - 1),
        near_a,
        x_got,
        kv_sum,
        low,
    )
    a_got = {dy: y_shift(a_sends[dy - 1], dy) for dy in (2, 1, 3)}
    b_own, b_send = call(
        stage_b_kernel, "stage_b", [of((TB, 128), f32), of((TB, 128), bf16)], b_parts[0], *b_got
    )
    b_last = x_swap(b_send)

    return call(
        attention_kernel,
        "attention",
        of((rows, HEAD_SIZE), bf16),
        adapters,
        request_start,
        a_own,
        *[a_got[dy] for dy in (1, 2, 3)],
        b_own,
        b_last,
        kv_own,
        near,
        far,
        cosines,
        sines,
        scalars=2,
        scratch=[pltpu.VMEM((256, rows), bf16)] + [pltpu.VMEM((rows, HEAD_SIZE), bf16)] * 2 + [pltpu.VMEM((8, RANK, 128), bf16)],
        mib=8,
    )


def solution(mesh):
    fine = Mesh(mesh.devices.reshape(NXH, NC, NZ, NX, NY), REQ_AXES + TP_AXES)
    in_specs = (
        P(REQ_AXES, TP_AXES),
        P(None, TP_AXES),
        P(None, TP_AXES),
        P(REQ_AXES, TP_AXES, None),
        P(REQ_AXES, None, TP_AXES),
        P(REQ_AXES),
        P(REQ_AXES),
    )
    return jax.shard_map(
        body, mesh=fine, in_specs=in_specs, out_specs=P(REQ_AXES, TP_AXES), check_vma=False
    )
```

```python
import functools
import math

import jax
import jax.numpy as jnp
from jax import lax
from jax.experimental import pallas as pl
from jax.experimental.pallas import tpu as pltpu
from jax.sharding import Mesh, PartitionSpec as P

HEAD_SIZE = 128
BLOCK = 128
RANK = 32
ROPE_BASE = 500000.0
ADAPTER_SCALE = 2.0
NXH, NC, NZ, NX, NY = 2, 2, 8, 2, 4
REQ_AXES = ("xh", "c")
TP_AXES = ("z", "xl", "y")
NP = NX * NY
TA, TB = 384, 640
PACK_MIB = 56
VMEM = pl.BlockSpec(memory_space=pltpu.VMEM)
SMEM = pl.BlockSpec(memory_space=pltpu.SMEM)


def z_shift(v, s):
    return lax.ppermute(v, "z", [(i, (i + s) % NZ) for i in range(NZ)])


def z_xor(v, s):
    return lax.ppermute(v, "z", [(i, i ^ s) for i in range(NZ)])


def y_xor(v, s):
    return lax.ppermute(v, "y", [(i, i ^ s) for i in range(NY)])


def x_swap(v):
    return lax.ppermute(v, "xl", [(0, 1), (1, 0)])


def core_swap(v):
    return lax.ppermute(v, "c", [(0, 1), (1, 0)])


def xh_swap(v):
    return lax.ppermute(v, "xh", [(0, 1), (1, 0)])


def y_shift(v, s):
    return lax.ppermute(v, "y", [(i, (i + s) % NY) for i in range(NY)])


SERVED = ((1, 4, 6), (3, 5, 7, 2))
FLIP = [dx * NY + (-dy) % NY for dx in range(NX) for dy in range(NY)]


def weight_send(v, k):
    route = []
    for xh in range(NXH):
        for c in range(NC):
            if k >= len(SERVED[c]):
                continue
            dx, dy = divmod(SERVED[c][k], NY)
            for xl in range(NX):
                for y in range(NY):
                    at = xh * NX + xl
                    if dx:
                        to = at ^ 1 if c == 0 else (at + 1 if at % 2 else at - 1) % 4
                    else:
                        to = at
                    src = ((xh * NC + c) * NX + xl) * NY + y
                    dst = ((to // NX * NC + c) * NX + to % NX) * NY + (y + dy) % NY
                    route.append((src, dst))
    return lax.ppermute(v, ("xh", "c", "xl", "y"), route)


def run_copies(pairs, sem):
    copies = [pltpu.make_async_copy(src, dst, sem.at[i]) for i, (src, dst) in enumerate(pairs)]
    for copy in copies:
        copy.start()
    for copy in copies:
        copy.wait()


def weight_pairs(wq_ref, kv_ref, out, d):
    z, xl, y = (lax.axis_index(a) for a in ("z", "xl", "y"))
    p = (xl ^ (d // NY)) * NY + ((y + d) & (NY - 1))
    pairs = []
    for j in range(NZ):
        row = pl.multiple_of((((z + j) & (NZ - 1)) * NP + p) * 128, 128)
        pairs.append((wq_ref.at[pl.ds(row, 128), :], out.at[j * 128 : (j + 1) * 128, :]))
        pairs.append((kv_ref.at[:, pl.ds(row, 128)], out.at[1024 + j * 32 : 1056 + j * 32, :]))
    return pairs


def pack_first_kernel(wq_ref, kv_ref, down_ref, up_ref, out, maps, sem):
    d = jnp.where(lax.axis_index("c") == 0, SERVED[0][0], SERVED[1][0])
    pairs = [(down_ref, maps.at[:, 0:RANK, :]), (up_ref, maps.at[:, RANK : 2 * RANK, :])]
    run_copies(pairs + weight_pairs(wq_ref, kv_ref, out, d), sem)


def pack_kernel(wq_ref, kv_ref, *refs):
    outs, sem = refs[:4], refs[4]
    c = lax.axis_index("c")
    pairs = []
    for k, out in enumerate(outs, 1):
        d = jnp.where(c == 0, (SERVED[0] + (0,))[k], SERVED[1][k]) if k < 4 else 0
        pairs += weight_pairs(wq_ref, kv_ref, out, d)
    run_copies(pairs, sem)


def stack_kernel(*refs):
    for i, ref in enumerate(refs[:-1]):
        refs[-1][i] = ref[...]


def split_kernel(a_ref, b_ref, low_half, high_half):
    half = low_half.shape[0]
    low_half[...] = a_ref[0:half, :]
    high_half[...] = b_ref[half:, :]


def add_kernel(a_ref, b_ref, out_ref):
    out_ref[...] = a_ref[...] + b_ref[...].astype(jnp.float32)


def rope_kernel(start_ref, cos_ref, sin_ref):
    half = HEAD_SIZE // 2
    lane = lax.broadcasted_iota(jnp.int32, (BLOCK, HEAD_SIZE), 1)
    row = lax.broadcasted_iota(jnp.int32, (BLOCK, HEAD_SIZE), 0)
    steps = (lane & (half - 1)).astype(jnp.float32)
    inverse = jnp.exp(-(2.0 * steps / HEAD_SIZE) * math.log(ROPE_BASE))
    sign = jnp.where(lane < half, -1.0, 1.0).astype(jnp.float32)
    place = row.astype(jnp.float32) * inverse
    cos_in, sin_in = jnp.cos(place), jnp.sin(place)
    blocks = cos_ref.shape[0] // BLOCK
    ahead = lax.broadcasted_iota(jnp.int32, (8, HEAD_SIZE), 0).astype(jnp.float32) * BLOCK * inverse[0:8, :]
    cos_out, sin_out = jnp.cos(ahead), jnp.sin(ahead)
    first = (lax.axis_index("xh") * NC + lax.axis_index("c")) * blocks
    which = lax.broadcasted_iota(jnp.int32, (8, HEAD_SIZE), 0)
    for b in range(blocks):
        chosen = which == first + b - start_ref[b * BLOCK]
        co = jnp.sum(jnp.where(chosen, cos_out, 0.0), axis=0, keepdims=True)
        so = jnp.sum(jnp.where(chosen, sin_out, 0.0), axis=0, keepdims=True)
        rows = slice(b * BLOCK, (b + 1) * BLOCK)
        cos_ref[rows, :] = cos_in * co - sin_in * so
        sin_ref[rows, :] = (sin_in * co + cos_in * so) * sign


def low_kernel(ad_ref, h_ref, near_ref, far_ref, out_ref, narrow_ref):
    c, xh = lax.axis_index("c"), lax.axis_index("xh")
    per = near_ref.shape[1]
    for b in range(h_ref.shape[0] // BLOCK):
        a = ad_ref[b]
        owner = a // per
        at = a - owner * per
        xr, cr = (owner // NC) ^ xh, (owner % NC) ^ c
        down = jnp.where(cr == 0, near_ref[xr, at, 0:RANK, :], far_ref[xr, at, 0:RANK, :])
        out_ref[:, b * BLOCK : (b + 1) * BLOCK] = lax.dot_general(
            down,
            h_ref[b * BLOCK : (b + 1) * BLOCK, :],
            (((1,), (1,)), ((), ())),
            preferred_element_type=jnp.float32,
        )
    narrow_ref[...] = out_ref[...].astype(jnp.bfloat16)


def for_each_piece(own, mine, other, place):
    place(own, 0)
    c = lax.axis_index("c")
    for core in range(NC):

        @pl.when(c == core)
        def _():
            for k, d in enumerate(SERVED[core]):
                place(mine[k], FLIP[d])
            for k, d in enumerate(SERVED[1 - core]):
                place(other[k], FLIP[d])


def kv_product_kernel(*refs):
    h_refs, own, mine, other, low_ref = refs[0:9], refs[9], refs[10:14], refs[14], refs[15]
    outs, hbuf, kvw = refs[16:20], refs[20], refs[21]
    other = [other.at[k] for k in range(4)]
    y = lax.axis_index("y")
    for j in range(4):
        hbuf[:, j * 128 : (j + 1) * 128] = h_refs[j][...]
        if j:
            hbuf[:, (4 + j) * 128 : (5 + j) * 128] = h_refs[5 + j][...]
    hbuf[0:512, 512:640] = h_refs[4][...]
    hbuf[512:1024, 512:640] = h_refs[5][...]
    for dy in range(NY):
        for t in range(2):
            at = pl.multiple_of((((y + dy) & (NY - 1)) * 2 + t) * 128, 128)
            outs[dy][512 + t * 32 : 544 + t * 32, :] = low_ref[:, pl.ds(at, 128)].astype(jnp.bfloat16)

    def place(ref, d):
        for j in range(NZ):
            kvw[d * 32 : (d + 1) * 32, j * 128 : (j + 1) * 128] = ref[1024 + j * 32 : 1056 + j * 32, :]

    for_each_piece(own, mine, other, place)
    kv = lax.dot_general(
        kvw[...], hbuf[...], (((1,), (1,)), ((), ())), preferred_element_type=jnp.float32
    ).astype(jnp.bfloat16)
    for d in range(NP):
        dx, dy = divmod(d, NY)
        for t in range(8):
            at = t * 64 + dx * 32
            outs[dy][at : at + 32, :] = kv[d * 32 : (d + 1) * 32, t * 128 : (t + 1) * 128]


def q_product_kernel(hbuf, own, *refs):
    mine, other = refs[0:4], [refs[4].at[k] for k in range(4)]
    near_ref, far_ref, outs, wq = refs[5], refs[6], refs[7:11], refs[11]

    def place(ref, d):
        dx, dy = divmod(d, NY)
        wq[dy, :, dx * 128 : (dx + 1) * 128] = ref[0:1024, :]

    for_each_piece(own, mine, other, place)
    for dy in range(NY):
        q = jnp.dot(hbuf[0:TA, :], wq[dy], preferred_element_type=jnp.float32).astype(jnp.bfloat16)
        near_ref[dy * TA : (dy + 1) * TA, :] = q[:, 0:128]
        far_ref[dy * TA : (dy + 1) * TA, :] = q[:, 128:256]
    for dy in range(NY):
        q = jnp.dot(hbuf[TA:1024, :], wq[dy], preferred_element_type=jnp.float32).astype(jnp.bfloat16)
        outs[dy][0:TB, :] = q[:, 0:128]
        outs[dy][TB : 2 * TB, :] = q[:, 128:256]


def wide(ref, rows):
    return ref[rows, :].astype(jnp.float32)


def kv_join_kernel(k0, k1, k2, k3, far_ref, sum_ref, low_ref, send_ref):
    total = wide(k0, ...) + wide(k1, ...) + wide(k2, ...) + wide(k3, ...)
    sum_ref[...] = total[0:512, :]
    low_ref[...] = total[512:576, :]
    send_ref[0 : NY * TA, :] = far_ref[...]
    send_ref[NY * TA :, :] = total[0:512, :].astype(jnp.bfloat16)


def stage_a_kernel(near_ref, got_ref, kv_ref, low_ref, own_ref, kv_out, *sends):
    for t in range(8):
        for dx in range(NX):
            a, b = t * 64 + dx * 32, NY * TA + t * 64 + (1 - dx) * 32
            kv_out[a : a + 32, :] = (kv_ref[a : a + 32, :] + wide(got_ref, slice(b, b + 32))).astype(jnp.bfloat16)
    kv_out[512:576, :] = low_ref[...].astype(jnp.bfloat16)
    for dy in range(NY):
        rows = slice(dy * TA, (dy + 1) * TA)
        total = wide(near_ref, rows) + wide(got_ref, rows)
        if dy == 0:
            own_ref[...] = total
        else:
            sends[dy - 1][0:TA, :] = total.astype(jnp.bfloat16)
            sends[dy - 1][TA:, :] = kv_out[...]


def stage_b_kernel(b0, b1, b2, b3, own_ref, send_ref):
    for dx, out in enumerate((own_ref, send_ref)):
        rows = slice(dx * TB, (dx + 1) * TB)
        out[...] = (wide(b0, rows) + wide(b1, rows) + wide(b2, rows) + wide(b3, rows)).astype(out.dtype)


def attention_kernel(ad_ref, start_ref, *refs):
    a_own, a_got, b_own, b_got, kv_own = refs[0], refs[1:4], refs[4], refs[5], refs[6]
    near_ref, far_ref, cos_ref, sin_ref = refs[7:11]
    out_ref = refs[11]
    kvt, k_buf, v_buf, low_buf = refs[12:16]
    xl, y, c, xh = (lax.axis_index(a) for a in ("xl", "y", "c", "xh"))
    first = (xh * NC + c) * 8
    for i in range(NY):
        ref, base = (kv_own, 0) if i == 0 else (a_got[i - 1], TA)
        for t in range(2):
            low_buf[((y - i) & (NY - 1)) * 2 + t] = ref[base + 512 + t * 32 : base + 544 + t * 32, :]
        for dx in range(NX):
            p = (xl ^ dx) * NY + ((y - i) & (NY - 1))
            at = pl.multiple_of(p * 32, 32)
            for t in range(8):
                kvt[pl.ds(at, 32), t * 128 : (t + 1) * 128] = ref[base + t * 64 + dx * 32 : base + t * 64 + dx * 32 + 32, :]

    def rope(v, rows):
        return v * cos_ref[rows, :] + pltpu.roll(v, 64, 1) * sin_ref[rows, :]

    for t in range(8):
        rows = slice(t * 128, (t + 1) * 128)
        k = kvt[0:128, rows].astype(jnp.float32).T
        k_buf[rows, :] = rope(k, rows).astype(jnp.bfloat16)
        v_buf[rows, :] = kvt[128:256, rows].T
    per = near_ref.shape[1]
    factor = math.log2(math.e) / math.sqrt(HEAD_SIZE)
    for b in range(8):
        rows = slice(b * 128, (b + 1) * 128)
        a = ad_ref[b]
        owner = a // per
        at = a - owner * per
        xr, cr = (owner // NC) ^ xh, (owner % NC) ^ c
        up = jnp.where(cr == 0, near_ref[xr, at, RANK : 2 * RANK, :], far_ref[xr, at, RANK : 2 * RANK, :])
        q = ADAPTER_SCALE * lax.dot_general(
            low_buf[b], up, (((0,), (0,)), ((), ())), preferred_element_type=jnp.float32
        )
        if b * 128 < TA:
            q += a_own[rows, :]
            for ref in a_got:
                q += wide(ref, rows)
        else:
            part = slice(b * 128 - TA, (b + 1) * 128 - TA)
            q += b_own[part, :] + wide(b_got, part)
        q = rope(q, rows).astype(jnp.bfloat16)
        n = (b + 1) * 128
        s = lax.dot_general(
            q, k_buf[0:n, :], (((1,), (1,)), ((), ())), preferred_element_type=jnp.float32
        )
        col = lax.broadcasted_iota(jnp.int32, (128, n), 1)
        row = lax.broadcasted_iota(jnp.int32, (128, n), 0) + b * 128
        allowed = (col >= (start_ref[b * BLOCK] - first) * BLOCK) & (col <= row)
        s = jnp.where(allowed, s, -1e30)
        e = jnp.exp2((s - jnp.max(s, axis=1, keepdims=True)) * factor)
        mixed = jnp.dot(e.astype(jnp.bfloat16), v_buf[0:n, :], preferred_element_type=jnp.float32)
        out_ref[rows, :] = (mixed * (1.0 / jnp.sum(e, axis=1, keepdims=True))).astype(jnp.bfloat16)


def call(kernel, name, outs, *args, scalars=0, scratch=(), mib=4, space=pltpu.VMEM):
    single = isinstance(outs, jax.ShapeDtypeStruct)
    return pl.pallas_call(
        kernel,
        out_shape=outs,
        in_specs=[SMEM] * scalars + [pl.BlockSpec(memory_space=space)] * (len(args) - scalars),
        out_specs=VMEM if single else [VMEM] * len(outs),
        scratch_shapes=scratch,
        compiler_params=pltpu.CompilerParams(vmem_limit_bytes=mib << 20),
        name=name,
    )(*args)


def after(value, *others):
    return lax.optimization_barrier((value, *others))[0]


def body(hidden, query_weight, key_value_weight, down_maps, up_maps, request_start, adapters):
    rows = hidden.shape[0]
    bf16, f32 = jnp.bfloat16, jnp.float32
    of = jax.ShapeDtypeStruct
    kv_rows = key_value_weight.T
    first, maps = call(
        pack_first_kernel,
        "pack_first",
        [of((1280, 128), bf16), of((down_maps.shape[0], 2 * RANK, 128), bf16)],
        query_weight,
        kv_rows,
        jnp.transpose(down_maps, (0, 2, 1)),
        up_maps,
        scratch=[pltpu.SemaphoreType.DMA((2 * NZ + 2,))],
        space=pltpu.HBM,
        mib=PACK_MIB,
    )
    cosines, sines = call(rope_kernel, "rope", [of((rows, HEAD_SIZE), f32)] * 2, request_start, scalars=1)
    sends = call(
        pack_kernel,
        "pack",
        [of((1280, 128), bf16)] * 4,
        after(query_weight, first, cosines),
        kv_rows,
        scratch=[pltpu.SemaphoreType.DMA((8 * NZ,))],
        space=pltpu.HBM,
        mib=PACK_MIB,
    )
    sends = [first, *sends]
    twin = xh_swap(maps)
    ring = [(hidden, hidden)]

    def ring_step(*others):
        r, l = ring[-1]
        if len(ring) > 1:
            r, l = after(r, l, *others), after(l, r, *others)
        ring.append((z_shift(r, 1), z_shift(l, -1)))

    def added(low, sent):
        return call(add_kernel, "low_add", of(low.shape, f32), low, sent)

    ring_step()
    mine = [weight_send(sends[0], 0)]
    mine += [weight_send(after(sends[k], *ring[1]), k) for k in (1, 2)] + [weight_send(sends[3], 3)]
    near = jnp.stack([maps, after(twin, *ring[1])])
    far = core_swap(near)
    low, narrow = call(
        low_kernel, "low", [of((RANK, rows), f32), of((RANK, rows), bf16)], adapters, hidden, near, far, scalars=1
    )
    ring_step(sends[1], narrow)
    low = added(low, z_xor(narrow, 4))
    mine[3] = after(mine[3], *ring[2])
    stacked = call(stack_kernel, "stack", of((4, 1280, 128), bf16), *mine)
    ring_step(stacked)
    other = core_swap(stacked)
    halves = call(split_kernel, "split", [of((rows // 2, 128), bf16)] * 2, after(ring[2][0], stacked), ring[2][1])
    across = [z_shift(halves[0], 2), z_shift(halves[1], -2)]
    right, left = zip(*ring)

    shards = [hidden, left[1], left[2], left[3], *across, right[3], right[2], right[1]]
    weights = (sends[4], *mine, other)
    *kv_parts, gathered = call(
        kv_product_kernel,
        "kv_product",
        [of((576, 128), bf16)] * NY + [of((rows, 1024), bf16)],
        *shards,
        *weights,
        low,
        scratch=[pltpu.VMEM((256, 1024), bf16)],
        mib=8,
    )
    kv_got = [y_shift(kv_parts[dy], dy) for dy in (2, 1, 3)]
    near_a, far_a, *b_parts = call(
        q_product_kernel,
        "q_product",
        [of((NY * TA, 128), bf16)] * 2 + [of((2 * TB, 128), bf16)] * NY,
        gathered,
        *weights,
        scratch=[pltpu.VMEM((NY, 1024, 256), bf16)],
        mib=10,
    )
    b_got = [y_shift(b_parts[dy], dy) for dy in (2, 1, 3)]
    kv_sum, low, x_send = call(
        kv_join_kernel,
        "kv_join",
        [of((512, 128), f32), of((64, 128), f32), of((NY * TA + 512, 128), bf16)],
        kv_parts[0],
        *kv_got,
        far_a,
    )
    x_got = x_swap(x_send)
    low = added(low, z_xor(low, 1))
    low = added(low, z_xor(low, 2))
    low = added(low, x_swap(low))
    a_own, kv_own, *a_sends = call(
        stage_a_kernel,
        "stage_a",
        [of((TA, 128), f32), of((576, 128), bf16)] + [of((TA + 576, 128), bf16)] * (NY - 1),
        near_a,
        x_got,
        kv_sum,
        low,
    )
    a_got = {dy: y_shift(a_sends[dy - 1], dy) for dy in (2, 1, 3)}
    b_own, b_send = call(
        stage_b_kernel, "stage_b", [of((TB, 128), f32), of((TB, 128), bf16)], b_parts[0], *b_got
    )
    b_last = x_swap(b_send)

    return call(
        attention_kernel,
        "attention",
        of((rows, HEAD_SIZE), bf16),
        adapters,
        request_start,
        a_own,
        *[a_got[dy] for dy in (1, 2, 3)],
        b_own,
        b_last,
        kv_own,
        near,
        far,
        cosines,
        sines,
        scalars=2,
        scratch=[pltpu.VMEM((256, rows), bf16)] + [pltpu.VMEM((rows, HEAD_SIZE), bf16)] * 2 + [pltpu.VMEM((8, RANK, 128), bf16)],
        mib=8,
    )


def solution(mesh):
    fine = Mesh(mesh.devices.reshape(NXH, NC, NZ, NX, NY), REQ_AXES + TP_AXES)
    in_specs = (
        P(REQ_AXES, TP_AXES),
        P(None, TP_AXES),
        P(None, TP_AXES),
        P(REQ_AXES, TP_AXES, None),
        P(REQ_AXES, None, TP_AXES),
        P(REQ_AXES),
        P(REQ_AXES),
    )
    return jax.shard_map(
        body, mesh=fine, in_specs=in_specs, out_specs=P(REQ_AXES, TP_AXES), check_vma=False
    )
```

```python
import functools
import math

import jax
import jax.numpy as jnp
from jax import lax
from jax.experimental import pallas as pl
from jax.experimental.pallas import tpu as pltpu
from jax.sharding import Mesh, PartitionSpec as P

HEAD_SIZE = 128
BLOCK = 128
RANK = 32
ROPE_BASE = 500000.0
ADAPTER_SCALE = 2.0
NXH, NC, NZ, NX, NY = 2, 2, 8, 2, 4
REQ_AXES = ("xh", "c")
TP_AXES = ("z", "xl", "y")
NP = NX * NY
TA, TB = 384, 640
PACK_MIB = 56
VMEM = pl.BlockSpec(memory_space=pltpu.VMEM)
SMEM = pl.BlockSpec(memory_space=pltpu.SMEM)


def z_shift(v, s):
    return lax.ppermute(v, "z", [(i, (i + s) % NZ) for i in range(NZ)])


def z_xor(v, s):
    return lax.ppermute(v, "z", [(i, i ^ s) for i in range(NZ)])


def y_xor(v, s):
    return lax.ppermute(v, "y", [(i, i ^ s) for i in range(NY)])


def x_swap(v):
    return lax.ppermute(v, "xl", [(0, 1), (1, 0)])


def core_swap(v):
    return lax.ppermute(v, "c", [(0, 1), (1, 0)])


def xh_swap(v):
    return lax.ppermute(v, "xh", [(0, 1), (1, 0)])


def y_shift(v, s):
    return lax.ppermute(v, "y", [(i, (i + s) % NY) for i in range(NY)])


SERVED = ((1, 4, 6), (3, 5, 7, 2))
FLIP = [dx * NY + (-dy) % NY for dx in range(NX) for dy in range(NY)]


def weight_send(v, k):
    route = []
    for xh in range(NXH):
        for c in range(NC):
            if k >= len(SERVED[c]):
                continue
            dx, dy = divmod(SERVED[c][k], NY)
            for xl in range(NX):
                for y in range(NY):
                    at = xh * NX + xl
                    if dx:
                        to = at ^ 1 if c == 0 else (at + 1 if at % 2 else at - 1) % 4
                    else:
                        to = at
                    src = ((xh * NC + c) * NX + xl) * NY + y
                    dst = ((to // NX * NC + c) * NX + to % NX) * NY + (y + dy) % NY
                    route.append((src, dst))
    return lax.ppermute(v, ("xh", "c", "xl", "y"), route)


def run_copies(pairs, sem):
    copies = [pltpu.make_async_copy(src, dst, sem.at[i]) for i, (src, dst) in enumerate(pairs)]
    for copy in copies:
        copy.start()
    for copy in copies:
        copy.wait()


def weight_pairs(wq_ref, kv_ref, out, d):
    z, xl, y = (lax.axis_index(a) for a in ("z", "xl", "y"))
    p = (xl ^ (d // NY)) * NY + ((y + d) & (NY - 1))
    pairs = []
    for j in range(NZ):
        row = pl.multiple_of((((z + j) & (NZ - 1)) * NP + p) * 128, 128)
        pairs.append((wq_ref.at[pl.ds(row, 128), :], out.at[j * 128 : (j + 1) * 128, :]))
        pairs.append((kv_ref.at[:, pl.ds(row, 128)], out.at[1024 + j * 32 : 1056 + j * 32, :]))
    return pairs


def pack_first_kernel(wq_ref, kv_ref, down_ref, up_ref, out, maps, sem):
    d = jnp.where(lax.axis_index("c") == 0, SERVED[0][0], SERVED[1][0])
    pairs = [(down_ref, maps.at[:, 0:RANK, :]), (up_ref, maps.at[:, RANK : 2 * RANK, :])]
    run_copies(pairs + weight_pairs(wq_ref, kv_ref, out, d), sem)


def pack_kernel(wq_ref, kv_ref, *refs):
    outs, sem = refs[:4], refs[4]
    c = lax.axis_index("c")
    pairs = []
    for k, out in enumerate(outs, 1):
        d = jnp.where(c == 0, (SERVED[0] + (0,))[k], SERVED[1][k]) if k < 4 else 0
        pairs += weight_pairs(wq_ref, kv_ref, out, d)
    run_copies(pairs, sem)


def stack_kernel(*refs):
    for i, ref in enumerate(refs[:-1]):
        refs[-1][i] = ref[...]


def add_kernel(a_ref, b_ref, out_ref):
    out_ref[...] = a_ref[...] + b_ref[...].astype(jnp.float32)


def rope_kernel(start_ref, cos_ref, sin_ref, cos_t_ref, sin_t_ref):
    half = HEAD_SIZE // 2
    lane = lax.broadcasted_iota(jnp.int32, (BLOCK, HEAD_SIZE), 1)
    row = lax.broadcasted_iota(jnp.int32, (BLOCK, HEAD_SIZE), 0)
    steps = (lane & (half - 1)).astype(jnp.float32)
    inverse = jnp.exp(-(2.0 * steps / HEAD_SIZE) * math.log(ROPE_BASE))
    sign = jnp.where(lane < half, -1.0, 1.0).astype(jnp.float32)
    place = row.astype(jnp.float32) * inverse
    cos_in, sin_in = jnp.cos(place), jnp.sin(place)
    blocks = cos_ref.shape[0] // BLOCK
    ahead = lax.broadcasted_iota(jnp.int32, (8, HEAD_SIZE), 0).astype(jnp.float32) * BLOCK * inverse[0:8, :]
    cos_out, sin_out = jnp.cos(ahead), jnp.sin(ahead)
    first = (lax.axis_index("xh") * NC + lax.axis_index("c")) * blocks
    which = lax.broadcasted_iota(jnp.int32, (8, HEAD_SIZE), 0)
    for b in range(blocks):
        chosen = which == first + b - start_ref[b * BLOCK]
        co = jnp.sum(jnp.where(chosen, cos_out, 0.0), axis=0, keepdims=True)
        so = jnp.sum(jnp.where(chosen, sin_out, 0.0), axis=0, keepdims=True)
        rows = slice(b * BLOCK, (b + 1) * BLOCK)
        cos_ref[rows, :] = cos_in * co - sin_in * so
        sin_ref[rows, :] = (sin_in * co + cos_in * so) * sign
        cos_t_ref[:, rows] = cos_ref[rows, :].T
        sin_t_ref[:, rows] = sin_ref[rows, :].T


def low_kernel(ad_ref, h_ref, near_ref, far_ref, out_ref, narrow_ref):
    c, xh = lax.axis_index("c"), lax.axis_index("xh")
    per = near_ref.shape[1]
    for b in range(h_ref.shape[0] // BLOCK):
        a = ad_ref[b]
        owner = a // per
        at = a - owner * per
        xr, cr = (owner // NC) ^ xh, (owner % NC) ^ c
        down = jnp.where(cr == 0, near_ref[xr, at, 0:RANK, :], far_ref[xr, at, 0:RANK, :])
        out_ref[:, b * BLOCK : (b + 1) * BLOCK] = lax.dot_general(
            down,
            h_ref[b * BLOCK : (b + 1) * BLOCK, :],
            (((1,), (1,)), ((), ())),
            preferred_element_type=jnp.float32,
        )
    narrow_ref[...] = out_ref[...].astype(jnp.bfloat16)


def for_each_piece(own, mine, other, place):
    place(own, 0)
    c = lax.axis_index("c")
    for core in range(NC):

        @pl.when(c == core)
        def _():
            for k, d in enumerate(SERVED[core]):
                place(mine[k], FLIP[d])
            for k, d in enumerate(SERVED[1 - core]):
                place(other[k], FLIP[d])


def kv_product_kernel(*refs):
    h_refs, own, mine, other, low_ref = refs[0:8], refs[8], refs[9:13], refs[13], refs[14]
    outs, hbuf, kvw = refs[15:19], refs[19], refs[20]
    other = [other.at[k] for k in range(4)]
    y = lax.axis_index("y")
    for j in range(8):
        hbuf[:, j * 128 : (j + 1) * 128] = h_refs[j][...]
    for dy in range(NY):
        for t in range(2):
            at = pl.multiple_of((((y + dy) & (NY - 1)) * 2 + t) * 128, 128)
            outs[dy][512 + t * 32 : 544 + t * 32, :] = low_ref[:, pl.ds(at, 128)].astype(jnp.bfloat16)

    def place(ref, d):
        for j in range(NZ):
            kvw[d * 32 : (d + 1) * 32, j * 128 : (j + 1) * 128] = ref[1024 + j * 32 : 1056 + j * 32, :]

    for_each_piece(own, mine, other, place)
    kv = lax.dot_general(
        kvw[...], hbuf[...], (((1,), (1,)), ((), ())), preferred_element_type=jnp.float32
    ).astype(jnp.bfloat16)
    for d in range(NP):
        dx, dy = divmod(d, NY)
        for t in range(8):
            at = t * 64 + dx * 32
            outs[dy][at : at + 32, :] = kv[d * 32 : (d + 1) * 32, t * 128 : (t + 1) * 128]


def q_product_kernel(hbuf, own, *refs):
    mine, other = refs[0:4], [refs[4].at[k] for k in range(4)]
    near_ref, far_ref, outs, wq = refs[5], refs[6], refs[7:11], refs[11]

    def place(ref, d):
        dx, dy = divmod(d, NY)
        wq[dy, :, dx * 128 : (dx + 1) * 128] = ref[0:1024, :]

    for_each_piece(own, mine, other, place)
    for dy in range(NY):
        q = jnp.dot(hbuf[0:TA, :], wq[dy], preferred_element_type=jnp.float32).astype(jnp.bfloat16)
        near_ref[dy * TA : (dy + 1) * TA, :] = q[:, 0:128]
        far_ref[dy * TA : (dy + 1) * TA, :] = q[:, 128:256]
    for dy in range(NY):
        q = jnp.dot(hbuf[TA:1024, :], wq[dy], preferred_element_type=jnp.float32).astype(jnp.bfloat16)
        outs[dy][0:TB, :] = q[:, 0:128]
        outs[dy][TB : 2 * TB, :] = q[:, 128:256]


def wide(ref, rows):
    return ref[rows, :].astype(jnp.float32)


def kv_join_kernel(k0, k1, k2, k3, far_ref, sum_ref, low_ref, send_ref):
    total = wide(k0, ...) + wide(k1, ...) + wide(k2, ...) + wide(k3, ...)
    sum_ref[...] = total[0:512, :]
    low_ref[...] = total[512:576, :]
    send_ref[0 : NY * TA, :] = far_ref[...]
    send_ref[NY * TA :, :] = total[0:512, :].astype(jnp.bfloat16)


def stage_a_kernel(near_ref, got_ref, kv_ref, low_ref, own_ref, kv_out, *sends):
    for t in range(8):
        for dx in range(NX):
            a, b = t * 64 + dx * 32, NY * TA + t * 64 + (1 - dx) * 32
            kv_out[a : a + 32, :] = (kv_ref[a : a + 32, :] + wide(got_ref, slice(b, b + 32))).astype(jnp.bfloat16)
    kv_out[512:576, :] = low_ref[...].astype(jnp.bfloat16)
    for dy in range(NY):
        rows = slice(dy * TA, (dy + 1) * TA)
        total = wide(near_ref, rows) + wide(got_ref, rows)
        if dy == 0:
            own_ref[...] = total
        else:
            sends[dy - 1][0:TA, :] = total.astype(jnp.bfloat16)
            sends[dy - 1][TA:, :] = kv_out[...]


def stage_b_kernel(b0, b1, b2, b3, own_ref, send_ref):
    for dx, out in enumerate((own_ref, send_ref)):
        rows = slice(dx * TB, (dx + 1) * TB)
        out[...] = (wide(b0, rows) + wide(b1, rows) + wide(b2, rows) + wide(b3, rows)).astype(out.dtype)


def attention_kernel(ad_ref, start_ref, *refs):
    a_own, a_got, b_own, b_got, kv_own = refs[0], refs[1:4], refs[4], refs[5], refs[6]
    near_ref, far_ref, cos_ref, sin_ref, cos_t_ref, sin_t_ref = refs[7:13]
    out_ref = refs[13]
    kvt, k_buf, v_buf, low_buf = refs[14:18]
    xl, y, c, xh = (lax.axis_index(a) for a in ("xl", "y", "c", "xh"))
    first = (xh * NC + c) * 8
    for i in range(NY):
        ref, base = (kv_own, 0) if i == 0 else (a_got[i - 1], TA)
        for t in range(2):
            low_buf[((y - i) & (NY - 1)) * 2 + t] = ref[base + 512 + t * 32 : base + 544 + t * 32, :]
        for dx in range(NX):
            p = (xl ^ dx) * NY + ((y - i) & (NY - 1))
            at = pl.multiple_of(p * 32, 32)
            for t in range(8):
                kvt[pl.ds(at, 32), t * 128 : (t + 1) * 128] = ref[base + t * 64 + dx * 32 : base + t * 64 + dx * 32 + 32, :]

    def rope(v, rows):
        return v * cos_ref[rows, :] + pltpu.roll(v, 64, 1) * sin_ref[rows, :]

    for t in range(8):
        rows = slice(t * 128, (t + 1) * 128)
        k = kvt[0:128, rows].astype(jnp.float32)
        turned = jnp.concatenate([k[64:128, :], k[0:64, :]], axis=0)
        k_buf[:, rows] = (k * cos_t_ref[:, rows] + turned * sin_t_ref[:, rows]).astype(jnp.bfloat16)
        v_buf[rows, :] = kvt[128:256, rows].T
    per = near_ref.shape[1]
    factor = math.log2(math.e) / math.sqrt(HEAD_SIZE)
    for b in range(8):
        rows = slice(b * 128, (b + 1) * 128)
        a = ad_ref[b]
        owner = a // per
        at = a - owner * per
        xr, cr = (owner // NC) ^ xh, (owner % NC) ^ c
        up = jnp.where(cr == 0, near_ref[xr, at, RANK : 2 * RANK, :], far_ref[xr, at, RANK : 2 * RANK, :])
        q = ADAPTER_SCALE * lax.dot_general(
            low_buf[b], up, (((0,), (0,)), ((), ())), preferred_element_type=jnp.float32
        )
        if b * 128 < TA:
            q += a_own[rows, :]
            for ref in a_got:
                q += wide(ref, rows)
        else:
            part = slice(b * 128 - TA, (b + 1) * 128 - TA)
            q += b_own[part, :] + wide(b_got, part)
        q = rope(q, rows).astype(jnp.bfloat16)
        n = (b + 1) * 128
        s = jnp.dot(q, k_buf[:, 0:n], preferred_element_type=jnp.float32)
        col = lax.broadcasted_iota(jnp.int32, (128, n), 1)
        row = lax.broadcasted_iota(jnp.int32, (128, n), 0) + b * 128
        allowed = (col >= (start_ref[b * BLOCK] - first) * BLOCK) & (col <= row)
        s = jnp.where(allowed, s, -1e30)
        e = jnp.exp2((s - jnp.max(s, axis=1, keepdims=True)) * factor)
        mixed = jnp.dot(e.astype(jnp.bfloat16), v_buf[0:n, :], preferred_element_type=jnp.float32)
        out_ref[rows, :] = (mixed * (1.0 / jnp.sum(e, axis=1, keepdims=True))).astype(jnp.bfloat16)


def call(kernel, name, outs, *args, scalars=0, scratch=(), mib=4, space=pltpu.VMEM):
    single = isinstance(outs, jax.ShapeDtypeStruct)
    return pl.pallas_call(
        kernel,
        out_shape=outs,
        in_specs=[SMEM] * scalars + [pl.BlockSpec(memory_space=space)] * (len(args) - scalars),
        out_specs=VMEM if single else [VMEM] * len(outs),
        scratch_shapes=scratch,
        compiler_params=pltpu.CompilerParams(vmem_limit_bytes=mib << 20),
        name=name,
    )(*args)


def after(value, *others):
    return lax.optimization_barrier((value, *others))[0]


def body(hidden, query_weight, key_value_weight, down_maps, up_maps, request_start, adapters):
    rows = hidden.shape[0]
    bf16, f32 = jnp.bfloat16, jnp.float32
    of = jax.ShapeDtypeStruct
    kv_rows = key_value_weight.T
    first, maps = call(
        pack_first_kernel,
        "pack_first",
        [of((1280, 128), bf16), of((down_maps.shape[0], 2 * RANK, 128), bf16)],
        query_weight,
        kv_rows,
        jnp.transpose(down_maps, (0, 2, 1)),
        up_maps,
        scratch=[pltpu.SemaphoreType.DMA((2 * NZ + 2,))],
        space=pltpu.HBM,
        mib=PACK_MIB,
    )
    cosines, *turns = call(
        rope_kernel,
        "rope",
        [of((rows, HEAD_SIZE), f32)] * 2 + [of((HEAD_SIZE, rows), f32)] * 2,
        request_start,
        scalars=1,
    )
    sends = call(
        pack_kernel,
        "pack",
        [of((1280, 128), bf16)] * 4,
        after(query_weight, first, cosines),
        kv_rows,
        scratch=[pltpu.SemaphoreType.DMA((8 * NZ,))],
        space=pltpu.HBM,
        mib=PACK_MIB,
    )
    sends = [first, *sends]
    twin = xh_swap(maps)
    ring = [(hidden, hidden)]

    def ring_step(*others):
        r, l = ring[-1]
        if len(ring) > 1:
            r, l = after(r, l, *others), after(l, r, *others)
        ring.append((z_shift(r, 1), z_shift(l, -1) if len(ring) < 4 else None))

    def added(low, sent):
        return call(add_kernel, "low_add", of(low.shape, f32), low, sent)

    ring_step()
    mine = [weight_send(after(sends[0], sends[1]), 0), weight_send(after(sends[1], *ring[1]), 1), None, weight_send(sends[3], 3)]
    near = jnp.stack([maps, after(twin, *ring[1])])
    ring_step(mine[0], near)
    far = core_swap(near)
    mine[2] = weight_send(after(sends[2], *ring[2]), 2)
    low, narrow = call(
        low_kernel, "low", [of((RANK, rows), f32), of((RANK, rows), bf16)], adapters, hidden, near, far, scalars=1
    )
    low = added(low, z_xor(narrow, 4))
    ring_step(mine[1], mine[3], low)
    ring_step(mine[2])
    mine[3] = after(mine[3], *ring[3])
    other = core_swap(call(stack_kernel, "stack", of((4, 1280, 128), bf16), *mine))
    right, left = zip(*ring)

    shards = [hidden, left[1], left[2], left[3], right[4], right[3], right[2], right[1]]
    weights = (sends[4], *mine, other)
    *kv_parts, gathered = call(
        kv_product_kernel,
        "kv_product",
        [of((576, 128), bf16)] * NY + [of((rows, 1024), bf16)],
        *shards,
        *weights,
        low,
        scratch=[pltpu.VMEM((256, 1024), bf16)],
        mib=8,
    )
    kv_got = [y_shift(kv_parts[dy], dy) for dy in (2, 1, 3)]
    near_a, far_a, *b_parts = call(
        q_product_kernel,
        "q_product",
        [of((NY * TA, 128), bf16)] * 2 + [of((2 * TB, 128), bf16)] * NY,
        gathered,
        *weights,
        scratch=[pltpu.VMEM((NY, 1024, 256), bf16)],
        mib=10,
    )
    b_got = [y_shift(b_parts[dy], dy) for dy in (2, 1, 3)]
    kv_sum, low, x_send = call(
        kv_join_kernel,
        "kv_join",
        [of((512, 128), f32), of((64, 128), f32), of((NY * TA + 512, 128), bf16)],
        kv_parts[0],
        *kv_got,
        far_a,
    )
    x_got = x_swap(x_send)
    low = added(low, z_xor(low, 1))
    low = added(low, z_xor(low, 2))
    low = added(low, x_swap(low))
    a_own, kv_own, *a_sends = call(
        stage_a_kernel,
        "stage_a",
        [of((TA, 128), f32), of((576, 128), bf16)] + [of((TA + 576, 128), bf16)] * (NY - 1),
        near_a,
        x_got,
        kv_sum,
        low,
    )
    a_got = {dy: y_shift(a_sends[dy - 1], dy) for dy in (2, 1, 3)}
    b_own, b_send = call(
        stage_b_kernel, "stage_b", [of((TB, 128), f32), of((TB, 128), bf16)], b_parts[0], *b_got
    )
    b_last = x_swap(b_send)

    return call(
        attention_kernel,
        "attention",
        of((rows, HEAD_SIZE), bf16),
        adapters,
        request_start,
        a_own,
        *[a_got[dy] for dy in (1, 2, 3)],
        b_own,
        b_last,
        kv_own,
        near,
        far,
        cosines,
        *turns,
        scalars=2,
        scratch=[pltpu.VMEM((256, rows), bf16)] + [pltpu.VMEM((HEAD_SIZE, rows), bf16), pltpu.VMEM((rows, HEAD_SIZE), bf16)] + [pltpu.VMEM((8, RANK, 128), bf16)],
        mib=8,
    )


def solution(mesh):
    fine = Mesh(mesh.devices.reshape(NXH, NC, NZ, NX, NY), REQ_AXES + TP_AXES)
    in_specs = (
        P(REQ_AXES, TP_AXES),
        P(None, TP_AXES),
        P(None, TP_AXES),
        P(REQ_AXES, TP_AXES, None),
        P(REQ_AXES, None, TP_AXES),
        P(REQ_AXES),
        P(REQ_AXES),
    )
    return jax.shard_map(
        body, mesh=fine, in_specs=in_specs, out_specs=P(REQ_AXES, TP_AXES), check_vma=False
    )
```

```python
import functools
import math

import jax
import jax.numpy as jnp
from jax import lax
from jax.experimental import pallas as pl
from jax.experimental.pallas import tpu as pltpu
from jax.sharding import Mesh, PartitionSpec as P

HEAD_SIZE = 128
BLOCK = 128
RANK = 32
ROPE_BASE = 500000.0
ADAPTER_SCALE = 2.0
NXH, NC, NZ, NX, NY = 2, 2, 8, 2, 4
REQ_AXES = ("xh", "c")
TP_AXES = ("z", "xl", "y")
NP = NX * NY
TA, TB = 384, 640
PACK_MIB = 56
VMEM = pl.BlockSpec(memory_space=pltpu.VMEM)
SMEM = pl.BlockSpec(memory_space=pltpu.SMEM)


def z_shift(v, s):
    return lax.ppermute(v, "z", [(i, (i + s) % NZ) for i in range(NZ)])


def z_xor(v, s):
    return lax.ppermute(v, "z", [(i, i ^ s) for i in range(NZ)])


def y_xor(v, s):
    return lax.ppermute(v, "y", [(i, i ^ s) for i in range(NY)])


def x_swap(v):
    return lax.ppermute(v, "xl", [(0, 1), (1, 0)])


def core_swap(v):
    return lax.ppermute(v, "c", [(0, 1), (1, 0)])


def xh_swap(v):
    return lax.ppermute(v, "xh", [(0, 1), (1, 0)])


def y_shift(v, s):
    return lax.ppermute(v, "y", [(i, (i + s) % NY) for i in range(NY)])


SERVED = ((1, 4, 6), (3, 5, 7, 2))
FLIP = [dx * NY + (-dy) % NY for dx in range(NX) for dy in range(NY)]


def weight_send(v, k):
    route = []
    for xh in range(NXH):
        for c in range(NC):
            if k >= len(SERVED[c]):
                continue
            dx, dy = divmod(SERVED[c][k], NY)
            for xl in range(NX):
                for y in range(NY):
                    at = xh * NX + xl
                    if dx:
                        to = at ^ 1 if c == 0 else (at + 1 if at % 2 else at - 1) % 4
                    else:
                        to = at
                    src = ((xh * NC + c) * NX + xl) * NY + y
                    dst = ((to // NX * NC + c) * NX + to % NX) * NY + (y + dy) % NY
                    route.append((src, dst))
    return lax.ppermute(v, ("xh", "c", "xl", "y"), route)


def run_copies(pairs, sem):
    copies = [pltpu.make_async_copy(src, dst, sem.at[i]) for i, (src, dst) in enumerate(pairs)]
    for copy in copies:
        copy.start()
    for copy in copies:
        copy.wait()


def weight_pairs(wq_ref, kv_ref, out, d):
    z, xl, y = (lax.axis_index(a) for a in ("z", "xl", "y"))
    p = (xl ^ (d // NY)) * NY + ((y + d) & (NY - 1))
    pairs = []
    for j in range(NZ):
        row = pl.multiple_of((((z + j) & (NZ - 1)) * NP + p) * 128, 128)
        pairs.append((wq_ref.at[pl.ds(row, 128), :], out.at[j * 128 : (j + 1) * 128, :]))
        pairs.append((kv_ref.at[:, pl.ds(row, 128)], out.at[1024 + j * 32 : 1056 + j * 32, :]))
    return pairs


def pack_kernel(wq_ref, kv_ref, down_ref, up_ref, *refs):
    outs, maps, sem = refs[:5], refs[5], refs[6]
    c = lax.axis_index("c")
    pairs = [(down_ref, maps.at[:, 0:RANK, :]), (up_ref, maps.at[:, RANK : 2 * RANK, :])]
    for k, out in enumerate(outs):
        d = jnp.where(c == 0, (SERVED[0] + (0,))[k], SERVED[1][k]) if k < 4 else 0
        pairs += weight_pairs(wq_ref, kv_ref, out, d)
    run_copies(pairs, sem)


def stack_kernel(*refs):
    for i, ref in enumerate(refs[:-1]):
        refs[-1][i] = ref[...]


def add_kernel(a_ref, b_ref, *outs):
    total = a_ref[...] + b_ref[...].astype(jnp.float32)
    for out in outs:
        out[...] = total.astype(out.dtype)


def rope_kernel(start_ref, cos_ref, sin_ref, cos_t_ref, sin_t_ref):
    half = HEAD_SIZE // 2
    lane = lax.broadcasted_iota(jnp.int32, (BLOCK, HEAD_SIZE), 1)
    row = lax.broadcasted_iota(jnp.int32, (BLOCK, HEAD_SIZE), 0)
    steps = (lane & (half - 1)).astype(jnp.float32)
    inverse = jnp.exp(-(2.0 * steps / HEAD_SIZE) * math.log(ROPE_BASE))
    sign = jnp.where(lane < half, -1.0, 1.0).astype(jnp.float32)
    place = row.astype(jnp.float32) * inverse
    cos_in, sin_in = jnp.cos(place), jnp.sin(place)
    blocks = cos_ref.shape[0] // BLOCK
    ahead = lax.broadcasted_iota(jnp.int32, (8, HEAD_SIZE), 0).astype(jnp.float32) * BLOCK * inverse[0:8, :]
    cos_out, sin_out = jnp.cos(ahead), jnp.sin(ahead)
    first = (lax.axis_index("xh") * NC + lax.axis_index("c")) * blocks
    which = lax.broadcasted_iota(jnp.int32, (8, HEAD_SIZE), 0)
    for b in range(blocks):
        chosen = which == first + b - start_ref[b * BLOCK]
        co = jnp.sum(jnp.where(chosen, cos_out, 0.0), axis=0, keepdims=True)
        so = jnp.sum(jnp.where(chosen, sin_out, 0.0), axis=0, keepdims=True)
        rows = slice(b * BLOCK, (b + 1) * BLOCK)
        cos_ref[rows, :] = cos_in * co - sin_in * so
        sin_ref[rows, :] = (sin_in * co + cos_in * so) * sign
        cos_t_ref[:, rows] = cos_ref[rows, :].T
        sin_t_ref[:, rows] = sin_ref[rows, :].T


def low_kernel(ad_ref, h_ref, near_ref, far_ref, out_ref, narrow_ref):
    c, xh = lax.axis_index("c"), lax.axis_index("xh")
    per = near_ref.shape[1]
    for b in range(h_ref.shape[0] // BLOCK):
        a = ad_ref[b]
        owner = a // per
        at = a - owner * per
        xr, cr = (owner // NC) ^ xh, (owner % NC) ^ c
        down = jnp.where(cr == 0, near_ref[xr, at, 0:RANK, :], far_ref[xr, at, 0:RANK, :])
        out_ref[:, b * BLOCK : (b + 1) * BLOCK] = lax.dot_general(
            down,
            h_ref[b * BLOCK : (b + 1) * BLOCK, :],
            (((1,), (1,)), ((), ())),
            preferred_element_type=jnp.float32,
        )
    narrow_ref[...] = out_ref[...].astype(jnp.bfloat16)


def for_each_piece(own, mine, other, place):
    place(own, 0)
    c = lax.axis_index("c")
    for core in range(NC):

        @pl.when(c == core)
        def _():
            for k, d in enumerate(SERVED[core]):
                place(mine[k], FLIP[d])
            for k, d in enumerate(SERVED[1 - core]):
                place(other[k], FLIP[d])


def kv_product_kernel(*refs):
    h_refs, own, mine, other, low_ref = refs[0:8], refs[8], refs[9:13], refs[13], refs[14]
    outs, hbuf, kvw = refs[15:19], refs[19], refs[20]
    other = [other.at[k] for k in range(4)]
    y = lax.axis_index("y")
    for j in range(8):
        hbuf[:, j * 128 : (j + 1) * 128] = h_refs[j][...]
    for dy in range(NY):
        for t in range(2):
            at = pl.multiple_of((((y + dy) & (NY - 1)) * 2 + t) * 128, 128)
            outs[dy][512 + t * 32 : 544 + t * 32, :] = low_ref[:, pl.ds(at, 128)].astype(jnp.bfloat16)

    def place(ref, d):
        for j in range(NZ):
            kvw[d * 32 : (d + 1) * 32, j * 128 : (j + 1) * 128] = ref[1024 + j * 32 : 1056 + j * 32, :]

    for_each_piece(own, mine, other, place)
    kv = lax.dot_general(
        kvw[...], hbuf[...], (((1,), (1,)), ((), ())), preferred_element_type=jnp.float32
    ).astype(jnp.bfloat16)
    for d in range(NP):
        dx, dy = divmod(d, NY)
        for t in range(8):
            at = t * 64 + dx * 32
            outs[dy][at : at + 32, :] = kv[d * 32 : (d + 1) * 32, t * 128 : (t + 1) * 128]


def q_product_kernel(hbuf, own, *refs):
    mine, other = refs[0:4], [refs[4].at[k] for k in range(4)]
    near_ref, far_ref, outs, wq = refs[5], refs[6], refs[7:11], refs[11]

    def place(ref, d):
        dx, dy = divmod(d, NY)
        wq[dy, :, dx * 128 : (dx + 1) * 128] = ref[0:1024, :]

    for_each_piece(own, mine, other, place)
    for dy in range(NY):
        q = jnp.dot(hbuf[0:TA, :], wq[dy], preferred_element_type=jnp.float32).astype(jnp.bfloat16)
        near_ref[dy * TA : (dy + 1) * TA, :] = q[:, 0:128]
        far_ref[dy * TA : (dy + 1) * TA, :] = q[:, 128:256]
    for dy in range(NY):
        q = jnp.dot(hbuf[TA:1024, :], wq[dy], preferred_element_type=jnp.float32).astype(jnp.bfloat16)
        outs[dy][0:TB, :] = q[:, 0:128]
        outs[dy][TB : 2 * TB, :] = q[:, 128:256]


def wide(ref, rows):
    return ref[rows, :].astype(jnp.float32)


def kv_join_kernel(k0, k1, k2, k3, far_ref, sum_ref, low_ref, send_ref):
    total = wide(k0, ...) + wide(k1, ...) + wide(k2, ...) + wide(k3, ...)
    sum_ref[...] = total[0:512, :]
    low_ref[...] = total[512:576, :]
    send_ref[0 : NY * TA, :] = far_ref[...]
    send_ref[NY * TA :, :] = total[0:512, :].astype(jnp.bfloat16)


def stage_a_kernel(near_ref, got_ref, kv_ref, low_ref, own_ref, kv_out, *sends):
    for t in range(8):
        for dx in range(NX):
            a, b = t * 64 + dx * 32, NY * TA + t * 64 + (1 - dx) * 32
            kv_out[a : a + 32, :] = (kv_ref[a : a + 32, :] + wide(got_ref, slice(b, b + 32))).astype(jnp.bfloat16)
    kv_out[512:576, :] = low_ref[...].astype(jnp.bfloat16)
    for dy in range(NY):
        rows = slice(dy * TA, (dy + 1) * TA)
        total = wide(near_ref, rows) + wide(got_ref, rows)
        if dy == 0:
            own_ref[...] = total
        else:
            sends[dy - 1][0:TA, :] = total.astype(jnp.bfloat16)
            sends[dy - 1][TA:, :] = kv_out[...]


def stage_b_kernel(b0, b1, b2, b3, own_ref, send_ref):
    for dx, out in enumerate((own_ref, send_ref)):
        rows = slice(dx * TB, (dx + 1) * TB)
        out[...] = (wide(b0, rows) + wide(b1, rows) + wide(b2, rows) + wide(b3, rows)).astype(out.dtype)


def attention_kernel(ad_ref, start_ref, *refs):
    a_own, a_got, b_own, b_got, kv_own = refs[0], refs[1:4], refs[4], refs[5], refs[6]
    near_ref, far_ref, cos_ref, sin_ref, cos_t_ref, sin_t_ref = refs[7:13]
    out_ref = refs[13]
    kvt, k_buf, v_buf, low_buf = refs[14:18]
    xl, y, c, xh = (lax.axis_index(a) for a in ("xl", "y", "c", "xh"))
    first = (xh * NC + c) * 8
    for i in range(NY):
        ref, base = (kv_own, 0) if i == 0 else (a_got[i - 1], TA)
        for t in range(2):
            low_buf[((y - i) & (NY - 1)) * 2 + t] = ref[base + 512 + t * 32 : base + 544 + t * 32, :]
        for dx in range(NX):
            p = (xl ^ dx) * NY + ((y - i) & (NY - 1))
            at = pl.multiple_of(p * 32, 32)
            for t in range(8):
                kvt[pl.ds(at, 32), t * 128 : (t + 1) * 128] = ref[base + t * 64 + dx * 32 : base + t * 64 + dx * 32 + 32, :]

    def rope(v, rows):
        return v * cos_ref[rows, :] + pltpu.roll(v, 64, 1) * sin_ref[rows, :]

    for t in range(8):
        rows = slice(t * 128, (t + 1) * 128)
        k = kvt[0:128, rows].astype(jnp.float32)
        turned = jnp.concatenate([k[64:128, :], k[0:64, :]], axis=0)
        k_buf[:, rows] = (k * cos_t_ref[:, rows] + turned * sin_t_ref[:, rows]).astype(jnp.bfloat16)
        v_buf[rows, :] = kvt[128:256, rows].T
    per = near_ref.shape[1]
    factor = math.log2(math.e) / math.sqrt(HEAD_SIZE)
    for b in range(8):
        rows = slice(b * 128, (b + 1) * 128)
        a = ad_ref[b]
        owner = a // per
        at = a - owner * per
        xr, cr = (owner // NC) ^ xh, (owner % NC) ^ c
        up = jnp.where(cr == 0, near_ref[xr, at, RANK : 2 * RANK, :], far_ref[xr, at, RANK : 2 * RANK, :])
        q = ADAPTER_SCALE * lax.dot_general(
            low_buf[b], up, (((0,), (0,)), ((), ())), preferred_element_type=jnp.float32
        )
        if b * 128 < TA:
            q += a_own[rows, :]
            for ref in a_got:
                q += wide(ref, rows)
        else:
            part = slice(b * 128 - TA, (b + 1) * 128 - TA)
            q += b_own[part, :] + wide(b_got, part)
        q = rope(q, rows).astype(jnp.bfloat16)
        n = (b + 1) * 128
        s = jnp.dot(q, k_buf[:, 0:n], preferred_element_type=jnp.float32)
        col = lax.broadcasted_iota(jnp.int32, (128, n), 1)
        row = lax.broadcasted_iota(jnp.int32, (128, n), 0) + b * 128
        allowed = (col >= (start_ref[b * BLOCK] - first) * BLOCK) & (col <= row)
        s = jnp.where(allowed, s, -1e30)
        e = jnp.exp2((s - jnp.max(s, axis=1, keepdims=True)) * factor)
        mixed = jnp.dot(e.astype(jnp.bfloat16), v_buf[0:n, :], preferred_element_type=jnp.float32)
        out_ref[rows, :] = (mixed * (1.0 / jnp.sum(e, axis=1, keepdims=True))).astype(jnp.bfloat16)


def call(kernel, name, outs, *args, scalars=0, scratch=(), mib=4, space=pltpu.VMEM):
    single = isinstance(outs, jax.ShapeDtypeStruct)
    return pl.pallas_call(
        kernel,
        out_shape=outs,
        in_specs=[SMEM] * scalars + [pl.BlockSpec(memory_space=space)] * (len(args) - scalars),
        out_specs=VMEM if single else [VMEM] * len(outs),
        scratch_shapes=scratch,
        compiler_params=pltpu.CompilerParams(vmem_limit_bytes=mib << 20),
        name=name,
    )(*args)


def after(value, *others):
    return lax.optimization_barrier((value, *others))[0]


def body(hidden, query_weight, key_value_weight, down_maps, up_maps, request_start, adapters):
    rows = hidden.shape[0]
    bf16, f32 = jnp.bfloat16, jnp.float32
    of = jax.ShapeDtypeStruct
    *sends, maps = call(
        pack_kernel,
        "pack",
        [of((1280, 128), bf16)] * 5 + [of((down_maps.shape[0], 2 * RANK, 128), bf16)],
        query_weight,
        key_value_weight.T,
        jnp.transpose(down_maps, (0, 2, 1)),
        up_maps,
        scratch=[pltpu.SemaphoreType.DMA((10 * NZ + 2,))],
        space=pltpu.HBM,
        mib=PACK_MIB,
    )
    cosines, *turns = call(
        rope_kernel,
        "rope",
        [of((rows, HEAD_SIZE), f32)] * 2 + [of((HEAD_SIZE, rows), f32)] * 2,
        request_start,
        scalars=1,
    )
    twin = xh_swap(maps)
    ring = [(hidden, hidden)]

    def ring_step(*others):
        r, l = ring[-1]
        if len(ring) > 1:
            r, l = after(r, l, *others), after(l, r, *others)
        ring.append((z_shift(r, 1), z_shift(l, -1) if len(ring) < 4 else None))

    def added(low, sent, narrow=False):
        outs = [of(low.shape, f32)] + [of(low.shape, bf16)] * narrow
        out = call(add_kernel, "low_add", outs, low, sent)
        return out if narrow else out[0]

    ring_step()
    mine = [weight_send(sends[0], 0), weight_send(after(sends[1], *ring[1]), 1), None, weight_send(sends[3], 3)]
    near = jnp.stack([maps, after(twin, *ring[1])])
    ring_step(mine[0], mine[3], near)
    far = core_swap(near)
    mine[2] = weight_send(after(sends[2], *ring[2]), 2)
    low, narrow = call(
        low_kernel, "low", [of((RANK, rows), f32), of((RANK, rows), bf16)], adapters, hidden, near, far, scalars=1
    )
    low, narrow = added(low, z_xor(narrow, 4), narrow=True)
    ring_step(mine[1], low)
    ring_step(mine[2])
    low = added(low, z_xor(after(narrow, *ring[3]), 1))
    mine[3] = after(mine[3], *ring[3])
    other = core_swap(call(stack_kernel, "stack", of((4, 1280, 128), bf16), *mine))
    right, left = zip(*ring)

    shards = [hidden, left[1], left[2], left[3], right[4], right[3], right[2], right[1]]
    weights = (sends[4], *mine, other)
    *kv_parts, gathered = call(
        kv_product_kernel,
        "kv_product",
        [of((576, 128), bf16)] * NY + [of((rows, 1024), bf16)],
        *shards,
        *weights,
        low,
        scratch=[pltpu.VMEM((256, 1024), bf16)],
        mib=8,
    )
    kv_got = [y_shift(kv_parts[dy], dy) for dy in (2, 1, 3)]
    near_a, far_a, *b_parts = call(
        q_product_kernel,
        "q_product",
        [of((NY * TA, 128), bf16)] * 2 + [of((2 * TB, 128), bf16)] * NY,
        gathered,
        *weights,
        scratch=[pltpu.VMEM((NY, 1024, 256), bf16)],
        mib=10,
    )
    b_got = [y_shift(b_parts[dy], dy) for dy in (2, 1, 3)]
    kv_sum, low, x_send = call(
        kv_join_kernel,
        "kv_join",
        [of((512, 128), f32), of((64, 128), f32), of((NY * TA + 512, 128), bf16)],
        kv_parts[0],
        *kv_got,
        far_a,
    )
    x_got = x_swap(x_send)
    low = added(low, z_xor(low, 2))
    low = added(low, x_swap(low))
    a_own, kv_own, *a_sends = call(
        stage_a_kernel,
        "stage_a",
        [of((TA, 128), f32), of((576, 128), bf16)] + [of((TA + 576, 128), bf16)] * (NY - 1),
        near_a,
        x_got,
        kv_sum,
        low,
    )
    a_got = {dy: y_shift(a_sends[dy - 1], dy) for dy in (2, 1, 3)}
    b_own, b_send = call(
        stage_b_kernel, "stage_b", [of((TB, 128), f32), of((TB, 128), bf16)], b_parts[0], *b_got
    )
    b_last = x_swap(b_send)

    return call(
        attention_kernel,
        "attention",
        of((rows, HEAD_SIZE), bf16),
        adapters,
        request_start,
        a_own,
        *[a_got[dy] for dy in (1, 2, 3)],
        b_own,
        b_last,
        kv_own,
        near,
        far,
        cosines,
        *turns,
        scalars=2,
        scratch=[pltpu.VMEM((256, rows), bf16)] + [pltpu.VMEM((HEAD_SIZE, rows), bf16), pltpu.VMEM((rows, HEAD_SIZE), bf16)] + [pltpu.VMEM((8, RANK, 128), bf16)],
        mib=8,
    )


def solution(mesh):
    fine = Mesh(mesh.devices.reshape(NXH, NC, NZ, NX, NY), REQ_AXES + TP_AXES)
    in_specs = (
        P(REQ_AXES, TP_AXES),
        P(None, TP_AXES),
        P(None, TP_AXES),
        P(REQ_AXES, TP_AXES, None),
        P(REQ_AXES, None, TP_AXES),
        P(REQ_AXES),
        P(REQ_AXES),
    )
    return jax.shard_map(
        body, mesh=fine, in_specs=in_specs, out_specs=P(REQ_AXES, TP_AXES), check_vma=False
    )
```

```python
import functools
import math

import jax
import jax.numpy as jnp
from jax import lax
from jax.experimental import pallas as pl
from jax.experimental.pallas import tpu as pltpu
from jax.sharding import Mesh, PartitionSpec as P

HEAD_SIZE = 128
BLOCK = 128
RANK = 32
ROPE_BASE = 500000.0
ADAPTER_SCALE = 2.0
NXH, NC, NZ, NX, NY = 2, 2, 8, 2, 4
REQ_AXES = ("xh", "c")
TP_AXES = ("z", "xl", "y")
NP = NX * NY
TA, TB = 384, 640
PACK_MIB = 56
VMEM = pl.BlockSpec(memory_space=pltpu.VMEM)
SMEM = pl.BlockSpec(memory_space=pltpu.SMEM)


def z_shift(v, s):
    return lax.ppermute(v, "z", [(i, (i + s) % NZ) for i in range(NZ)])


def z_xor(v, s):
    return lax.ppermute(v, "z", [(i, i ^ s) for i in range(NZ)])


def y_xor(v, s):
    return lax.ppermute(v, "y", [(i, i ^ s) for i in range(NY)])


def x_swap(v):
    return lax.ppermute(v, "xl", [(0, 1), (1, 0)])


def core_swap(v):
    return lax.ppermute(v, "c", [(0, 1), (1, 0)])


def xh_swap(v):
    return lax.ppermute(v, "xh", [(0, 1), (1, 0)])


def y_shift(v, s):
    return lax.ppermute(v, "y", [(i, (i + s) % NY) for i in range(NY)])


SERVED = ((1, 4, 6), (3, 5, 7, 2))
FLIP = [dx * NY + (-dy) % NY for dx in range(NX) for dy in range(NY)]


def weight_send(v, k):
    route = []
    for xh in range(NXH):
        for c in range(NC):
            if k >= len(SERVED[c]):
                continue
            dx, dy = divmod(SERVED[c][k], NY)
            for xl in range(NX):
                for y in range(NY):
                    at = xh * NX + xl
                    if dx:
                        to = at ^ 1 if c == 0 else (at + 1 if at % 2 else at - 1) % 4
                    else:
                        to = at
                    src = ((xh * NC + c) * NX + xl) * NY + y
                    dst = ((to // NX * NC + c) * NX + to % NX) * NY + (y + dy) % NY
                    route.append((src, dst))
    return lax.ppermute(v, ("xh", "c", "xl", "y"), route)


def run_copies(pairs, sem):
    copies = [pltpu.make_async_copy(src, dst, sem.at[i]) for i, (src, dst) in enumerate(pairs)]
    for copy in copies:
        copy.start()
    for copy in copies:
        copy.wait()


def weight_pairs(wq_ref, kv_ref, out, d):
    z, xl, y = (lax.axis_index(a) for a in ("z", "xl", "y"))
    p = (xl ^ (d // NY)) * NY + ((y + d) & (NY - 1))
    pairs = []
    for j in range(NZ):
        row = pl.multiple_of((((z + j) & (NZ - 1)) * NP + p) * 128, 128)
        pairs.append((wq_ref.at[pl.ds(row, 128), :], out.at[j * 128 : (j + 1) * 128, :]))
        pairs.append((kv_ref.at[:, pl.ds(row, 128)], out.at[1024 + j * 32 : 1056 + j * 32, :]))
    return pairs


def pack_kernel(wq_ref, kv_ref, *refs):
    outs, sem = refs[:5], refs[5]
    c = lax.axis_index("c")
    pairs = []
    for k, out in enumerate(outs):
        d = jnp.where(c == 0, (SERVED[0] + (0,))[k], SERVED[1][k]) if k < 4 else 0
        pairs += weight_pairs(wq_ref, kv_ref, out, d)
    run_copies(pairs, sem)


def stack_kernel(*refs):
    for i, ref in enumerate(refs[:-1]):
        refs[-1][i] = ref[...]


def add_kernel(a_ref, b_ref, *outs):
    total = a_ref[...] + b_ref[...].astype(jnp.float32)
    for out in outs:
        out[...] = total.astype(out.dtype)


def rope_kernel(start_ref, cos_ref, sin_ref, cos_t_ref, sin_t_ref):
    half = HEAD_SIZE // 2
    lane = lax.broadcasted_iota(jnp.int32, (BLOCK, HEAD_SIZE), 1)
    row = lax.broadcasted_iota(jnp.int32, (BLOCK, HEAD_SIZE), 0)
    steps = (lane & (half - 1)).astype(jnp.float32)
    inverse = jnp.exp(-(2.0 * steps / HEAD_SIZE) * math.log(ROPE_BASE))
    sign = jnp.where(lane < half, -1.0, 1.0).astype(jnp.float32)
    place = row.astype(jnp.float32) * inverse
    cos_in, sin_in = jnp.cos(place), jnp.sin(place)
    blocks = cos_ref.shape[0] // BLOCK
    ahead = lax.broadcasted_iota(jnp.int32, (8, HEAD_SIZE), 0).astype(jnp.float32) * BLOCK * inverse[0:8, :]
    cos_out, sin_out = jnp.cos(ahead), jnp.sin(ahead)
    first = (lax.axis_index("xh") * NC + lax.axis_index("c")) * blocks
    which = lax.broadcasted_iota(jnp.int32, (8, HEAD_SIZE), 0)
    for b in range(blocks):
        chosen = which == first + b - start_ref[b * BLOCK]
        co = jnp.sum(jnp.where(chosen, cos_out, 0.0), axis=0, keepdims=True)
        so = jnp.sum(jnp.where(chosen, sin_out, 0.0), axis=0, keepdims=True)
        rows = slice(b * BLOCK, (b + 1) * BLOCK)
        cos_ref[rows, :] = cos_in * co - sin_in * so
        sin_ref[rows, :] = (sin_in * co + cos_in * so) * sign
        cos_t_ref[:, rows] = cos_ref[rows, :].T
        sin_t_ref[:, rows] = sin_ref[rows, :].T


def low_kernel(ad_ref, h_ref, near_ref, far_ref, out_ref, narrow_ref):
    c, xh = lax.axis_index("c"), lax.axis_index("xh")
    per = near_ref.shape[1]
    for b in range(h_ref.shape[0] // BLOCK):
        a = ad_ref[b]
        owner = a // per
        at = a - owner * per
        xr, cr = (owner // NC) ^ xh, (owner % NC) ^ c
        down = jnp.where(cr == 0, near_ref[xr, at], far_ref[xr, at])
        out_ref[:, b * BLOCK : (b + 1) * BLOCK] = lax.dot_general(
            down,
            h_ref[b * BLOCK : (b + 1) * BLOCK, :],
            (((1,), (1,)), ((), ())),
            preferred_element_type=jnp.float32,
        )
    narrow_ref[...] = out_ref[...].astype(jnp.bfloat16)


def for_each_piece(own, mine, other, place):
    place(own, 0)
    c = lax.axis_index("c")
    for core in range(NC):

        @pl.when(c == core)
        def _():
            for k, d in enumerate(SERVED[core]):
                place(mine[k], FLIP[d])
            for k, d in enumerate(SERVED[1 - core]):
                place(other[k], FLIP[d])


def kv_product_kernel(*refs):
    h_refs, own, mine, other, low_ref = refs[0:8], refs[8], refs[9:13], refs[13], refs[14]
    outs, hbuf, kvw = refs[15:19], refs[19], refs[20]
    other = [other.at[k] for k in range(4)]
    y = lax.axis_index("y")
    for j in range(8):
        hbuf[:, j * 128 : (j + 1) * 128] = h_refs[j][...]
    for dy in range(NY):
        for t in range(2):
            at = pl.multiple_of((((y + dy) & (NY - 1)) * 2 + t) * 128, 128)
            outs[dy][512 + t * 32 : 544 + t * 32, :] = low_ref[:, pl.ds(at, 128)].astype(jnp.bfloat16)

    def place(ref, d):
        for j in range(NZ):
            kvw[d * 32 : (d + 1) * 32, j * 128 : (j + 1) * 128] = ref[1024 + j * 32 : 1056 + j * 32, :]

    for_each_piece(own, mine, other, place)
    kv = lax.dot_general(
        kvw[...], hbuf[...], (((1,), (1,)), ((), ())), preferred_element_type=jnp.float32
    ).astype(jnp.bfloat16)
    for d in range(NP):
        dx, dy = divmod(d, NY)
        for t in range(8):
            at = t * 64 + dx * 32
            outs[dy][at : at + 32, :] = kv[d * 32 : (d + 1) * 32, t * 128 : (t + 1) * 128]


def q_product_kernel(hbuf, own, *refs):
    mine, other = refs[0:4], [refs[4].at[k] for k in range(4)]
    near_ref, far_ref, outs, wq = refs[5], refs[6], refs[7:11], refs[11]

    def place(ref, d):
        dx, dy = divmod(d, NY)
        wq[dy, :, dx * 128 : (dx + 1) * 128] = ref[0:1024, :]

    for_each_piece(own, mine, other, place)
    for dy in range(NY):
        q = jnp.dot(hbuf[0:TA, :], wq[dy], preferred_element_type=jnp.float32).astype(jnp.bfloat16)
        near_ref[dy * TA : (dy + 1) * TA, :] = q[:, 0:128]
        far_ref[dy * TA : (dy + 1) * TA, :] = q[:, 128:256]
    for dy in range(NY):
        q = jnp.dot(hbuf[TA:1024, :], wq[dy], preferred_element_type=jnp.float32).astype(jnp.bfloat16)
        outs[dy][0:TB, :] = q[:, 0:128]
        outs[dy][TB : 2 * TB, :] = q[:, 128:256]


def wide(ref, rows):
    return ref[rows, :].astype(jnp.float32)


def kv_join_kernel(k0, k1, k2, k3, far_ref, sum_ref, low_ref, send_ref):
    total = wide(k0, ...) + wide(k1, ...) + wide(k2, ...) + wide(k3, ...)
    sum_ref[...] = total[0:512, :]
    low_ref[...] = total[512:576, :]
    send_ref[0 : NY * TA, :] = far_ref[...]
    send_ref[NY * TA :, :] = total[0:512, :].astype(jnp.bfloat16)


def stage_a_kernel(near_ref, got_ref, kv_ref, low_ref, own_ref, kv_out, *sends):
    for t in range(8):
        for dx in range(NX):
            a, b = t * 64 + dx * 32, NY * TA + t * 64 + (1 - dx) * 32
            kv_out[a : a + 32, :] = (kv_ref[a : a + 32, :] + wide(got_ref, slice(b, b + 32))).astype(jnp.bfloat16)
    kv_out[512:576, :] = low_ref[...].astype(jnp.bfloat16)
    for dy in range(NY):
        rows = slice(dy * TA, (dy + 1) * TA)
        total = wide(near_ref, rows) + wide(got_ref, rows)
        if dy == 0:
            own_ref[...] = total
        else:
            sends[dy - 1][0:TA, :] = total.astype(jnp.bfloat16)
            sends[dy - 1][TA:, :] = kv_out[...]


def stage_b_kernel(b0, b1, b2, b3, own_ref, send_ref):
    for dx, out in enumerate((own_ref, send_ref)):
        rows = slice(dx * TB, (dx + 1) * TB)
        out[...] = (wide(b0, rows) + wide(b1, rows) + wide(b2, rows) + wide(b3, rows)).astype(out.dtype)


def attention_kernel(ad_ref, start_ref, *refs):
    a_own, a_got, b_own, b_got, kv_own = refs[0], refs[1:4], refs[4], refs[5], refs[6]
    near_ref, far_ref, cos_ref, sin_ref, cos_t_ref, sin_t_ref = refs[7:13]
    out_ref = refs[13]
    kvt, k_buf, v_buf, low_buf = refs[14:18]
    xl, y, c, xh = (lax.axis_index(a) for a in ("xl", "y", "c", "xh"))
    first = (xh * NC + c) * 8
    for i in range(NY):
        ref, base = (kv_own, 0) if i == 0 else (a_got[i - 1], TA)
        for t in range(2):
            low_buf[((y - i) & (NY - 1)) * 2 + t] = ref[base + 512 + t * 32 : base + 544 + t * 32, :]
        for dx in range(NX):
            p = (xl ^ dx) * NY + ((y - i) & (NY - 1))
            at = pl.multiple_of(p * 32, 32)
            for t in range(8):
                kvt[pl.ds(at, 32), t * 128 : (t + 1) * 128] = ref[base + t * 64 + dx * 32 : base + t * 64 + dx * 32 + 32, :]

    def rope(v, rows):
        return v * cos_ref[rows, :] + pltpu.roll(v, 64, 1) * sin_ref[rows, :]

    for t in range(8):
        rows = slice(t * 128, (t + 1) * 128)
        k = kvt[0:128, rows].astype(jnp.float32)
        turned = jnp.concatenate([k[64:128, :], k[0:64, :]], axis=0)
        k_buf[:, rows] = (k * cos_t_ref[:, rows] + turned * sin_t_ref[:, rows]).astype(jnp.bfloat16)
        v_buf[rows, :] = kvt[128:256, rows].T
    per = near_ref.shape[1]
    factor = math.log2(math.e) / math.sqrt(HEAD_SIZE)
    for b in range(8):
        rows = slice(b * 128, (b + 1) * 128)
        a = ad_ref[b]
        owner = a // per
        at = a - owner * per
        xr, cr = (owner // NC) ^ xh, (owner % NC) ^ c
        up = jnp.where(cr == 0, near_ref[xr, at], far_ref[xr, at])
        q = ADAPTER_SCALE * lax.dot_general(
            low_buf[b], up, (((0,), (0,)), ((), ())), preferred_element_type=jnp.float32
        )
        if b * 128 < TA:
            q += a_own[rows, :]
            for ref in a_got:
                q += wide(ref, rows)
        else:
            part = slice(b * 128 - TA, (b + 1) * 128 - TA)
            q += b_own[part, :] + wide(b_got, part)
        q = rope(q, rows).astype(jnp.bfloat16)
        n = (b + 1) * 128
        s = jnp.dot(q, k_buf[:, 0:n], preferred_element_type=jnp.float32)
        col = lax.broadcasted_iota(jnp.int32, (128, n), 1)
        row = lax.broadcasted_iota(jnp.int32, (128, n), 0) + b * 128
        allowed = (col >= (start_ref[b * BLOCK] - first) * BLOCK) & (col <= row)
        s = jnp.where(allowed, s, -1e30)
        e = jnp.exp2((s - jnp.max(s, axis=1, keepdims=True)) * factor)
        mixed = jnp.dot(e.astype(jnp.bfloat16), v_buf[0:n, :], preferred_element_type=jnp.float32)
        out_ref[rows, :] = (mixed * (1.0 / jnp.sum(e, axis=1, keepdims=True))).astype(jnp.bfloat16)


def call(kernel, name, outs, *args, scalars=0, scratch=(), mib=4, space=pltpu.VMEM):
    single = isinstance(outs, jax.ShapeDtypeStruct)
    return pl.pallas_call(
        kernel,
        out_shape=outs,
        in_specs=[SMEM] * scalars + [pl.BlockSpec(memory_space=space)] * (len(args) - scalars),
        out_specs=VMEM if single else [VMEM] * len(outs),
        scratch_shapes=scratch,
        compiler_params=pltpu.CompilerParams(vmem_limit_bytes=mib << 20),
        name=name,
    )(*args)


def after(value, *others):
    return lax.optimization_barrier((value, *others))[0]


def body(hidden, query_weight, key_value_weight, down_maps, up_maps, request_start, adapters):
    rows = hidden.shape[0]
    bf16, f32 = jnp.bfloat16, jnp.float32
    of = jax.ShapeDtypeStruct
    sends = call(
        pack_kernel,
        "pack",
        [of((1280, 128), bf16)] * 5,
        query_weight,
        key_value_weight.T,
        scratch=[pltpu.SemaphoreType.DMA((10 * NZ,))],
        space=pltpu.HBM,
        mib=PACK_MIB,
    )
    cosines, *turns = call(
        rope_kernel,
        "rope",
        [of((rows, HEAD_SIZE), f32)] * 2 + [of((HEAD_SIZE, rows), f32)] * 2,
        request_start,
        scalars=1,
    )
    down_maps = jnp.transpose(down_maps, (0, 2, 1))
    pair = of((2, *down_maps.shape), bf16)
    twin = xh_swap(down_maps)
    ring = [(hidden, hidden)]

    def ring_step(*others):
        r, l = ring[-1]
        if len(ring) > 1:
            r, l = after(r, l, *others), after(l, r, *others)
        ring.append((z_shift(r, 1), z_shift(l, -1) if len(ring) < 4 else None))

    def added(low, sent, narrow=False):
        outs = [of(low.shape, f32)] + [of(low.shape, bf16)] * narrow
        out = call(add_kernel, "low_add", outs, low, sent)
        return out if narrow else out[0]

    ring_step()
    mine = [weight_send(sends[0], 0), weight_send(after(sends[1], *ring[1]), 1), None, weight_send(sends[3], 3)]
    near = call(stack_kernel, "near", pair, down_maps, after(twin, *ring[1]))
    ring_step(mine[0], mine[3], near)
    far = core_swap(near)
    mine[2] = weight_send(after(sends[2], *ring[2]), 2)
    low, narrow = call(
        low_kernel, "low", [of((RANK, rows), f32), of((RANK, rows), bf16)], adapters, hidden, near, far, scalars=1
    )
    low, narrow = added(low, z_xor(narrow, 4), narrow=True)
    ring_step(mine[1], low)
    ring_step(mine[2])
    low = added(low, z_xor(after(narrow, *ring[3]), 1))
    mine[3] = after(mine[3], *ring[3])
    other = core_swap(call(stack_kernel, "stack", of((4, 1280, 128), bf16), *mine))
    near = call(stack_kernel, "near", pair, up_maps, xh_swap(after(up_maps, *ring[3])))
    far = core_swap(near)
    right, left = zip(*ring)

    shards = [after(hidden, near), left[1], left[2], left[3], right[4], right[3], right[2], right[1]]
    weights = (sends[4], *mine, other)
    *kv_parts, gathered = call(
        kv_product_kernel,
        "kv_product",
        [of((576, 128), bf16)] * NY + [of((rows, 1024), bf16)],
        *shards,
        *weights,
        low,
        scratch=[pltpu.VMEM((256, 1024), bf16)],
        mib=8,
    )
    kv_got = [y_shift(kv_parts[dy], dy) for dy in (2, 1, 3)]
    near_a, far_a, *b_parts = call(
        q_product_kernel,
        "q_product",
        [of((NY * TA, 128), bf16)] * 2 + [of((2 * TB, 128), bf16)] * NY,
        gathered,
        *weights,
        scratch=[pltpu.VMEM((NY, 1024, 256), bf16)],
        mib=10,
    )
    b_got = [y_shift(b_parts[dy], dy) for dy in (2, 1, 3)]
    kv_sum, low, x_send = call(
        kv_join_kernel,
        "kv_join",
        [of((512, 128), f32), of((64, 128), f32), of((NY * TA + 512, 128), bf16)],
        kv_parts[0],
        *kv_got,
        far_a,
    )
    x_got = x_swap(x_send)
    low = added(low, z_xor(low, 2))
    low = added(low, x_swap(low))
    a_own, kv_own, *a_sends = call(
        stage_a_kernel,
        "stage_a",
        [of((TA, 128), f32), of((576, 128), bf16)] + [of((TA + 576, 128), bf16)] * (NY - 1),
        near_a,
        x_got,
        kv_sum,
        low,
    )
    a_got = {dy: y_shift(a_sends[dy - 1], dy) for dy in (2, 1, 3)}
    b_own, b_send = call(
        stage_b_kernel, "stage_b", [of((TB, 128), f32), of((TB, 128), bf16)], b_parts[0], *b_got
    )
    b_last = x_swap(b_send)

    return call(
        attention_kernel,
        "attention",
        of((rows, HEAD_SIZE), bf16),
        adapters,
        request_start,
        a_own,
        *[a_got[dy] for dy in (1, 2, 3)],
        b_own,
        b_last,
        kv_own,
        near,
        far,
        cosines,
        *turns,
        scalars=2,
        scratch=[pltpu.VMEM((256, rows), bf16)] + [pltpu.VMEM((HEAD_SIZE, rows), bf16), pltpu.VMEM((rows, HEAD_SIZE), bf16)] + [pltpu.VMEM((8, RANK, 128), bf16)],
        mib=8,
    )


def solution(mesh):
    fine = Mesh(mesh.devices.reshape(NXH, NC, NZ, NX, NY), REQ_AXES + TP_AXES)
    in_specs = (
        P(REQ_AXES, TP_AXES),
        P(None, TP_AXES),
        P(None, TP_AXES),
        P(REQ_AXES, TP_AXES, None),
        P(REQ_AXES, None, TP_AXES),
        P(REQ_AXES),
        P(REQ_AXES),
    )
    return jax.shard_map(
        body, mesh=fine, in_specs=in_specs, out_specs=P(REQ_AXES, TP_AXES), check_vma=False
    )
```

```python
import functools
import math

import jax
import jax.numpy as jnp
from jax import lax
from jax.experimental import pallas as pl
from jax.experimental.pallas import tpu as pltpu
from jax.sharding import Mesh, PartitionSpec as P

HEAD_SIZE = 128
BLOCK = 128
RANK = 32
ROPE_BASE = 500000.0
ADAPTER_SCALE = 2.0
NXH, NC, NZ, NX, NY = 2, 2, 8, 2, 4
REQ_AXES = ("xh", "c")
TP_AXES = ("z", "xl", "y")
NP = NX * NY
TA, TB = 512, 512
PACK_MIB = 56
VMEM = pl.BlockSpec(memory_space=pltpu.VMEM)
SMEM = pl.BlockSpec(memory_space=pltpu.SMEM)


def z_shift(v, s):
    return lax.ppermute(v, "z", [(i, (i + s) % NZ) for i in range(NZ)])


def z_xor(v, s):
    return lax.ppermute(v, "z", [(i, i ^ s) for i in range(NZ)])


def y_xor(v, s):
    return lax.ppermute(v, "y", [(i, i ^ s) for i in range(NY)])


def x_swap(v):
    return lax.ppermute(v, "xl", [(0, 1), (1, 0)])


def core_swap(v):
    return lax.ppermute(v, "c", [(0, 1), (1, 0)])


def xh_swap(v):
    return lax.ppermute(v, "xh", [(0, 1), (1, 0)])


def y_shift(v, s):
    return lax.ppermute(v, "y", [(i, (i + s) % NY) for i in range(NY)])


SERVED = ((1, 4, 6), (3, 5, 7, 2))
FLIP = [dx * NY + (-dy) % NY for dx in range(NX) for dy in range(NY)]


def weight_send(v, k):
    route = []
    for xh in range(NXH):
        for c in range(NC):
            if k >= len(SERVED[c]):
                continue
            dx, dy = divmod(SERVED[c][k], NY)
            for xl in range(NX):
                for y in range(NY):
                    at = xh * NX + xl
                    if dx:
                        to = at ^ 1 if c == 0 else (at + 1 if at % 2 else at - 1) % 4
                    else:
                        to = at
                    src = ((xh * NC + c) * NX + xl) * NY + y
                    dst = ((to // NX * NC + c) * NX + to % NX) * NY + (y + dy) % NY
                    route.append((src, dst))
    return lax.ppermute(v, ("xh", "c", "xl", "y"), route)


def run_copies(pairs, sem):
    copies = [pltpu.make_async_copy(src, dst, sem.at[i]) for i, (src, dst) in enumerate(pairs)]
    for copy in copies:
        copy.start()
    for copy in copies:
        copy.wait()


def weight_pairs(wq_ref, kv_ref, out, d):
    z, xl, y = (lax.axis_index(a) for a in ("z", "xl", "y"))
    p = (xl ^ (d // NY)) * NY + ((y + d) & (NY - 1))
    pairs = []
    for j in range(NZ):
        row = pl.multiple_of((((z + j) & (NZ - 1)) * NP + p) * 128, 128)
        pairs.append((wq_ref.at[pl.ds(row, 128), :], out.at[j * 128 : (j + 1) * 128, :]))
        pairs.append((kv_ref.at[:, pl.ds(row, 128)], out.at[1024 + j * 32 : 1056 + j * 32, :]))
    return pairs


def pack_kernel(wq_ref, kv_ref, down_ref, up_ref, *refs):
    outs, maps, sem = refs[:5], refs[5], refs[6]
    c = lax.axis_index("c")
    pairs = [(down_ref, maps.at[:, 0:RANK, :]), (up_ref, maps.at[:, RANK : 2 * RANK, :])]
    for k, out in enumerate(outs):
        d = jnp.where(c == 0, (SERVED[0] + (0,))[k], SERVED[1][k]) if k < 4 else 0
        pairs += weight_pairs(wq_ref, kv_ref, out, d)
    run_copies(pairs, sem)


def stack_kernel(*refs):
    for i, ref in enumerate(refs[:-1]):
        refs[-1][i] = ref[...]


def add_kernel(a_ref, b_ref, *outs):
    total = a_ref[...] + b_ref[...].astype(jnp.float32)
    for out in outs:
        out[...] = total.astype(out.dtype)


def rope_kernel(start_ref, cos_ref, sin_ref, cos_t_ref, sin_t_ref):
    half = HEAD_SIZE // 2
    lane = lax.broadcasted_iota(jnp.int32, (BLOCK, HEAD_SIZE), 1)
    row = lax.broadcasted_iota(jnp.int32, (BLOCK, HEAD_SIZE), 0)
    steps = (lane & (half - 1)).astype(jnp.float32)
    inverse = jnp.exp(-(2.0 * steps / HEAD_SIZE) * math.log(ROPE_BASE))
    sign = jnp.where(lane < half, -1.0, 1.0).astype(jnp.float32)
    place = row.astype(jnp.float32) * inverse
    cos_in, sin_in = jnp.cos(place), jnp.sin(place)
    blocks = cos_ref.shape[0] // BLOCK
    ahead = lax.broadcasted_iota(jnp.int32, (8, HEAD_SIZE), 0).astype(jnp.float32) * BLOCK * inverse[0:8, :]
    cos_out, sin_out = jnp.cos(ahead), jnp.sin(ahead)
    first = (lax.axis_index("xh") * NC + lax.axis_index("c")) * blocks
    which = lax.broadcasted_iota(jnp.int32, (8, HEAD_SIZE), 0)
    for b in range(blocks):
        chosen = which == first + b - start_ref[b * BLOCK]
        co = jnp.sum(jnp.where(chosen, cos_out, 0.0), axis=0, keepdims=True)
        so = jnp.sum(jnp.where(chosen, sin_out, 0.0), axis=0, keepdims=True)
        rows = slice(b * BLOCK, (b + 1) * BLOCK)
        cos_ref[rows, :] = cos_in * co - sin_in * so
        sin_ref[rows, :] = (sin_in * co + cos_in * so) * sign
        cos_t_ref[:, rows] = cos_ref[rows, :].T
        sin_t_ref[:, rows] = sin_ref[rows, :].T


def low_kernel(ad_ref, h_ref, near_ref, far_ref, out_ref, narrow_ref):
    c, xh = lax.axis_index("c"), lax.axis_index("xh")
    per = near_ref.shape[1]
    for b in range(h_ref.shape[0] // BLOCK):
        a = ad_ref[b]
        owner = a // per
        at = a - owner * per
        xr, cr = (owner // NC) ^ xh, (owner % NC) ^ c
        down = jnp.where(cr == 0, near_ref[xr, at, 0:RANK, :], far_ref[xr, at, 0:RANK, :])
        out_ref[:, b * BLOCK : (b + 1) * BLOCK] = lax.dot_general(
            down,
            h_ref[b * BLOCK : (b + 1) * BLOCK, :],
            (((1,), (1,)), ((), ())),
            preferred_element_type=jnp.float32,
        )
    narrow_ref[...] = out_ref[...].astype(jnp.bfloat16)


def for_each_piece(own, mine, other, place):
    place(own, 0)
    c = lax.axis_index("c")
    for core in range(NC):

        @pl.when(c == core)
        def _():
            for k, d in enumerate(SERVED[core]):
                place(mine[k], FLIP[d])
            for k, d in enumerate(SERVED[1 - core]):
                place(other[k], FLIP[d])


def kv_product_kernel(*refs):
    h_refs, own, mine, other, low_ref = refs[0:8], refs[8], refs[9:13], refs[13], refs[14]
    outs, hbuf, kvw = refs[15:19], refs[19], refs[20]
    other = [other.at[k] for k in range(4)]
    y = lax.axis_index("y")
    for j in range(8):
        hbuf[:, j * 128 : (j + 1) * 128] = h_refs[j][...]
    for dy in range(NY):
        for t in range(2):
            at = pl.multiple_of((((y + dy) & (NY - 1)) * 2 + t) * 128, 128)
            outs[dy][512 + t * 32 : 544 + t * 32, :] = low_ref[:, pl.ds(at, 128)].astype(jnp.bfloat16)

    def place(ref, d):
        for j in range(NZ):
            kvw[d * 32 : (d + 1) * 32, j * 128 : (j + 1) * 128] = ref[1024 + j * 32 : 1056 + j * 32, :]

    for_each_piece(own, mine, other, place)
    kv = lax.dot_general(
        kvw[...], hbuf[...], (((1,), (1,)), ((), ())), preferred_element_type=jnp.float32
    ).astype(jnp.bfloat16)
    for d in range(NP):
        dx, dy = divmod(d, NY)
        for t in range(8):
            at = t * 64 + dx * 32
            outs[dy][at : at + 32, :] = kv[d * 32 : (d + 1) * 32, t * 128 : (t + 1) * 128]


def q_product_kernel(hbuf, own, *refs):
    mine, other = refs[0:4], [refs[4].at[k] for k in range(4)]
    near_ref, far_ref, outs, wq = refs[5], refs[6], refs[7:11], refs[11]

    def place(ref, d):
        dx, dy = divmod(d, NY)
        wq[dy, :, dx * 128 : (dx + 1) * 128] = ref[0:1024, :]

    for_each_piece(own, mine, other, place)
    for dy in range(NY):
        q = jnp.dot(hbuf[0:TA, :], wq[dy], preferred_element_type=jnp.float32).astype(jnp.bfloat16)
        near_ref[dy * TA : (dy + 1) * TA, :] = q[:, 0:128]
        far_ref[dy * TA : (dy + 1) * TA, :] = q[:, 128:256]
    for dy in range(NY):
        q = jnp.dot(hbuf[TA:1024, :], wq[dy], preferred_element_type=jnp.float32).astype(jnp.bfloat16)
        outs[dy][0:TB, :] = q[:, 0:128]
        outs[dy][TB : 2 * TB, :] = q[:, 128:256]


def wide(ref, rows):
    return ref[rows, :].astype(jnp.float32)


def kv_join_kernel(k0, k1, k2, k3, far_ref, sum_ref, low_ref, send_ref):
    total = wide(k0, ...) + wide(k1, ...) + wide(k2, ...) + wide(k3, ...)
    sum_ref[...] = total[0:512, :]
    low_ref[...] = total[512:576, :]
    send_ref[0 : NY * TA, :] = far_ref[...]
    send_ref[NY * TA :, :] = total[0:512, :].astype(jnp.bfloat16)


def stage_a_kernel(near_ref, got_ref, kv_ref, low_ref, own_ref, kv_out, *sends):
    for t in range(8):
        for dx in range(NX):
            a, b = t * 64 + dx * 32, NY * TA + t * 64 + (1 - dx) * 32
            kv_out[a : a + 32, :] = (kv_ref[a : a + 32, :] + wide(got_ref, slice(b, b + 32))).astype(jnp.bfloat16)
    kv_out[512:576, :] = low_ref[...].astype(jnp.bfloat16)
    for dy in range(NY):
        rows = slice(dy * TA, (dy + 1) * TA)
        total = wide(near_ref, rows) + wide(got_ref, rows)
        if dy == 0:
            own_ref[...] = total
        else:
            sends[dy - 1][0:TA, :] = total.astype(jnp.bfloat16)
            sends[dy - 1][TA:, :] = kv_out[...]


def stage_b_kernel(b0, b1, b2, b3, own_ref, send_ref):
    for dx, out in enumerate((own_ref, send_ref)):
        rows = slice(dx * TB, (dx + 1) * TB)
        out[...] = (wide(b0, rows) + wide(b1, rows) + wide(b2, rows) + wide(b3, rows)).astype(out.dtype)


def attention_kernel(ad_ref, start_ref, *refs):
    a_own, a_got, b_own, b_got, kv_own = refs[0], refs[1:4], refs[4], refs[5], refs[6]
    near_ref, far_ref, cos_ref, sin_ref, cos_t_ref, sin_t_ref = refs[7:13]
    out_ref = refs[13]
    kvt, k_buf, v_buf, low_buf = refs[14:18]
    xl, y, c, xh = (lax.axis_index(a) for a in ("xl", "y", "c", "xh"))
    first = (xh * NC + c) * 8
    for i in range(NY):
        ref, base = (kv_own, 0) if i == 0 else (a_got[i - 1], TA)
        for t in range(2):
            low_buf[((y - i) & (NY - 1)) * 2 + t] = ref[base + 512 + t * 32 : base + 544 + t * 32, :]
        for dx in range(NX):
            p = (xl ^ dx) * NY + ((y - i) & (NY - 1))
            at = pl.multiple_of(p * 32, 32)
            for t in range(8):
                kvt[pl.ds(at, 32), t * 128 : (t + 1) * 128] = ref[base + t * 64 + dx * 32 : base + t * 64 + dx * 32 + 32, :]

    def rope(v, rows):
        return v * cos_ref[rows, :] + pltpu.roll(v, 64, 1) * sin_ref[rows, :]

    for t in range(8):
        rows = slice(t * 128, (t + 1) * 128)
        k = kvt[0:128, rows].astype(jnp.float32)
        turned = jnp.concatenate([k[64:128, :], k[0:64, :]], axis=0)
        k_buf[:, rows] = (k * cos_t_ref[:, rows] + turned * sin_t_ref[:, rows]).astype(jnp.bfloat16)
        v_buf[rows, :] = kvt[128:256, rows].T
    per = near_ref.shape[1]
    factor = math.log2(math.e) / math.sqrt(HEAD_SIZE)
    for b in range(8):
        rows = slice(b * 128, (b + 1) * 128)
        a = ad_ref[b]
        owner = a // per
        at = a - owner * per
        xr, cr = (owner // NC) ^ xh, (owner % NC) ^ c
        up = jnp.where(cr == 0, near_ref[xr, at, RANK : 2 * RANK, :], far_ref[xr, at, RANK : 2 * RANK, :])
        q = ADAPTER_SCALE * lax.dot_general(
            low_buf[b], up, (((0,), (0,)), ((), ())), preferred_element_type=jnp.float32
        )
        if b * 128 < TA:
            q += a_own[rows, :]
            for ref in a_got:
                q += wide(ref, rows)
        else:
            part = slice(b * 128 - TA, (b + 1) * 128 - TA)
            q += b_own[part, :] + wide(b_got, part)
        q = rope(q, rows).astype(jnp.bfloat16)
        n = (b + 1) * 128
        s = jnp.dot(q, k_buf[:, 0:n], preferred_element_type=jnp.float32)
        col = lax.broadcasted_iota(jnp.int32, (128, n), 1)
        row = lax.broadcasted_iota(jnp.int32, (128, n), 0) + b * 128
        allowed = (col >= (start_ref[b * BLOCK] - first) * BLOCK) & (col <= row)
        s = jnp.where(allowed, s, -1e30)
        e = jnp.exp2((s - jnp.max(s, axis=1, keepdims=True)) * factor)
        mixed = jnp.dot(e.astype(jnp.bfloat16), v_buf[0:n, :], preferred_element_type=jnp.float32)
        out_ref[rows, :] = (mixed * (1.0 / jnp.sum(e, axis=1, keepdims=True))).astype(jnp.bfloat16)


def call(kernel, name, outs, *args, scalars=0, scratch=(), mib=4, space=pltpu.VMEM):
    single = isinstance(outs, jax.ShapeDtypeStruct)
    return pl.pallas_call(
        kernel,
        out_shape=outs,
        in_specs=[SMEM] * scalars + [pl.BlockSpec(memory_space=space)] * (len(args) - scalars),
        out_specs=VMEM if single else [VMEM] * len(outs),
        scratch_shapes=scratch,
        compiler_params=pltpu.CompilerParams(vmem_limit_bytes=mib << 20),
        name=name,
    )(*args)


def after(value, *others):
    return lax.optimization_barrier((value, *others))[0]


def body(hidden, query_weight, key_value_weight, down_maps, up_maps, request_start, adapters):
    rows = hidden.shape[0]
    bf16, f32 = jnp.bfloat16, jnp.float32
    of = jax.ShapeDtypeStruct
    *sends, maps = call(
        pack_kernel,
        "pack",
        [of((1280, 128), bf16)] * 5 + [of((down_maps.shape[0], 2 * RANK, 128), bf16)],
        query_weight,
        key_value_weight.T,
        jnp.transpose(down_maps, (0, 2, 1)),
        up_maps,
        scratch=[pltpu.SemaphoreType.DMA((10 * NZ + 2,))],
        space=pltpu.HBM,
        mib=PACK_MIB,
    )
    cosines, *turns = call(
        rope_kernel,
        "rope",
        [of((rows, HEAD_SIZE), f32)] * 2 + [of((HEAD_SIZE, rows), f32)] * 2,
        request_start,
        scalars=1,
    )
    twin = xh_swap(maps)
    ring = [(hidden, hidden)]

    def ring_step(*others):
        r, l = ring[-1]
        if len(ring) > 1:
            r, l = after(r, l, *others), after(l, r, *others)
        ring.append((z_shift(r, 1), z_shift(l, -1) if len(ring) < 4 else None))

    def added(low, sent, narrow=False):
        outs = [of(low.shape, f32)] + [of(low.shape, bf16)] * narrow
        out = call(add_kernel, "low_add", outs, low, sent)
        return out if narrow else out[0]

    ring_step()
    mine = [weight_send(sends[0], 0), weight_send(after(sends[1], *ring[1]), 1), None, weight_send(sends[3], 3)]
    near = call(stack_kernel, "near", of((2, *maps.shape), bf16), maps, after(twin, *ring[1]))
    ring_step(mine[0], mine[3], near)
    far = core_swap(near)
    mine[2] = weight_send(after(sends[2], *ring[2]), 2)
    low, narrow = call(
        low_kernel, "low", [of((RANK, rows), f32), of((RANK, rows), bf16)], adapters, hidden, near, far, scalars=1
    )
    low, narrow = added(low, z_xor(narrow, 4), narrow=True)
    ring_step(mine[1], low)
    ring_step(mine[2])
    low = added(low, z_xor(after(narrow, *ring[3]), 1))
    mine[3] = after(mine[3], *ring[3])
    other = core_swap(call(stack_kernel, "stack", of((4, 1280, 128), bf16), *mine))
    right, left = zip(*ring)

    shards = [hidden, left[1], left[2], left[3], right[4], right[3], right[2], right[1]]
    weights = (sends[4], *mine, other)
    *kv_parts, gathered = call(
        kv_product_kernel,
        "kv_product",
        [of((576, 128), bf16)] * NY + [of((rows, 1024), bf16)],
        *shards,
        *weights,
        low,
        scratch=[pltpu.VMEM((256, 1024), bf16)],
        mib=8,
    )
    kv_got = [y_shift(kv_parts[dy], dy) for dy in (2, 1, 3)]
    near_a, far_a, *b_parts = call(
        q_product_kernel,
        "q_product",
        [of((NY * TA, 128), bf16)] * 2 + [of((2 * TB, 128), bf16)] * NY,
        gathered,
        *weights,
        scratch=[pltpu.VMEM((NY, 1024, 256), bf16)],
        mib=10,
    )
    b_got = [y_shift(b_parts[dy], dy) for dy in (2, 1, 3)]
    kv_sum, low, x_send = call(
        kv_join_kernel,
        "kv_join",
        [of((512, 128), f32), of((64, 128), f32), of((NY * TA + 512, 128), bf16)],
        kv_parts[0],
        *kv_got,
        far_a,
    )
    x_got = x_swap(x_send)
    low = added(low, z_xor(low, 2))
    low = added(low, x_swap(low))
    a_own, kv_own, *a_sends = call(
        stage_a_kernel,
        "stage_a",
        [of((TA, 128), f32), of((576, 128), bf16)] + [of((TA + 576, 128), bf16)] * (NY - 1),
        near_a,
        x_got,
        kv_sum,
        low,
    )
    a_got = {dy: y_shift(a_sends[dy - 1], dy) for dy in (2, 1, 3)}
    b_own, b_send = call(
        stage_b_kernel, "stage_b", [of((TB, 128), f32), of((TB, 128), bf16)], b_parts[0], *b_got
    )
    b_last = x_swap(b_send)

    return call(
        attention_kernel,
        "attention",
        of((rows, HEAD_SIZE), bf16),
        adapters,
        request_start,
        a_own,
        *[a_got[dy] for dy in (1, 2, 3)],
        b_own,
        b_last,
        kv_own,
        near,
        far,
        cosines,
        *turns,
        scalars=2,
        scratch=[pltpu.VMEM((256, rows), bf16)] + [pltpu.VMEM((HEAD_SIZE, rows), bf16), pltpu.VMEM((rows, HEAD_SIZE), bf16)] + [pltpu.VMEM((8, RANK, 128), bf16)],
        mib=8,
    )


def solution(mesh):
    fine = Mesh(mesh.devices.reshape(NXH, NC, NZ, NX, NY), REQ_AXES + TP_AXES)
    in_specs = (
        P(REQ_AXES, TP_AXES),
        P(None, TP_AXES),
        P(None, TP_AXES),
        P(REQ_AXES, TP_AXES, None),
        P(REQ_AXES, None, TP_AXES),
        P(REQ_AXES),
        P(REQ_AXES),
    )
    return jax.shard_map(
        body, mesh=fine, in_specs=in_specs, out_specs=P(REQ_AXES, TP_AXES), check_vma=False
    )
```

```python
import functools
import math

import jax
import jax.numpy as jnp
from jax import lax
from jax.experimental import pallas as pl
from jax.experimental.pallas import tpu as pltpu
from jax.sharding import Mesh, PartitionSpec as P

HEAD_SIZE = 128
BLOCK = 128
RANK = 32
ROPE_BASE = 500000.0
ADAPTER_SCALE = 2.0
NXH, NC, NZ, NX, NY = 2, 2, 8, 2, 4
REQ_AXES = ("xh", "c")
TP_AXES = ("z", "xl", "y")
NP = NX * NY
TA, TB = 256, 768
PACK_MIB = 56
VMEM = pl.BlockSpec(memory_space=pltpu.VMEM)
SMEM = pl.BlockSpec(memory_space=pltpu.SMEM)


def z_shift(v, s):
    return lax.ppermute(v, "z", [(i, (i + s) % NZ) for i in range(NZ)])


def z_xor(v, s):
    return lax.ppermute(v, "z", [(i, i ^ s) for i in range(NZ)])


def y_xor(v, s):
    return lax.ppermute(v, "y", [(i, i ^ s) for i in range(NY)])


def x_swap(v):
    return lax.ppermute(v, "xl", [(0, 1), (1, 0)])


def core_swap(v):
    return lax.ppermute(v, "c", [(0, 1), (1, 0)])


def xh_swap(v):
    return lax.ppermute(v, "xh", [(0, 1), (1, 0)])


def y_shift(v, s):
    return lax.ppermute(v, "y", [(i, (i + s) % NY) for i in range(NY)])


SERVED = ((1, 4, 6), (3, 5, 7, 2))
FLIP = [dx * NY + (-dy) % NY for dx in range(NX) for dy in range(NY)]


def weight_send(v, k):
    route = []
    for xh in range(NXH):
        for c in range(NC):
            if k >= len(SERVED[c]):
                continue
            dx, dy = divmod(SERVED[c][k], NY)
            for xl in range(NX):
                for y in range(NY):
                    at = xh * NX + xl
                    if dx:
                        to = at ^ 1 if c == 0 else (at + 1 if at % 2 else at - 1) % 4
                    else:
                        to = at
                    src = ((xh * NC + c) * NX + xl) * NY + y
                    dst = ((to // NX * NC + c) * NX + to % NX) * NY + (y + dy) % NY
                    route.append((src, dst))
    return lax.ppermute(v, ("xh", "c", "xl", "y"), route)


def run_copies(pairs, sem):
    copies = [pltpu.make_async_copy(src, dst, sem.at[i]) for i, (src, dst) in enumerate(pairs)]
    for copy in copies:
        copy.start()
    for copy in copies:
        copy.wait()


def weight_pairs(wq_ref, kv_ref, out, d):
    z, xl, y = (lax.axis_index(a) for a in ("z", "xl", "y"))
    p = (xl ^ (d // NY)) * NY + ((y + d) & (NY - 1))
    pairs = []
    for j in range(NZ):
        row = pl.multiple_of((((z + j) & (NZ - 1)) * NP + p) * 128, 128)
        pairs.append((wq_ref.at[pl.ds(row, 128), :], out.at[j * 128 : (j + 1) * 128, :]))
        pairs.append((kv_ref.at[:, pl.ds(row, 128)], out.at[1024 + j * 32 : 1056 + j * 32, :]))
    return pairs


def pack_kernel(wq_ref, kv_ref, down_ref, up_ref, *refs):
    outs, maps, sem = refs[:5], refs[5], refs[6]
    c = lax.axis_index("c")
    pairs = [(down_ref, maps.at[:, 0:RANK, :]), (up_ref, maps.at[:, RANK : 2 * RANK, :])]
    for k, out in enumerate(outs):
        d = jnp.where(c == 0, (SERVED[0] + (0,))[k], SERVED[1][k]) if k < 4 else 0
        pairs += weight_pairs(wq_ref, kv_ref, out, d)
    run_copies(pairs, sem)


def stack_kernel(*refs):
    for i, ref in enumerate(refs[:-1]):
        refs[-1][i] = ref[...]


def add_kernel(a_ref, b_ref, *outs):
    total = a_ref[...] + b_ref[...].astype(jnp.float32)
    for out in outs:
        out[...] = total.astype(out.dtype)


def rope_kernel(start_ref, cos_ref, sin_ref, cos_t_ref, sin_t_ref):
    half = HEAD_SIZE // 2
    lane = lax.broadcasted_iota(jnp.int32, (BLOCK, HEAD_SIZE), 1)
    row = lax.broadcasted_iota(jnp.int32, (BLOCK, HEAD_SIZE), 0)
    steps = (lane & (half - 1)).astype(jnp.float32)
    inverse = jnp.exp(-(2.0 * steps / HEAD_SIZE) * math.log(ROPE_BASE))
    sign = jnp.where(lane < half, -1.0, 1.0).astype(jnp.float32)
    place = row.astype(jnp.float32) * inverse
    cos_in, sin_in = jnp.cos(place), jnp.sin(place)
    blocks = cos_ref.shape[0] // BLOCK
    ahead = lax.broadcasted_iota(jnp.int32, (8, HEAD_SIZE), 0).astype(jnp.float32) * BLOCK * inverse[0:8, :]
    cos_out, sin_out = jnp.cos(ahead), jnp.sin(ahead)
    first = (lax.axis_index("xh") * NC + lax.axis_index("c")) * blocks
    which = lax.broadcasted_iota(jnp.int32, (8, HEAD_SIZE), 0)
    for b in range(blocks):
        chosen = which == first + b - start_ref[b * BLOCK]
        co = jnp.sum(jnp.where(chosen, cos_out, 0.0), axis=0, keepdims=True)
        so = jnp.sum(jnp.where(chosen, sin_out, 0.0), axis=0, keepdims=True)
        rows = slice(b * BLOCK, (b + 1) * BLOCK)
        cos_ref[rows, :] = cos_in * co - sin_in * so
        sin_ref[rows, :] = (sin_in * co + cos_in * so) * sign
        cos_t_ref[:, rows] = cos_ref[rows, :].T
        sin_t_ref[:, rows] = sin_ref[rows, :].T


def low_kernel(ad_ref, h_ref, near_ref, far_ref, out_ref, narrow_ref):
    c, xh = lax.axis_index("c"), lax.axis_index("xh")
    per = near_ref.shape[1]
    for b in range(h_ref.shape[0] // BLOCK):
        a = ad_ref[b]
        owner = a // per
        at = a - owner * per
        xr, cr = (owner // NC) ^ xh, (owner % NC) ^ c
        down = jnp.where(cr == 0, near_ref[xr, at, 0:RANK, :], far_ref[xr, at, 0:RANK, :])
        out_ref[:, b * BLOCK : (b + 1) * BLOCK] = lax.dot_general(
            down,
            h_ref[b * BLOCK : (b + 1) * BLOCK, :],
            (((1,), (1,)), ((), ())),
            preferred_element_type=jnp.float32,
        )
    narrow_ref[...] = out_ref[...].astype(jnp.bfloat16)


def for_each_piece(own, mine, other, place):
    place(own, 0)
    c = lax.axis_index("c")
    for core in range(NC):

        @pl.when(c == core)
        def _():
            for k, d in enumerate(SERVED[core]):
                place(mine[k], FLIP[d])
            for k, d in enumerate(SERVED[1 - core]):
                place(other[k], FLIP[d])


def kv_product_kernel(*refs):
    h_refs, own, mine, other, low_ref = refs[0:8], refs[8], refs[9:13], refs[13], refs[14]
    outs, hbuf, kvw = refs[15:19], refs[19], refs[20]
    other = [other.at[k] for k in range(4)]
    y = lax.axis_index("y")
    for j in range(8):
        hbuf[:, j * 128 : (j + 1) * 128] = h_refs[j][...]
    for dy in range(NY):
        for t in range(2):
            at = pl.multiple_of((((y + dy) & (NY - 1)) * 2 + t) * 128, 128)
            outs[dy][512 + t * 32 : 544 + t * 32, :] = low_ref[:, pl.ds(at, 128)].astype(jnp.bfloat16)

    def place(ref, d):
        for j in range(NZ):
            kvw[d * 32 : (d + 1) * 32, j * 128 : (j + 1) * 128] = ref[1024 + j * 32 : 1056 + j * 32, :]

    for_each_piece(own, mine, other, place)
    kv = lax.dot_general(
        kvw[...], hbuf[...], (((1,), (1,)), ((), ())), preferred_element_type=jnp.float32
    ).astype(jnp.bfloat16)
    for d in range(NP):
        dx, dy = divmod(d, NY)
        for t in range(8):
            at = t * 64 + dx * 32
            outs[dy][at : at + 32, :] = kv[d * 32 : (d + 1) * 32, t * 128 : (t + 1) * 128]


def q_product_kernel(hbuf, own, *refs):
    mine, other = refs[0:4], [refs[4].at[k] for k in range(4)]
    near_ref, far_ref, outs, wq = refs[5], refs[6], refs[7:11], refs[11]

    def place(ref, d):
        dx, dy = divmod(d, NY)
        wq[dy, :, dx * 128 : (dx + 1) * 128] = ref[0:1024, :]

    for_each_piece(own, mine, other, place)
    for dy in range(NY):
        q = jnp.dot(hbuf[0:TA, :], wq[dy], preferred_element_type=jnp.float32).astype(jnp.bfloat16)
        near_ref[dy * TA : (dy + 1) * TA, :] = q[:, 0:128]
        far_ref[dy * TA : (dy + 1) * TA, :] = q[:, 128:256]
    for dy in range(NY):
        q = jnp.dot(hbuf[TA:1024, :], wq[dy], preferred_element_type=jnp.float32).astype(jnp.bfloat16)
        outs[dy][0:TB, :] = q[:, 0:128]
        outs[dy][TB : 2 * TB, :] = q[:, 128:256]


def wide(ref, rows):
    return ref[rows, :].astype(jnp.float32)


def kv_join_kernel(k0, k1, k2, k3, far_ref, sum_ref, low_ref, send_ref):
    total = wide(k0, ...) + wide(k1, ...) + wide(k2, ...) + wide(k3, ...)
    sum_ref[...] = total[0:512, :]
    low_ref[...] = total[512:576, :]
    send_ref[0 : NY * TA, :] = far_ref[...]
    send_ref[NY * TA :, :] = total[0:512, :].astype(jnp.bfloat16)


def stage_a_kernel(near_ref, got_ref, kv_ref, low_ref, own_ref, kv_out, *sends):
    for t in range(8):
        for dx in range(NX):
            a, b = t * 64 + dx * 32, NY * TA + t * 64 + (1 - dx) * 32
            kv_out[a : a + 32, :] = (kv_ref[a : a + 32, :] + wide(got_ref, slice(b, b + 32))).astype(jnp.bfloat16)
    kv_out[512:576, :] = low_ref[...].astype(jnp.bfloat16)
    for dy in range(NY):
        rows = slice(dy * TA, (dy + 1) * TA)
        total = wide(near_ref, rows) + wide(got_ref, rows)
        if dy == 0:
            own_ref[...] = total
        else:
            sends[dy - 1][0:TA, :] = total.astype(jnp.bfloat16)
            sends[dy - 1][TA:, :] = kv_out[...]


def stage_b_kernel(b0, b1, b2, b3, own_ref, send_ref):
    for dx, out in enumerate((own_ref, send_ref)):
        rows = slice(dx * TB, (dx + 1) * TB)
        out[...] = (wide(b0, rows) + wide(b1, rows) + wide(b2, rows) + wide(b3, rows)).astype(out.dtype)


def attention_kernel(ad_ref, start_ref, *refs):
    a_own, a_got, b_own, b_got, kv_own = refs[0], refs[1:4], refs[4], refs[5], refs[6]
    near_ref, far_ref, cos_ref, sin_ref, cos_t_ref, sin_t_ref = refs[7:13]
    out_ref = refs[13]
    kvt, k_buf, v_buf, low_buf = refs[14:18]
    xl, y, c, xh = (lax.axis_index(a) for a in ("xl", "y", "c", "xh"))
    first = (xh * NC + c) * 8
    for i in range(NY):
        ref, base = (kv_own, 0) if i == 0 else (a_got[i - 1], TA)
        for t in range(2):
            low_buf[((y - i) & (NY - 1)) * 2 + t] = ref[base + 512 + t * 32 : base + 544 + t * 32, :]
        for dx in range(NX):
            p = (xl ^ dx) * NY + ((y - i) & (NY - 1))
            at = pl.multiple_of(p * 32, 32)
            for t in range(8):
                kvt[pl.ds(at, 32), t * 128 : (t + 1) * 128] = ref[base + t * 64 + dx * 32 : base + t * 64 + dx * 32 + 32, :]

    def rope(v, rows):
        return v * cos_ref[rows, :] + pltpu.roll(v, 64, 1) * sin_ref[rows, :]

    for t in range(8):
        rows = slice(t * 128, (t + 1) * 128)
        k = kvt[0:128, rows].astype(jnp.float32)
        turned = jnp.concatenate([k[64:128, :], k[0:64, :]], axis=0)
        k_buf[:, rows] = (k * cos_t_ref[:, rows] + turned * sin_t_ref[:, rows]).astype(jnp.bfloat16)
        v_buf[rows, :] = kvt[128:256, rows].T
    per = near_ref.shape[1]
    factor = math.log2(math.e) / math.sqrt(HEAD_SIZE)
    for b in range(8):
        rows = slice(b * 128, (b + 1) * 128)
        a = ad_ref[b]
        owner = a // per
        at = a - owner * per
        xr, cr = (owner // NC) ^ xh, (owner % NC) ^ c
        up = jnp.where(cr == 0, near_ref[xr, at, RANK : 2 * RANK, :], far_ref[xr, at, RANK : 2 * RANK, :])
        q = ADAPTER_SCALE * lax.dot_general(
            low_buf[b], up, (((0,), (0,)), ((), ())), preferred_element_type=jnp.float32
        )
        if b * 128 < TA:
            q += a_own[rows, :]
            for ref in a_got:
                q += wide(ref, rows)
        else:
            part = slice(b * 128 - TA, (b + 1) * 128 - TA)
            q += b_own[part, :] + wide(b_got, part)
        q = rope(q, rows).astype(jnp.bfloat16)
        n = (b + 1) * 128
        s = jnp.dot(q, k_buf[:, 0:n], preferred_element_type=jnp.float32)
        col = lax.broadcasted_iota(jnp.int32, (128, n), 1)
        row = lax.broadcasted_iota(jnp.int32, (128, n), 0) + b * 128
        allowed = (col >= (start_ref[b * BLOCK] - first) * BLOCK) & (col <= row)
        s = jnp.where(allowed, s, -1e30)
        e = jnp.exp2((s - jnp.max(s, axis=1, keepdims=True)) * factor)
        mixed = jnp.dot(e.astype(jnp.bfloat16), v_buf[0:n, :], preferred_element_type=jnp.float32)
        out_ref[rows, :] = (mixed * (1.0 / jnp.sum(e, axis=1, keepdims=True))).astype(jnp.bfloat16)


def call(kernel, name, outs, *args, scalars=0, scratch=(), mib=4, space=pltpu.VMEM):
    single = isinstance(outs, jax.ShapeDtypeStruct)
    return pl.pallas_call(
        kernel,
        out_shape=outs,
        in_specs=[SMEM] * scalars + [pl.BlockSpec(memory_space=space)] * (len(args) - scalars),
        out_specs=VMEM if single else [VMEM] * len(outs),
        scratch_shapes=scratch,
        compiler_params=pltpu.CompilerParams(vmem_limit_bytes=mib << 20),
        name=name,
    )(*args)


def after(value, *others):
    return lax.optimization_barrier((value, *others))[0]


def body(hidden, query_weight, key_value_weight, down_maps, up_maps, request_start, adapters):
    rows = hidden.shape[0]
    bf16, f32 = jnp.bfloat16, jnp.float32
    of = jax.ShapeDtypeStruct
    *sends, maps = call(
        pack_kernel,
        "pack",
        [of((1280, 128), bf16)] * 5 + [of((down_maps.shape[0], 2 * RANK, 128), bf16)],
        query_weight,
        key_value_weight.T,
        jnp.transpose(down_maps, (0, 2, 1)),
        up_maps,
        scratch=[pltpu.SemaphoreType.DMA((10 * NZ + 2,))],
        space=pltpu.HBM,
        mib=PACK_MIB,
    )
    cosines, *turns = call(
        rope_kernel,
        "rope",
        [of((rows, HEAD_SIZE), f32)] * 2 + [of((HEAD_SIZE, rows), f32)] * 2,
        request_start,
        scalars=1,
    )
    twin = xh_swap(maps)
    ring = [(hidden, hidden)]

    def ring_step(*others):
        r, l = ring[-1]
        if len(ring) > 1:
            r, l = after(r, l, *others), after(l, r, *others)
        ring.append((z_shift(r, 1), z_shift(l, -1) if len(ring) < 4 else None))

    def added(low, sent, narrow=False):
        outs = [of(low.shape, f32)] + [of(low.shape, bf16)] * narrow
        out = call(add_kernel, "low_add", outs, low, sent)
        return out if narrow else out[0]

    ring_step()
    mine = [weight_send(sends[0], 0), weight_send(after(sends[1], *ring[1]), 1), None, weight_send(sends[3], 3)]
    near = jnp.stack([maps, after(twin, *ring[1])])
    ring_step(mine[0], mine[3], near)
    far = core_swap(near)
    mine[2] = weight_send(after(sends[2], *ring[2]), 2)
    low, narrow = call(
        low_kernel, "low", [of((RANK, rows), f32), of((RANK, rows), bf16)], adapters, hidden, near, far, scalars=1
    )
    low, narrow = added(low, z_xor(narrow, 4), narrow=True)
    ring_step(mine[1], low)
    ring_step(mine[2])
    low = added(low, z_xor(after(narrow, *ring[3]), 1))
    mine[3] = after(mine[3], *ring[3])
    other = core_swap(call(stack_kernel, "stack", of((4, 1280, 128), bf16), *mine))
    right, left = zip(*ring)

    shards = [hidden, left[1], left[2], left[3], right[4], right[3], right[2], right[1]]
    weights = (sends[4], *mine, other)
    *kv_parts, gathered = call(
        kv_product_kernel,
        "kv_product",
        [of((576, 128), bf16)] * NY + [of((rows, 1024), bf16)],
        *shards,
        *weights,
        low,
        scratch=[pltpu.VMEM((256, 1024), bf16)],
        mib=8,
    )
    kv_got = [y_shift(kv_parts[dy], dy) for dy in (2, 1, 3)]
    near_a, far_a, *b_parts = call(
        q_product_kernel,
        "q_product",
        [of((NY * TA, 128), bf16)] * 2 + [of((2 * TB, 128), bf16)] * NY,
        gathered,
        *weights,
        scratch=[pltpu.VMEM((NY, 1024, 256), bf16)],
        mib=10,
    )
    b_got = [y_shift(b_parts[dy], dy) for dy in (2, 1, 3)]
    kv_sum, low, x_send = call(
        kv_join_kernel,
        "kv_join",
        [of((512, 128), f32), of((64, 128), f32), of((NY * TA + 512, 128), bf16)],
        kv_parts[0],
        *kv_got,
        far_a,
    )
    x_got = x_swap(x_send)
    low = added(low, z_xor(low, 2))
    low = added(low, x_swap(low))
    a_own, kv_own, *a_sends = call(
        stage_a_kernel,
        "stage_a",
        [of((TA, 128), f32), of((576, 128), bf16)] + [of((TA + 576, 128), bf16)] * (NY - 1),
        near_a,
        x_got,
        kv_sum,
        low,
    )
    a_got = {dy: y_shift(a_sends[dy - 1], dy) for dy in (2, 1, 3)}
    b_own, b_send = call(
        stage_b_kernel, "stage_b", [of((TB, 128), f32), of((TB, 128), bf16)], b_parts[0], *b_got
    )
    b_last = x_swap(b_send)

    return call(
        attention_kernel,
        "attention",
        of((rows, HEAD_SIZE), bf16),
        adapters,
        request_start,
        a_own,
        *[a_got[dy] for dy in (1, 2, 3)],
        b_own,
        b_last,
        kv_own,
        near,
        far,
        cosines,
        *turns,
        scalars=2,
        scratch=[pltpu.VMEM((256, rows), bf16)] + [pltpu.VMEM((HEAD_SIZE, rows), bf16), pltpu.VMEM((rows, HEAD_SIZE), bf16)] + [pltpu.VMEM((8, RANK, 128), bf16)],
        mib=8,
    )


def solution(mesh):
    fine = Mesh(mesh.devices.reshape(NXH, NC, NZ, NX, NY), REQ_AXES + TP_AXES)
    in_specs = (
        P(REQ_AXES, TP_AXES),
        P(None, TP_AXES),
        P(None, TP_AXES),
        P(REQ_AXES, TP_AXES, None),
        P(REQ_AXES, None, TP_AXES),
        P(REQ_AXES),
        P(REQ_AXES),
    )
    return jax.shard_map(
        body, mesh=fine, in_specs=in_specs, out_specs=P(REQ_AXES, TP_AXES), check_vma=False
    )
```
